32 devices in a mesh: dp: 4 (over y, x), feat: 8 (over z, core).
Axes of the slice: x: 2, y: 2, z: 4, core: 2. Of those that a mesh axis runs over, the one named last changes fastest.
Arguments:
- sketches: bfloat16 [4, 256, 65536], P('dp', None, 'feat'), may hold values from -24 to 24
Outputs:
- merged: bfloat16 [4, 256, 65536], P('dp', None, 'feat')
The draws below stay inside these ranges and needn't reach their ends.
All inputs are finite; a program needn't handle non-finite values.
Results may differ from the reference program's by a relative error of at most 0.001.
The reference program's roundings to bfloat16 on the way (of `current`, `stacked` and `weights`) count: a program that leaves them out, or rounds other values in their place, can miss the bound.
Values may be sent and summed in bfloat16 or wider, within the bound.
No kernel may reach another device: no remote copies, remote signals or barrier semaphores. Data moves between devices by JAX's collectives and lax.ppermute only.
A program may use at most 128 MiB of HBM per device.

```python
import math
import jax
import jax.numpy as jnp
from jax import lax

SKETCH_ROWS = 256
LEVELS = 2
FEATURES = 65536
SKETCHES = 4


def draw_sketches(key, part):
    key_rows, key_cols, key_base = jax.random.split(key, 3)
    row_scale = jnp.exp(jax.random.uniform(key_rows, (SKETCHES, SKETCH_ROWS, 1), jnp.float32, math.log(0.3), math.log(3.0)))
    col_scale = jnp.exp(jax.random.uniform(key_cols, (1, 1, FEATURES), jnp.float32, math.log(0.5), math.log(2.0)))
    base = jax.random.normal(key_base, (SKETCHES, SKETCH_ROWS, FEATURES), jnp.float32)
    return jnp.clip(base * row_scale * col_scale, -24.0, 24.0).astype(jnp.bfloat16)


def setup_inputs(seed: int = 0) -> dict:
    keys = jax.random.split(jax.random.key(seed), 2)
    sketches = draw_sketches(jax.random.fold_in(keys[1], 71), 0)
    return {"sketches": sketches}


def solve_rows(gram, count):
    size = gram.shape[0]
    average = jnp.trace(gram) / size
    kernel = jnp.eye(size, dtype=jnp.float32) + gram / average
    factor = jnp.linalg.cholesky(kernel)
    target = jnp.eye(size, count, dtype=jnp.float32)
    middle = lax.linalg.triangular_solve(factor, target, left_side=True, lower=True)
    inverse = lax.linalg.triangular_solve(factor, middle, left_side=True, lower=True, transpose_a=True)
    return inverse.T.astype(jnp.bfloat16)

def merge_pair(pair):
    lower, upper = pair
    stacked = jnp.concatenate([lower, upper], axis=0)
    gram = jnp.dot(stacked.astype(jnp.float32), stacked.T.astype(jnp.float32), preferred_element_type=jnp.float32)
    weights = solve_rows(gram, lower.shape[0])
    update = jnp.dot(weights.astype(jnp.float32), stacked.astype(jnp.float32), preferred_element_type=jnp.float32)
    return (lower.astype(jnp.float32) - update).astype(jnp.bfloat16)

def reference(sketches):
    current = sketches
    for level in range(LEVELS):
        span = 2 ** level
        groups = SKETCHES // (2 * span)
        grouped = current.reshape(groups, 2, span, SKETCH_ROWS, FEATURES)
        lower = grouped[:, 0].reshape(groups * span, SKETCH_ROWS, FEATURES)
        upper = grouped[:, 1].reshape(groups * span, SKETCH_ROWS, FEATURES)
        fresh = lax.map(merge_pair, (lower, upper))
        fresh = fresh.reshape(groups, 1, span, SKETCH_ROWS, FEATURES)
        current = jnp.concatenate([fresh, fresh], axis=1).reshape(SKETCHES, SKETCH_ROWS, FEATURES)
    return current
```

```python
import functools

import jax
import jax.numpy as jnp
from jax import lax
from jax.experimental import pallas as pl
from jax.experimental.pallas import tpu as pltpu
from jax.sharding import PartitionSpec as P

LEVELS = 2
GROUP = 2**LEVELS
CORES = 2
F32, BF16 = jnp.float32, jnp.bfloat16
NT = (((1,), (1,)), ((), ()))
NN = (((1,), (0,)), ((), ()))
VMEM = pl.BlockSpec(memory_space=pltpu.VMEM)
SMEM = pl.BlockSpec(memory_space=pltpu.SMEM)


def send(block, axis, shift):
    count = lax.axis_size(axis)
    return lax.ppermute(block, axis, [(i, i ^ shift) for i in range(count)])


def dot(a, b, dims=NN):
    return lax.dot_general(a, b, dims, preferred_element_type=F32)


def shape(*dims, dtype=F32):
    return jax.ShapeDtypeStruct(dims, dtype)


def cost(flops, nbytes):
    return pl.CostEstimate(flops=int(flops), bytes_accessed=int(nbytes), transcendentals=0)


def halves(a):
    high = a.astype(BF16)
    return high, (a - high.astype(F32)).astype(BF16)


def product(a, b, dims=NN):
    (ah, al), (bh, bl) = a, b
    return dot(ah, bh, dims) + (dot(ah, bl, dims) + dot(al, bh, dims))


def eye_mask(n):
    return lax.broadcasted_iota(jnp.int32, (n, n), 0) == lax.broadcasted_iota(jnp.int32, (n, n), 1)


def invert(kernels, x_ref, limit):
    n = kernels[0].shape[0]
    mask = eye_mask(n)
    eye = jnp.where(mask, 1.0, 0.0)
    parts = [halves(k) for k in kernels]
    for j, k in enumerate(kernels):
        diag = jnp.where(mask, k, 0.0)
        row = 1.0 / jnp.sum(diag, axis=0, keepdims=True)
        col = 1.0 / jnp.sum(diag, axis=1, keepdims=True)
        scaled = jnp.where(mask, 0.0, k) * row
        spread = jnp.sum(scaled * (jnp.where(mask, 0.0, k) * col))
        bound = jnp.minimum(jnp.max(jnp.sum(jnp.abs(k), axis=1, keepdims=True)), limit)
        near = jnp.where(mask, row, -scaled * col)
        far = eye * (2.0 / (1.0 + bound))
        x_ref[j] = jnp.where(spread < 0.9, near, far)

    def step(state):
        count, _ = state
        worst = jnp.float32(0.0)
        for j, part in enumerate(parts):
            x = x_ref[j]
            xs = halves(x)
            rest = eye - product(part, xs)
            worst = jnp.maximum(worst, jnp.sum(rest * rest))
            x_ref[j] = x + product(xs, halves(rest))
        return count + 1, worst

    lax.while_loop(lambda s: (s[0] < 24) & (s[1] > 1e-6), step, (jnp.int32(0), jnp.float32(1.0)))


def resolvent(grams, x_ref, out_ref):
    n = grams[0][0].shape[0]
    mask = eye_mask(n)
    eye = jnp.where(mask, 1.0, 0.0)
    scaled = []
    for a, b, d in grams:
        average = jnp.sum(jnp.where(mask, a + d, 0.0)) / (2 * n)
        scaled.append((eye + a / average, b / average, eye + d / average))
    limit = 1.0 + 2 * n
    invert([d for _, _, d in scaled], x_ref, limit)
    ties, schurs = [], []
    for j, (a, b, d) in enumerate(scaled):
        bs = halves(b)
        tie = halves(product(bs, halves(x_ref[j])))
        ties.append(tie)
        schurs.append(a - product(tie, bs, NT))
    invert(schurs, x_ref, limit)
    for j, tie in enumerate(ties):
        x = x_ref[j]
        out_ref[j, :, :n] = x.astype(BF16)
        out_ref[j, :, n:] = (-product(halves(x), tie)).astype(BF16)


def own_gram_kernel(place, x_ref, keep_ref, give_ref, acc):
    step = pl.program_id(0)
    core = place[1]
    half = keep_ref.shape[0]

    @pl.when(step == 0)
    def _():
        acc[...] = jnp.zeros_like(acc)

    acc[...] += dot(x_ref[...], x_ref[...], NT)

    @pl.when(step == pl.num_programs(0) - 1)
    def _():
        keep_ref[...] = acc[pl.ds(pl.multiple_of(core * half, half), half), :]
        give_ref[...] = acc[pl.ds(pl.multiple_of((1 - core) * half, half), half), :]


def own_gram(place, x, tile=2048):
    rows, columns = x.shape
    half = shape(rows // CORES, rows)
    spec = pl.BlockSpec((rows // CORES, rows), lambda k, place: (0, 0))
    return pl.pallas_call(
        own_gram_kernel,
        out_shape=(half, half),
        grid_spec=pltpu.PrefetchScalarGridSpec(
            num_scalar_prefetch=1,
            grid=(columns // tile,),
            in_specs=[pl.BlockSpec((rows, tile), lambda k, place: (0, k))],
            out_specs=(spec, spec),
            scratch_shapes=[pltpu.VMEM((rows, rows), F32)],
        ),
        cost_estimate=cost(2 * rows * rows * columns, 2 * rows * columns),
        name="own_gram",
    )(place, x)


def cross_gram_kernel(place, own, p1, p2, p3, keep_ref, give_ref, block, acc):
    step = pl.program_id(0)
    me, core = place[0], place[1]
    pairs = GROUP // 2
    for s, piece in enumerate((own, p1, p2, p3)):
        block[me ^ s] = piece[...]

    @pl.when(step == 0)
    def _():
        acc[...] = jnp.zeros_like(acc)

    for j in range(pairs):
        acc[j] += dot(block[2 * j], block[2 * j + 1], NT)

    @pl.when(step == pl.num_programs(0) - 1)
    def _():
        part = keep_ref.shape[1]
        for s in range(GROUP):
            to = me ^ s
            pair, start = to // 2, (to % 2) * (CORES * part)
            keep_ref[s] = acc[pair, pl.ds(pl.multiple_of(start + core * part, part), part), :]
            give_ref[s] = acc[pair, pl.ds(pl.multiple_of(start + (1 - core) * part, part), part), :]


def cross_gram(place, x, pieces, tile=1024):
    rows, share = pieces[0].shape
    part = rows // (2 * CORES)
    steps = share // tile
    out = shape(GROUP, part, rows)
    spec = pl.BlockSpec(out.shape, lambda k, place: (0, 0, 0))
    piece = pl.BlockSpec((rows, tile), lambda k, place: (0, k))
    return pl.pallas_call(
        cross_gram_kernel,
        out_shape=(out, out),
        grid_spec=pltpu.PrefetchScalarGridSpec(
            num_scalar_prefetch=1,
            grid=(steps,),
            in_specs=[pl.BlockSpec((rows, tile), lambda k, place: (0, place[0] * steps + k))] + [piece] * 3,
            out_specs=(spec, spec),
            scratch_shapes=[pltpu.VMEM((GROUP, rows, tile), BF16), pltpu.VMEM((GROUP // 2, rows, rows), F32)],
        ),
        cost_estimate=cost(4 * rows * rows * share, 2 * GROUP * rows * share),
        name="cross_gram",
    )(place, x, *pieces)


def fold_kernel(count, *refs):
    mine, theirs, outs = refs[0], refs[1], refs[2:]
    for s in range(count):
        outs[s][...] = mine[s] + theirs[s]


def fold(mine, theirs):
    count = mine.shape[0]
    piece = shape(*mine.shape[1:])
    return pl.pallas_call(
        functools.partial(fold_kernel, count),
        out_shape=(piece,) * count,
        in_specs=[VMEM, VMEM],
        out_specs=(VMEM,) * count,
        cost_estimate=cost(mine.size, 12 * mine.size),
        name="fold",
    )(mine, theirs)


def total_kernel(count, *refs):
    out = refs[-1]
    rows = refs[0].shape[0]
    value = refs[0][...]
    for ref in refs[1:count]:
        value = value + ref[...]
    out[:rows] = value
    if len(refs) > count + 1:
        out[rows:] = refs[count][...]


def total(arrays, tail=None):
    rows, columns = arrays[0].shape
    extra = [] if tail is None else [tail]
    out = shape(rows + sum(t.shape[0] for t in extra), columns)
    return pl.pallas_call(
        functools.partial(total_kernel, len(arrays)),
        out_shape=out,
        in_specs=[VMEM] * (len(arrays) + len(extra)),
        out_specs=VMEM,
        cost_estimate=cost(len(arrays) * rows * columns, 4 * (len(arrays) + 1) * rows * columns),
        name="total",
    )(*arrays, *extra)


def first_solve_kernel(rows, place, *refs):
    bundles, w_ref, cross, diag, x_ref = refs[: 2 * GROUP], *refs[2 * GROUP :]
    me, core = place[0], place[1]
    part, half = rows // (2 * CORES), rows // CORES
    for c in range(CORES):
        for s in range(GROUP):
            source, seat = me ^ s, core ^ c
            bundle = bundles[c * GROUP + s]
            start = (source % 2) * (CORES * part) + seat * part
            cross[source // 2, pl.ds(pl.multiple_of(start, part), part), :] = bundle[:part]
            diag[source, pl.ds(pl.multiple_of(seat * half, half), half), :] = bundle[part:]
    grams = [(diag[2 * j], cross[j], diag[2 * j + 1]) for j in range(GROUP // 2)]
    resolvent(grams, x_ref, w_ref)


def first_solve(place, bundles):
    rows = bundles[0].shape[1]
    pairs = GROUP // 2
    return pl.pallas_call(
        functools.partial(first_solve_kernel, rows),
        out_shape=shape(pairs, rows, 2 * rows, dtype=BF16),
        in_specs=[SMEM] + [VMEM] * len(bundles),
        out_specs=VMEM,
        scratch_shapes=[
            pltpu.VMEM((pairs, rows, rows), F32),
            pltpu.VMEM((GROUP, rows, rows), F32),
            pltpu.VMEM((pairs, rows, rows), F32),
        ],
        cost_estimate=cost(2 * pairs * rows**3 * 40, 4 * 8 * rows * rows),
        name="first_solve",
    )(place, *bundles)


def merge_rows(lower, upper, w):
    rows = lower.shape[0]
    update = dot(w[:, :rows], lower) + dot(w[:, rows:], upper)
    return (lower.astype(F32) - update).astype(BF16)


def first_merge_kernel(place, own, p1, p2, p3, w, m_ref, keep_ref, give_ref, block, acc):
    step = pl.program_id(0)
    me, core = place[0], place[1]
    for s, piece in enumerate((own, p1, p2, p3)):
        block[me ^ s] = piece[...]

    @pl.when(step == 0)
    def _():
        acc[...] = jnp.zeros_like(acc)

    m0 = merge_rows(block[0], block[1], w[0])
    m1 = merge_rows(block[2], block[3], w[1])
    m_ref[0] = m0
    m_ref[1] = m1
    acc[0] += dot(m0, m0, NT)
    acc[1] += dot(m0, m1, NT)
    acc[2] += dot(m1, m1, NT)

    @pl.when(step == pl.num_programs(0) - 1)
    def _():
        part = keep_ref.shape[1] // 3
        for s in range(GROUP):
            to = me ^ s
            for b in range(3):
                here = pl.ds(b * part, part)
                keep_ref[s, here, :] = acc[b, pl.ds(pl.multiple_of((to * CORES + core) * part, part), part), :]
                give_ref[s, here, :] = acc[b, pl.ds(pl.multiple_of((to * CORES + 1 - core) * part, part), part), :]


def first_merge(place, x, pieces, w, tile=512):
    rows, share = pieces[0].shape
    steps = share // tile
    out = shape(GROUP, 3 * rows // (GROUP * CORES), rows)
    spec = pl.BlockSpec(out.shape, lambda k, place: (0, 0, 0))
    piece = pl.BlockSpec((rows, tile), lambda k, place: (0, k))
    return pl.pallas_call(
        first_merge_kernel,
        out_shape=(shape(2, rows, share, dtype=BF16), out, out),
        grid_spec=pltpu.PrefetchScalarGridSpec(
            num_scalar_prefetch=1,
            grid=(steps,),
            in_specs=[pl.BlockSpec((rows, tile), lambda k, place: (0, place[0] * steps + k))]
            + [piece] * 3
            + [pl.BlockSpec(w.shape, lambda k, place: (0, 0, 0))],
            out_specs=(pl.BlockSpec((2, rows, tile), lambda k, place: (0, 0, k)), spec, spec),
            scratch_shapes=[pltpu.VMEM((GROUP, rows, tile), BF16), pltpu.VMEM((3, rows, rows), F32)],
        ),
        cost_estimate=cost(14 * rows * rows * share, 12 * rows * share),
        name="first_merge",
    )(place, x, *pieces, w)


def second_solve_kernel(rows, place, *refs):
    bundles, w_ref, gram, x_ref = refs[: 2 * GROUP], *refs[2 * GROUP :]
    me, core = place[0], place[1]
    part = rows // (GROUP * CORES)
    for c in range(CORES):
        for s in range(GROUP):
            seat = (me ^ s) * CORES + (core ^ c)
            for b in range(3):
                gram[b, pl.ds(pl.multiple_of(seat * part, part), part), :] = bundles[c * GROUP + s][b * part : (b + 1) * part]
    resolvent([(gram[0], gram[1], gram[2])], x_ref, w_ref)


def second_solve(place, bundles):
    rows = bundles[0].shape[1]
    return pl.pallas_call(
        functools.partial(second_solve_kernel, rows),
        out_shape=shape(1, rows, 2 * rows, dtype=BF16),
        in_specs=[SMEM] + [VMEM] * len(bundles),
        out_specs=VMEM,
        scratch_shapes=[pltpu.VMEM((3, rows, rows), F32), pltpu.VMEM((1, rows, rows), F32)],
        cost_estimate=cost(2 * rows**3 * 40, 4 * 6 * rows * rows),
        name="second_solve",
    )(place, *bundles)


def second_merge_kernel(m, w, a_ref, b_ref):
    step = pl.program_id(0)
    merged = merge_rows(m[0], m[1], w[0])
    first = step < pl.num_programs(0) // 2

    @pl.when(first)
    def _():
        a_ref[...] = merged

    @pl.when(jnp.logical_not(first))
    def _():
        b_ref[...] = merged


def second_merge(m, w, tile=512):
    _, rows, share = m.shape
    steps = share // tile
    out = shape(rows, share // 2, dtype=BF16)
    return pl.pallas_call(
        second_merge_kernel,
        out_shape=(out, out),
        grid=(steps,),
        in_specs=[pl.BlockSpec((2, rows, tile), lambda k: (0, 0, k)), pl.BlockSpec(w.shape, lambda k: (0, 0, 0))],
        out_specs=(
            pl.BlockSpec((rows, tile), lambda k: (0, jnp.minimum(k, steps // 2 - 1))),
            pl.BlockSpec((rows, tile), lambda k: (0, jnp.maximum(k - steps // 2, 0))),
        ),
        cost_estimate=cost(4 * rows * rows * share, 6 * rows * share),
        name="second_merge",
    )(m, w)


def over_chips(block, tail=None):
    chips = lax.axis_size("feat") // CORES
    return total([block] + [send(block, "feat", CORES * s) for s in range(1, chips)], tail)


def reduce_group(keep, give):
    pieces = fold(keep, send(give, "feat", 1))
    return total([pieces[0]] + [send(pieces[s], "dp", s) for s in range(1, GROUP)])


def gather_group(bundle):
    mine = [bundle] + [send(bundle, "dp", s) for s in range(1, GROUP)]
    return mine + [send(b, "feat", 1) for b in mine]


def per_device(sketches):
    x = sketches[0]
    rows, columns = x.shape
    share = columns // GROUP
    me = lax.axis_index("dp") % GROUP
    place = jnp.stack([me, lax.axis_index("feat") % CORES]).astype(jnp.int32)

    pieces = [send(lax.dynamic_slice(x, (0, (me ^ s) * share), (rows, share)), "dp", s) for s in range(1, GROUP)]
    keep, give = own_gram(place, x)
    own = over_chips(total([keep, send(give, "feat", 1)]))

    keep, give = cross_gram(place, x, pieces)
    bundle = over_chips(reduce_group(keep, give), own)
    w = first_solve(place, gather_group(bundle))

    m, keep, give = first_merge(place, x, pieces, w)
    bundle = over_chips(reduce_group(keep, give))
    w = second_solve(place, gather_group(bundle))
    a, b = second_merge(m, w)

    ax, by = send(a, "dp", 1), send(b, "dp", 2)
    bx, ay = send(b, "dp", 1), send(a, "dp", 2)
    ad, bd = send(ax, "dp", 2), send(by, "dp", 1)
    out = jnp.zeros((rows, columns), BF16)
    for s, (left, right) in enumerate(((a, b), (ax, bx), (ay, by), (ad, bd))):
        out = lax.dynamic_update_slice(out, left, (0, (me ^ s) * share))
        out = lax.dynamic_update_slice(out, right, (0, (me ^ s) * share + share // 2))
    return out[None]


def solution(mesh):
    spec = P("dp", None, "feat")
    return jax.shard_map(per_device, mesh=mesh, in_specs=(spec,), out_specs=spec, check_vma=False)
```

```python
import functools

import jax
import jax.numpy as jnp
from jax import lax
from jax.experimental import pallas as pl
from jax.experimental.pallas import tpu as pltpu
from jax.sharding import PartitionSpec as P

LEVELS = 2
GROUP = 2**LEVELS
CORES = 2
F32, BF16 = jnp.float32, jnp.bfloat16
NT = (((1,), (1,)), ((), ()))
NN = (((1,), (0,)), ((), ()))
VMEM = pl.BlockSpec(memory_space=pltpu.VMEM)
SMEM = pl.BlockSpec(memory_space=pltpu.SMEM)
ANY = pl.BlockSpec(memory_space=pl.ANY)


def send(block, axis, shift):
    count = lax.axis_size(axis)
    return lax.ppermute(block, axis, [(i, i ^ shift) for i in range(count)])


def dot(a, b, dims=NN):
    return lax.dot_general(a, b, dims, preferred_element_type=F32)


def shape(*dims, dtype=F32):
    return jax.ShapeDtypeStruct(dims, dtype)


def cost(flops, nbytes):
    return pl.CostEstimate(flops=int(flops), bytes_accessed=int(nbytes), transcendentals=0)


def halves(a):
    high = a.astype(BF16)
    return high, (a - high.astype(F32)).astype(BF16)


def product(a, b, dims=NN):
    (ah, al), (bh, bl) = a, b
    return dot(ah, bh, dims) + (dot(ah, bl, dims) + dot(al, bh, dims))


def eye_mask(n):
    return lax.broadcasted_iota(jnp.int32, (n, n), 0) == lax.broadcasted_iota(jnp.int32, (n, n), 1)


def invert(kernels, x_ref, limit):
    n = kernels[0].shape[0]
    mask = eye_mask(n)
    eye = jnp.where(mask, 1.0, 0.0)
    parts = [halves(k) for k in kernels]
    for j, k in enumerate(kernels):
        diag = jnp.where(mask, k, 0.0)
        row = 1.0 / jnp.sum(diag, axis=0, keepdims=True)
        col = 1.0 / jnp.sum(diag, axis=1, keepdims=True)
        scaled = jnp.where(mask, 0.0, k) * row
        spread = jnp.sum(scaled * (jnp.where(mask, 0.0, k) * col))
        bound = jnp.minimum(jnp.max(jnp.sum(jnp.abs(k), axis=1, keepdims=True)), limit)
        near = jnp.where(mask, row, -scaled * col)
        far = eye * (2.0 / (1.0 + bound))
        x_ref[j] = jnp.where(spread < 0.9, near, far)

    def step(state):
        count, _ = state
        worst = jnp.float32(0.0)
        for j, part in enumerate(parts):
            x = x_ref[j]
            xs = halves(x)
            rest = eye - product(part, xs)
            worst = jnp.maximum(worst, jnp.sum(rest * rest))
            x_ref[j] = x + product(xs, halves(rest))
        return count + 1, worst

    lax.while_loop(lambda s: (s[0] < 24) & (s[1] > 1e-6), step, (jnp.int32(0), jnp.float32(1.0)))


def resolvent(grams, x_ref, out_ref):
    n = grams[0][0].shape[0]
    mask = eye_mask(n)
    eye = jnp.where(mask, 1.0, 0.0)
    scaled = []
    for a, b, d in grams:
        average = jnp.sum(jnp.where(mask, a + d, 0.0)) / (2 * n)
        scaled.append((eye + a / average, b / average, eye + d / average))
    limit = 1.0 + 2 * n
    invert([d for _, _, d in scaled], x_ref, limit)
    ties, schurs = [], []
    for j, (a, b, d) in enumerate(scaled):
        bs = halves(b)
        tie = halves(product(bs, halves(x_ref[j])))
        ties.append(tie)
        schurs.append(a - product(tie, bs, NT))
    invert(schurs, x_ref, limit)
    for j, tie in enumerate(ties):
        x = x_ref[j]
        out_ref[j, :, :n] = x.astype(BF16)
        out_ref[j, :, n:] = (-product(halves(x), tie)).astype(BF16)


def own_gram_kernel(place, x_ref, keep_ref, give_ref, acc):
    step = pl.program_id(0)
    core = place[1]
    half = keep_ref.shape[0]

    @pl.when(step == 0)
    def _():
        acc[...] = jnp.zeros_like(acc)

    acc[...] += dot(x_ref[...], x_ref[...], NT)

    @pl.when(step == pl.num_programs(0) - 1)
    def _():
        keep_ref[...] = acc[pl.ds(pl.multiple_of(core * half, half), half), :]
        give_ref[...] = acc[pl.ds(pl.multiple_of((1 - core) * half, half), half), :]


def own_gram(place, x, tile=2048):
    rows, columns = x.shape
    half = shape(rows // CORES, rows)
    spec = pl.BlockSpec((rows // CORES, rows), lambda k, place: (0, 0))
    return pl.pallas_call(
        own_gram_kernel,
        out_shape=(half, half),
        grid_spec=pltpu.PrefetchScalarGridSpec(
            num_scalar_prefetch=1,
            grid=(columns // tile,),
            in_specs=[pl.BlockSpec((rows, tile), lambda k, place: (0, k))],
            out_specs=(spec, spec),
            scratch_shapes=[pltpu.VMEM((rows, rows), F32)],
        ),
        cost_estimate=cost(2 * rows * rows * columns, 2 * rows * columns),
        name="own_gram",
    )(place, x)


def cross_gram_kernel(place, own, p1, p2, p3, keep_ref, give_ref, block, acc):
    step = pl.program_id(0)
    me, core = place[0], place[1]
    pairs = GROUP // 2
    for s, piece in enumerate((own, p1, p2, p3)):
        block[me ^ s] = piece[...]

    @pl.when(step == 0)
    def _():
        acc[...] = jnp.zeros_like(acc)

    for j in range(pairs):
        acc[j] += dot(block[2 * j], block[2 * j + 1], NT)

    @pl.when(step == pl.num_programs(0) - 1)
    def _():
        part = keep_ref.shape[1]
        for s in range(GROUP):
            to = me ^ s
            pair, start = to // 2, (to % 2) * (CORES * part)
            keep_ref[s] = acc[pair, pl.ds(pl.multiple_of(start + core * part, part), part), :]
            give_ref[s] = acc[pair, pl.ds(pl.multiple_of(start + (1 - core) * part, part), part), :]


def cross_gram(place, x, pieces, tile=1024):
    rows, share = pieces[0].shape
    part = rows // (2 * CORES)
    steps = share // tile
    out = shape(GROUP, part, rows)
    spec = pl.BlockSpec(out.shape, lambda k, place: (0, 0, 0))
    piece = pl.BlockSpec((rows, tile), lambda k, place: (0, k))
    return pl.pallas_call(
        cross_gram_kernel,
        out_shape=(out, out),
        grid_spec=pltpu.PrefetchScalarGridSpec(
            num_scalar_prefetch=1,
            grid=(steps,),
            in_specs=[pl.BlockSpec((rows, tile), lambda k, place: (0, place[0] * steps + k))] + [piece] * 3,
            out_specs=(spec, spec),
            scratch_shapes=[pltpu.VMEM((GROUP, rows, tile), BF16), pltpu.VMEM((GROUP // 2, rows, rows), F32)],
        ),
        cost_estimate=cost(4 * rows * rows * share, 2 * GROUP * rows * share),
        name="cross_gram",
    )(place, x, *pieces)


def fold(mine, theirs):
    return [mine[s] + theirs[s] for s in range(mine.shape[0])]


def total(arrays):
    return functools.reduce(jnp.add, arrays)


def merge_rows(lower, upper, w):
    rows = lower.shape[0]
    update = dot(w[:, :rows], lower) + dot(w[:, rows:], upper)
    return (lower.astype(F32) - update).astype(BF16)


def first_kernel(tile, *refs):
    place, tails, crosses, (x, p1, p2, p3), refs = refs[0], refs[1:9], refs[9:17], refs[17:21], refs[21:]
    m_ref, keep_ref, give_ref, cross, diag, inverse, w, block, m, acc, load, save = refs
    me, core = place[0], place[1]
    rows, share = p1.shape
    loads = [pltpu.make_async_copy(x.at[:, pl.ds(pl.multiple_of(me * share, share), share)], block.at[me], load.at[0])]
    loads += [pltpu.make_async_copy(p, block.at[me ^ s], load.at[s]) for s, p in ((1, p1), (2, p2), (3, p3))]
    for copy in loads:
        copy.start()

    part, half = rows // (2 * CORES), rows // CORES
    for c in range(CORES):
        for s in range(GROUP):
            source, seat = me ^ s, core ^ c
            start = (source % 2) * (CORES * part) + seat * part
            cross[source // 2, pl.ds(pl.multiple_of(start, part), part), :] = crosses[c * GROUP + s][...]
            diag[source, pl.ds(pl.multiple_of(seat * half, half), half), :] = tails[c * GROUP + s][...]
    grams = [(diag[2 * j], cross[j], diag[2 * j + 1]) for j in range(GROUP // 2)]
    resolvent(grams, inverse, w)
    for copy in loads:
        copy.wait()

    acc[...] = jnp.zeros_like(acc)
    saves = []
    for k in range(share // tile):
        here = slice(k * tile, (k + 1) * tile)
        m0 = merge_rows(block[0, :, here], block[1, :, here], w[0])
        m1 = merge_rows(block[2, :, here], block[3, :, here], w[1])
        m[0, :, here] = m0
        m[1, :, here] = m1
        copy = pltpu.make_async_copy(m.at[:, :, here], m_ref.at[:, :, here], save.at[k])
        copy.start()
        saves.append(copy)
        acc[0] += dot(m0, m0, NT)
        acc[1] += dot(m0, m1, NT)
        acc[2] += dot(m1, m1, NT)
    part = rows // (GROUP * CORES)
    for s in range(GROUP):
        to = me ^ s
        for b in range(3):
            here = pl.ds(b * part, part)
            keep_ref[s, here, :] = acc[b, pl.ds(pl.multiple_of((to * CORES + core) * part, part), part), :]
            give_ref[s, here, :] = acc[b, pl.ds(pl.multiple_of((to * CORES + 1 - core) * part, part), part), :]
    for copy in saves:
        copy.wait()


def first(place, diagonals, crosses, x, pieces, tile=512):
    rows, share = pieces[0].shape
    pairs = GROUP // 2
    out = shape(GROUP, 3 * rows // (GROUP * CORES), rows)
    return pl.pallas_call(
        functools.partial(first_kernel, tile),
        out_shape=(shape(pairs, rows, share, dtype=BF16), out, out),
        in_specs=[SMEM] + [VMEM] * (4 * GROUP) + [ANY] * 4,
        out_specs=(ANY, VMEM, VMEM),
        scratch_shapes=[
            pltpu.VMEM((pairs, rows, rows), F32),
            pltpu.VMEM((GROUP, rows, rows), F32),
            pltpu.VMEM((pairs, rows, rows), F32),
            pltpu.VMEM((pairs, rows, 2 * rows), BF16),
            pltpu.VMEM((GROUP, rows, share), BF16),
            pltpu.VMEM((pairs, rows, share), BF16),
            pltpu.VMEM((3, rows, rows), F32),
            pltpu.SemaphoreType.DMA((GROUP,)),
            pltpu.SemaphoreType.DMA((share // tile,)),
        ],
        cost_estimate=cost(2 * pairs * rows**3 * 40 + 14 * rows * rows * share, 12 * rows * share),
        name="first",
    )(place, *diagonals, *crosses, x, *pieces)


def second_kernel(tile, *refs):
    place, bundles, m_ref, refs = refs[0], refs[1:9], refs[9], refs[10:]
    a_ref, b_ref, gram, inverse, w, m, load = refs
    me, core = place[0], place[1]
    rows, share = m.shape[1:]
    copy = pltpu.make_async_copy(m_ref, m, load)
    copy.start()
    part = rows // (GROUP * CORES)
    for c in range(CORES):
        for s in range(GROUP):
            seat = (me ^ s) * CORES + (core ^ c)
            for b in range(3):
                gram[b, pl.ds(pl.multiple_of(seat * part, part), part), :] = bundles[c * GROUP + s][b * part : (b + 1) * part]
    resolvent([(gram[0], gram[1], gram[2])], inverse, w)
    copy.wait()
    for k in range(share // tile):
        here = slice(k * tile, (k + 1) * tile)
        merged = merge_rows(m[0, :, here], m[1, :, here], w[0])
        if k * tile < share // 2:
            a_ref[:, here] = merged
        else:
            b_ref[:, k * tile - share // 2 : (k + 1) * tile - share // 2] = merged


def second(place, bundles, m, tile=512):
    _, rows, share = m.shape
    out = shape(rows, share // 2, dtype=BF16)
    return pl.pallas_call(
        functools.partial(second_kernel, tile),
        out_shape=(out, out),
        in_specs=[SMEM] + [VMEM] * (2 * GROUP) + [ANY],
        out_specs=(VMEM, VMEM),
        scratch_shapes=[
            pltpu.VMEM((3, rows, rows), F32),
            pltpu.VMEM((1, rows, rows), F32),
            pltpu.VMEM((1, rows, 2 * rows), BF16),
            pltpu.VMEM(m.shape, BF16),
            pltpu.SemaphoreType.DMA,
        ],
        cost_estimate=cost(2 * rows**3 * 40 + 4 * rows * rows * share, 6 * rows * share),
        name="second",
    )(place, *bundles, m)


def over_chips(block):
    chips = lax.axis_size("feat") // CORES
    return total([block] + [send(block, "feat", CORES * s) for s in range(1, chips)])


def reduce_group(keep, give):
    pieces = fold(keep, send(give, "feat", 1))
    return total([pieces[0]] + [send(pieces[s], "dp", s) for s in range(1, GROUP)])


def gather_group(bundle):
    mine = [bundle] + [send(bundle, "dp", s) for s in range(1, GROUP)]
    return mine + [send(b, "feat", 1) for b in mine]


def per_device(sketches):
    x = sketches[0]
    rows, columns = x.shape
    share = columns // GROUP
    me = lax.axis_index("dp") % GROUP
    place = jnp.stack([me, lax.axis_index("feat") % CORES]).astype(jnp.int32)

    pieces, source = [], x
    for s in (1, 3, 2):
        piece = lax.dynamic_slice(source, (0, (me ^ s) * share), (rows, share))
        source, piece = lax.optimization_barrier((source, piece))
        pieces.append(send(piece, "dp", s))
    p1, p3, p2 = pieces
    keep, give = own_gram(place, x)
    own = over_chips(total([keep, send(give, "feat", 1)]))
    diagonals = gather_group(own)
    p1, p2, p3, diagonals = lax.optimization_barrier((p1, p2, p3, diagonals))
    pieces = [p1, p2, p3]

    keep, give = cross_gram(place, x, pieces)
    crosses = gather_group(over_chips(reduce_group(keep, give)))
    m, keep, give = first(place, diagonals, crosses, x, pieces)
    a, b = second(place, gather_group(over_chips(reduce_group(keep, give))), m)

    ax, by = send(a, "dp", 1), send(b, "dp", 2)
    bx, ay = send(b, "dp", 1), send(a, "dp", 2)
    ad, bd = send(ax, "dp", 2), send(by, "dp", 1)
    out = jnp.zeros((rows, columns), BF16)
    for s, (left, right) in enumerate(((a, b), (ax, bx), (ay, by), (ad, bd))):
        out = lax.dynamic_update_slice(out, left, (0, (me ^ s) * share))
        out = lax.dynamic_update_slice(out, right, (0, (me ^ s) * share + share // 2))
    return out[None]


def solution(mesh):
    spec = P("dp", None, "feat")
    return jax.shard_map(per_device, mesh=mesh, in_specs=(spec,), out_specs=spec, check_vma=False)
```

```python
import functools

import jax
import jax.numpy as jnp
from jax import lax
from jax.experimental import pallas as pl
from jax.experimental.pallas import tpu as pltpu
from jax.sharding import PartitionSpec as P


LEVELS = 2
GROUP = 2**LEVELS
CORES = 2
F32, BF16 = jnp.float32, jnp.bfloat16
NT = (((1,), (1,)), ((), ()))
NN = (((1,), (0,)), ((), ()))
VMEM = pl.BlockSpec(memory_space=pltpu.VMEM)
SMEM = pl.BlockSpec(memory_space=pltpu.SMEM)
ANY = pl.BlockSpec(memory_space=pl.ANY)


def send(block, axis, shift):
    count = lax.axis_size(axis)
    return lax.ppermute(block, axis, [(i, i ^ shift) for i in range(count)])


def send_all(blocks, axis, shifts):
    return [send(b, axis, s) for b, s in zip(blocks, shifts)]


def dot(a, b, dims=NN):
    return lax.dot_general(a, b, dims, preferred_element_type=F32)


def shape(*dims, dtype=F32):
    return jax.ShapeDtypeStruct(dims, dtype)


def cost(flops, nbytes):
    return pl.CostEstimate(flops=int(flops), bytes_accessed=int(nbytes), transcendentals=0)


def halves(a):
    high = a.astype(BF16)
    return high, (a - high.astype(F32)).astype(BF16)


def product(a, b, dims=NN):
    (ah, al), (bh, bl) = a, b
    return dot(ah, bh, dims) + (dot(ah, bl, dims) + dot(al, bh, dims))


def eye_mask(n):
    return lax.broadcasted_iota(jnp.int32, (n, n), 0) == lax.broadcasted_iota(jnp.int32, (n, n), 1)


def invert(kernels, x_ref, limit):
    n = kernels[0].shape[0]
    mask = eye_mask(n)
    eye = jnp.where(mask, 1.0, 0.0)
    parts = [halves(k) for k in kernels]
    for j, k in enumerate(kernels):
        diag = jnp.where(mask, k, 0.0)
        row = 1.0 / jnp.sum(diag, axis=0, keepdims=True)
        col = 1.0 / jnp.sum(diag, axis=1, keepdims=True)
        scaled = jnp.where(mask, 0.0, k) * row
        spread = jnp.sum(scaled * (jnp.where(mask, 0.0, k) * col))
        bound = jnp.minimum(jnp.max(jnp.sum(jnp.abs(k), axis=1, keepdims=True)), limit)
        near = jnp.where(mask, row, -scaled * col)
        far = eye * (2.0 / (1.0 + bound))
        x_ref[j] = jnp.where(spread < 0.9, near, far)

    def step(state):
        count, _ = state
        worst = jnp.float32(0.0)
        for j, part in enumerate(parts):
            x = x_ref[j]
            xs = halves(x)
            rest = eye - product(part, xs)
            worst = jnp.maximum(worst, jnp.sum(rest * rest))
            x_ref[j] = x + product(xs, halves(rest))
        return count + 1, worst

    lax.while_loop(lambda s: (s[0] < 24) & (s[1] > 1e-6), step, (jnp.int32(0), jnp.float32(1.0)))


def resolvent(grams, x_ref, out_ref):
    n = grams[0][0].shape[0]
    mask = eye_mask(n)
    eye = jnp.where(mask, 1.0, 0.0)
    scaled = []
    for a, b, d in grams:
        average = jnp.sum(jnp.where(mask, a + d, 0.0)) / (2 * n)
        scaled.append((eye + a / average, b / average, eye + d / average))
    limit = 1.0 + 2 * n
    invert([d for _, _, d in scaled], x_ref, limit)
    ties, schurs = [], []
    for j, (a, b, d) in enumerate(scaled):
        bs = halves(b)
        tie = halves(product(bs, halves(x_ref[j])))
        ties.append(tie)
        schurs.append(a - product(tie, bs, NT))
    invert(schurs, x_ref, limit)
    for j, tie in enumerate(ties):
        x = x_ref[j]
        out_ref[j, :, :n] = x.astype(BF16)
        out_ref[j, :, n:] = (-product(halves(x), tie)).astype(BF16)


def own_gram_kernel(place, x_ref, keep_ref, give_ref, acc):
    step = pl.program_id(0)
    core = place[1]
    half = keep_ref.shape[0]

    @pl.when(step == 0)
    def _():
        acc[...] = jnp.zeros_like(acc)

    acc[...] += dot(x_ref[...], x_ref[...], NT)

    @pl.when(step == pl.num_programs(0) - 1)
    def _():
        keep_ref[...] = acc[pl.ds(pl.multiple_of(core * half, half), half), :]
        give_ref[...] = acc[pl.ds(pl.multiple_of((1 - core) * half, half), half), :]


def own_gram(place, x, tile=2048):
    rows, columns = x.shape
    half = shape(rows // CORES, rows)
    spec = pl.BlockSpec((rows // CORES, rows), lambda k, place: (0, 0))
    return pl.pallas_call(
        own_gram_kernel,
        out_shape=(half, half),
        grid_spec=pltpu.PrefetchScalarGridSpec(
            num_scalar_prefetch=1,
            grid=(columns // tile,),
            in_specs=[pl.BlockSpec((rows, tile), lambda k, place: (0, k))],
            out_specs=(spec, spec),
            scratch_shapes=[pltpu.VMEM((rows, rows), F32)],
        ),
        cost_estimate=cost(2 * rows * rows * columns, 2 * rows * columns),
        name="own_gram",
    )(place, x)


def near_gram_kernel(place, own, p1, out_ref, block):
    step = pl.program_id(0)
    for s, piece in enumerate((own, p1)):
        block[(place[0] ^ s) % 2] = piece[...]

    @pl.when(step == 0)
    def _():
        out_ref[...] = jnp.zeros_like(out_ref)

    out_ref[...] += dot(block[0], block[1], NT)


def near_gram(place, x, p1, tile=1024):
    rows, share = p1.shape
    steps = share // tile
    return pl.pallas_call(
        near_gram_kernel,
        out_shape=shape(rows, rows),
        grid_spec=pltpu.PrefetchScalarGridSpec(
            num_scalar_prefetch=1,
            grid=(steps,),
            in_specs=[
                pl.BlockSpec((rows, tile), lambda k, place: (0, place[0] * steps + k)),
                pl.BlockSpec((rows, tile), lambda k, place: (0, k)),
            ],
            out_specs=pl.BlockSpec((rows, rows), lambda k, place: (0, 0)),
            scratch_shapes=[pltpu.VMEM((2, rows, tile), BF16)],
        ),
        cost_estimate=cost(2 * rows * rows * share, 4 * rows * share),
        name="near_gram",
    )(place, x, p1)


def far_gram_kernel(place, near, p2, p3, keep_ref, give_ref, block, acc):
    step = pl.program_id(0)
    me, core = place[0], place[1]
    for s, piece in ((2, p2), (3, p3)):
        block[(me ^ s) % 2] = piece[...]

    @pl.when(step == 0)
    def _():
        acc[me // 2] = near[...]
        acc[1 - me // 2] = jnp.zeros_like(near)

    acc[1 - me // 2] += dot(block[0], block[1], NT)

    @pl.when(step == pl.num_programs(0) - 1)
    def _():
        part = keep_ref.shape[1]
        for s in range(GROUP):
            to = me ^ s
            pair, start = to // 2, (to % 2) * (CORES * part)
            keep_ref[s] = acc[pair, pl.ds(pl.multiple_of(start + core * part, part), part), :]
            give_ref[s] = acc[pair, pl.ds(pl.multiple_of(start + (1 - core) * part, part), part), :]


def far_gram(place, near, p2, p3, tile=1024):
    rows, share = p2.shape
    part = rows // (2 * CORES)
    out = shape(GROUP, part, rows)
    spec = pl.BlockSpec(out.shape, lambda k, place: (0, 0, 0))
    piece = pl.BlockSpec((rows, tile), lambda k, place: (0, k))
    return pl.pallas_call(
        far_gram_kernel,
        out_shape=(out, out),
        grid_spec=pltpu.PrefetchScalarGridSpec(
            num_scalar_prefetch=1,
            grid=(share // tile,),
            in_specs=[pl.BlockSpec((rows, rows), lambda k, place: (0, 0)), piece, piece],
            out_specs=(spec, spec),
            scratch_shapes=[pltpu.VMEM((2, rows, tile), BF16), pltpu.VMEM((GROUP // 2, rows, rows), F32)],
        ),
        cost_estimate=cost(2 * rows * rows * share, 4 * rows * share),
        name="far_gram",
    )(place, near, p2, p3)


def fold(mine, theirs):
    return [mine[s] + theirs[s] for s in range(mine.shape[0])]


def total(arrays):
    return functools.reduce(jnp.add, arrays)


def merge_rows(lower, upper, w):
    rows = lower.shape[0]
    update = dot(w[:, :rows], lower) + dot(w[:, rows:], upper)
    return (lower.astype(F32) - update).astype(BF16)


def first_kernel(tile, *refs):
    place, tails, crosses, (x, p1, p2, p3), refs = refs[0], refs[1:9], refs[9:17], refs[17:21], refs[21:]
    m_ref, e_ref, f_ref, keep_ref, give_ref, cross, diag, inverse, w, block, m, acc, load, save = refs
    ahead = e_ref.shape[2]
    me, core = place[0], place[1]
    rows, share = p1.shape
    loads = [pltpu.make_async_copy(x.at[:, pl.ds(pl.multiple_of(me * share, share), share)], block.at[me], load.at[0])]
    loads += [pltpu.make_async_copy(p, block.at[me ^ s], load.at[s]) for s, p in ((1, p1), (2, p2), (3, p3))]
    for copy in loads:
        copy.start()

    part, half = rows // (2 * CORES), rows // CORES
    for c in range(CORES):
        for s in range(GROUP):
            source, seat = me ^ s, core ^ c
            start = (source % 2) * (CORES * part) + seat * part
            cross[source // 2, pl.ds(pl.multiple_of(start, part), part), :] = crosses[c * GROUP + s][...]
            diag[source, pl.ds(pl.multiple_of(seat * half, half), half), :] = tails[c * GROUP + s][...]
    grams = [(diag[2 * j], cross[j], diag[2 * j + 1]) for j in range(GROUP // 2)]
    resolvent(grams, inverse, w)
    for copy in loads:
        copy.wait()

    acc[...] = jnp.zeros_like(acc)
    saves = []
    for k in range(share // tile):
        here = slice(k * tile, (k + 1) * tile)
        m0 = merge_rows(block[0, :, here], block[1, :, here], w[0])
        m1 = merge_rows(block[2, :, here], block[3, :, here], w[1])
        m[0, :, here] = m0
        m[1, :, here] = m1
        saves.append(pltpu.make_async_copy(m.at[:, :, here], m_ref.at[:, :, here], save.at[k]))
        saves[-1].start()
        acc[0] += dot(m0, m0, NT)
        acc[1] += dot(m0, m1, NT)
        acc[2] += dot(m1, m1, NT)
    for i, ref in enumerate((e_ref, f_ref)):
        source = m.at[:, :, i * ahead : (i + 1) * ahead]
        saves.append(pltpu.make_async_copy(source, ref, save.at[share // tile + i]))
        saves[-1].start()
    part = rows // (GROUP * CORES)
    for s in range(GROUP):
        to = me ^ s
        for b in range(3):
            here = pl.ds(b * part, part)
            keep_ref[s, here, :] = acc[b, pl.ds(pl.multiple_of((to * CORES + core) * part, part), part), :]
            give_ref[s, here, :] = acc[b, pl.ds(pl.multiple_of((to * CORES + 1 - core) * part, part), part), :]
    for copy in saves:
        copy.wait()


def first(place, diagonals, crosses, x, pieces, ahead, tile=512):
    rows, share = pieces[0].shape
    pairs = GROUP // 2
    out = shape(GROUP, 3 * rows // (GROUP * CORES), rows)
    return pl.pallas_call(
        functools.partial(first_kernel, tile),
        out_shape=tuple(shape(pairs, rows, n, dtype=BF16) for n in (share, ahead, ahead)) + (out, out),
        in_specs=[SMEM] + [VMEM] * (4 * GROUP) + [ANY] * 4,
        out_specs=(ANY, ANY, ANY, VMEM, VMEM),
        scratch_shapes=[
            pltpu.VMEM((pairs, rows, rows), F32),
            pltpu.VMEM((GROUP, rows, rows), F32),
            pltpu.VMEM((pairs, rows, rows), F32),
            pltpu.VMEM((pairs, rows, 2 * rows), BF16),
            pltpu.VMEM((GROUP, rows, share), BF16),
            pltpu.VMEM((pairs, rows, share), BF16),
            pltpu.VMEM((3, rows, rows), F32),
            pltpu.SemaphoreType.DMA((GROUP,)),
            pltpu.SemaphoreType.DMA((share // tile + 2,)),
        ],
        cost_estimate=cost(2 * pairs * rows**3 * 40 + 14 * rows * rows * share, 12 * rows * share),
        name="first",
    )(place, *diagonals, *crosses, x, *pieces)


def second_kernel(*refs):
    place, bundles, m_ref, refs = refs[0], refs[1:9], refs[9], refs[10:]
    a_ref, b_ref, e_ref, w_ref, gram, inverse, m, load = refs
    me, core = place[0], place[1]
    rows = m.shape[1]
    copy = pltpu.make_async_copy(m_ref, m, load)
    copy.start()
    part = rows // (GROUP * CORES)
    for c in range(CORES):
        for s in range(GROUP):
            seat = (me ^ s) * CORES + (core ^ c)
            for b in range(3):
                gram[b, pl.ds(pl.multiple_of(seat * part, part), part), :] = bundles[c * GROUP + s][b * part : (b + 1) * part]
    resolvent([(gram[0], gram[1], gram[2])], inverse, w_ref)
    copy.wait()
    start = 0
    for ref in (e_ref, a_ref, b_ref):
        here = slice(start, start + ref.shape[1])
        ref[...] = merge_rows(m[0, :, here], m[1, :, here], w_ref[0])
        start += ref.shape[1]


def second(place, bundles, m, ahead):
    _, rows, share = m.shape
    early, half = 2 * ahead, share // 2 - ahead
    return pl.pallas_call(
        second_kernel,
        out_shape=tuple(shape(rows, n, dtype=BF16) for n in (half, half, early)) + (shape(1, rows, 2 * rows, dtype=BF16),),
        in_specs=[SMEM] + [VMEM] * (2 * GROUP) + [ANY],
        out_specs=(VMEM,) * 4,
        scratch_shapes=[
            pltpu.VMEM((3, rows, rows), F32),
            pltpu.VMEM((1, rows, rows), F32),
            pltpu.VMEM(m.shape, BF16),
            pltpu.SemaphoreType.DMA,
        ],
        cost_estimate=cost(2 * rows**3 * 40 + 4 * rows * rows * share, 6 * rows * share),
        name="second",
    )(place, *bundles, m)


def late_kernel(share, place, w, a, b, e, *refs):
    early, (out, buffer, save) = refs[:-3], refs[-3:]
    me, ahead, half = place[0], e.shape[1] // 2, a.shape[1]
    saves = []

    def put(source, owner, column):
        target = out.at[:, pl.ds(pl.multiple_of(owner * share + column, 128), source.shape[1])]
        saves.append(pltpu.make_async_copy(source, target, save.at[len(saves)]))
        saves[-1].start()

    put(e, me, 0)
    put(a, me, 2 * ahead)
    put(b, me, 2 * ahead + half)
    for i, pair in enumerate(early):
        buffer[i] = merge_rows(pair[0], pair[1], w[0])
        put(buffer.at[i], me ^ (i % (GROUP - 1) + 1), i // (GROUP - 1) * ahead)
    for copy in saves:
        copy.wait()


def late(place, w, a, b, e, early, share):
    rows, ahead = e.shape[0], e.shape[1] // 2
    return pl.pallas_call(
        functools.partial(late_kernel, share),
        out_shape=shape(rows, GROUP * share, dtype=BF16),
        in_specs=[SMEM] + [VMEM] * (4 + len(early)),
        out_specs=ANY,
        scratch_shapes=[pltpu.VMEM((len(early), rows, ahead), BF16), pltpu.SemaphoreType.DMA((len(early) + 3,))],
        cost_estimate=cost(4 * rows * rows * ahead * len(early), 6 * rows * ahead * len(early)),
        name="late",
    )(place, w, a, b, e, *early)


def put_kernel(spots, share, place, *refs):
    blocks, out, save = refs[: len(spots)], refs[-2], refs[-1]
    saves = []
    for i, ((s, column), block) in enumerate(zip(spots, blocks)):
        start = pl.multiple_of((place[0] ^ s) * share + column, 128)
        saves.append(pltpu.make_async_copy(block, out.at[:, pl.ds(start, block.shape[1])], save.at[i]))
        saves[-1].start()
    for copy in saves:
        copy.wait()


def put(place, out, blocks, spots, share):
    size = sum(b.size for b in blocks)
    return pl.pallas_call(
        functools.partial(put_kernel, spots, share),
        out_shape=shape(*out.shape, dtype=out.dtype),
        in_specs=[SMEM] + [VMEM] * len(blocks) + [ANY],
        out_specs=ANY,
        scratch_shapes=[pltpu.SemaphoreType.DMA((len(blocks),))],
        input_output_aliases={1 + len(blocks): 0},
        cost_estimate=cost(0, 4 * size),
        name="put",
    )(place, *blocks, out)


PEERS = tuple(range(1, GROUP))


def over_chips(block):
    chips = lax.axis_size("feat") // CORES
    return total([block] + [send(block, "feat", CORES * s) for s in range(1, chips)])


def gather_group(bundle):
    mine = [bundle] + send_all([bundle] * len(PEERS), "dp", PEERS)
    return mine + [send(b, "feat", 1) for b in mine]


def run(sketches):
    x = sketches[0]
    rows, columns = x.shape
    share = columns // GROUP
    ahead = share // 8
    me = lax.axis_index("dp") % GROUP
    place = jnp.stack([me, lax.axis_index("feat") % CORES]).astype(jnp.int32)

    pieces, source = {}, x
    for s in (1, 3, 2):
        piece = lax.dynamic_slice(source, (0, (me ^ s) * share), (rows, share))
        source, piece = lax.optimization_barrier((source, piece))
        pieces[s] = send(piece, "dp", s)
    keep, give = own_gram(place, x)
    own = over_chips(total([keep, send(give, "feat", 1)]))
    near = near_gram(place, x, pieces[1])
    p2, p3, own, near = lax.optimization_barrier((pieces[2], pieces[3], own, near))

    keep, give = far_gram(place, near, p2, p3)
    parts = fold(keep, send(give, "feat", 1))
    parts, own = lax.optimization_barrier((parts, own))
    mine = total([parts[0]] + send_all(parts[1:], "dp", PEERS))
    diagonals = gather_group(own)
    crosses = gather_group(over_chips(mine))
    m, e, f, keep, give = first(place, diagonals, crosses, x, [pieces[1], p2, p3], ahead)

    parts = fold(keep, send(give, "feat", 1))
    parts, e = lax.optimization_barrier((parts, e))
    mine = total([parts[0]] + send_all(parts[1:], "dp", PEERS))
    early = send_all([e] * len(PEERS), "dp", PEERS)
    bundle = over_chips(mine)
    bundle, f = lax.optimization_barrier((bundle, f))
    bundles = gather_group(bundle)
    early += send_all([f] * len(PEERS), "dp", PEERS)
    a, b, e, w = second(place, bundles, m, ahead)

    ax, by = send(a, "dp", 1), send(b, "dp", 2)
    bx, ay = send(b, "dp", 1), send(a, "dp", 2)
    ad, bd = send(ax, "dp", 2), send(by, "dp", 1)
    left, right = 2 * ahead, ahead + share // 2
    out = late(place, w, a, b, e, early, share)
    out = put(place, out, [ax, by], ((1, left), (2, right)), share)
    out = put(place, out, [bx, ay], ((1, right), (2, left)), share)
    out = put(place, out, [ad, bd], ((3, left), (3, right)), share)
    return out[None]


def solution(mesh):
    spec = P("dp", None, "feat")
    return jax.shard_map(run, mesh=mesh, in_specs=(spec,), out_specs=spec, check_vma=False)
```

```python
import functools

import jax
import jax.numpy as jnp
from jax import lax
from jax.experimental import pallas as pl
from jax.experimental.pallas import tpu as pltpu
from jax.sharding import PartitionSpec as P


LEVELS = 2
GROUP = 2**LEVELS
CORES = 2
F32, BF16 = jnp.float32, jnp.bfloat16
NT = (((1,), (1,)), ((), ()))
NN = (((1,), (0,)), ((), ()))
VMEM = pl.BlockSpec(memory_space=pltpu.VMEM)
SMEM = pl.BlockSpec(memory_space=pltpu.SMEM)
ANY = pl.BlockSpec(memory_space=pl.ANY)
HBM = pl.BlockSpec(memory_space=pltpu.HBM)


def send(block, axis, shift):
    count = lax.axis_size(axis)
    return lax.ppermute(block, axis, [(i, i ^ shift) for i in range(count)])


def send_all(blocks, axis, shifts):
    return [send(b, axis, s) for b, s in zip(blocks, shifts)]


def dot(a, b, dims=NN):
    return lax.dot_general(a, b, dims, preferred_element_type=F32)


def shape(*dims, dtype=F32):
    return jax.ShapeDtypeStruct(dims, dtype)


WHOLE = pltpu.CompilerParams(vmem_limit_bytes=67_043_328)


def cost(flops, nbytes):
    return pl.CostEstimate(flops=int(flops), bytes_accessed=int(nbytes), transcendentals=0)


def halves(a):
    high = a.astype(BF16)
    return high, (a - high.astype(F32)).astype(BF16)


def product(a, b, dims=NN):
    (ah, al), (bh, bl) = a, b
    return dot(ah, bh, dims) + (dot(ah, bl, dims) + dot(al, bh, dims))


def eye_mask(n):
    return lax.broadcasted_iota(jnp.int32, (n, n), 0) == lax.broadcasted_iota(jnp.int32, (n, n), 1)


def invert(kernels, x_ref, limit):
    n = kernels[0].shape[0]
    mask = eye_mask(n)
    eye = jnp.where(mask, 1.0, 0.0)
    parts = [halves(k) for k in kernels]
    for j, k in enumerate(kernels):
        diag = jnp.where(mask, k, 0.0)
        row = 1.0 / jnp.sum(diag, axis=0, keepdims=True)
        col = 1.0 / jnp.sum(diag, axis=1, keepdims=True)
        scaled = jnp.where(mask, 0.0, k) * row
        spread = jnp.sum(scaled * (jnp.where(mask, 0.0, k) * col))
        bound = jnp.minimum(jnp.max(jnp.sum(jnp.abs(k), axis=1, keepdims=True)), limit)
        near = jnp.where(mask, row, -scaled * col)
        far = eye * (2.0 / (1.0 + bound))
        x_ref[j] = jnp.where(spread < 0.9, near, far)

    def step(state):
        count, _ = state
        worst = jnp.float32(0.0)
        for j, part in enumerate(parts):
            x = x_ref[j]
            xs = halves(x)
            rest = eye - product(part, xs)
            worst = jnp.maximum(worst, jnp.sum(rest * rest))
            x_ref[j] = x + dot(xs[0], rest.astype(BF16))
        return count + 1, worst

    lax.while_loop(lambda s: (s[0] < 24) & (s[1] > 1e-6), step, (jnp.int32(0), jnp.float32(1.0)))


def resolvent(grams, x_ref, out_ref):
    n = grams[0][0].shape[0]
    mask = eye_mask(n)
    eye = jnp.where(mask, 1.0, 0.0)
    scaled = []
    for a, b, d in grams:
        average = jnp.sum(jnp.where(mask, a + d, 0.0)) / (2 * n)
        scaled.append((eye + a / average, b / average, eye + d / average))
    limit = 1.0 + 2 * n
    invert([d for _, _, d in scaled], x_ref, limit)
    ties, schurs = [], []
    for j, (a, b, d) in enumerate(scaled):
        bs = halves(b)
        tie = halves(product(bs, halves(x_ref[j])))
        ties.append(tie)
        schurs.append(a - product(tie, bs, NT))
    invert(schurs, x_ref, limit)
    for j, tie in enumerate(ties):
        x = x_ref[j]
        out_ref[j, :, :n] = x.astype(BF16)
        out_ref[j, :, n:] = (-product(halves(x), tie)).astype(BF16)


def own_gram_kernel(place, x_ref, keep_ref, give_ref, acc):
    step = pl.program_id(0)
    core = place[1]
    half = keep_ref.shape[0]

    @pl.when(step == 0)
    def _():
        acc[...] = jnp.zeros_like(acc)

    acc[...] += dot(x_ref[...], x_ref[...], NT)

    @pl.when(step == pl.num_programs(0) - 1)
    def _():
        keep_ref[...] = acc[pl.ds(pl.multiple_of(core * half, half), half), :]
        give_ref[...] = acc[pl.ds(pl.multiple_of((1 - core) * half, half), half), :]


def own_gram(place, x, tile=2048):
    rows, columns = x.shape
    half = shape(rows // CORES, rows)
    spec = pl.BlockSpec((rows // CORES, rows), lambda k, place: (0, 0))
    return pl.pallas_call(
        own_gram_kernel,
        out_shape=(half, half),
        grid_spec=pltpu.PrefetchScalarGridSpec(
            num_scalar_prefetch=1,
            grid=(columns // tile,),
            in_specs=[pl.BlockSpec((rows, tile), lambda k, place: (0, k))],
            out_specs=(spec, spec),
            scratch_shapes=[pltpu.VMEM((rows, rows), F32)],
        ),
        cost_estimate=cost(2 * rows * rows * columns, 2 * rows * columns),
        name="own_gram",
    )(place, x)


def pair_gram(me, sources, block, load, chunk):
    rows, share = block.shape[1:]
    copies = []
    for k in range(share // chunk):
        here = slice(k * chunk, (k + 1) * chunk)
        for i, (s, source) in enumerate(sources):
            target = block.at[(me ^ s) % 2, :, here]
            copies.append(pltpu.make_async_copy(source(k * chunk, chunk), target, load.at[2 * k + i]))
            copies[-1].start()
    value = jnp.zeros((rows, rows), F32)
    for k in range(share // chunk):
        copies[2 * k].wait()
        copies[2 * k + 1].wait()
        here = slice(k * chunk, (k + 1) * chunk)
        value = value + dot(block[0, :, here], block[1, :, here], NT)
    return value


def near_gram_kernel(chunk, place, x, p1, out_ref, block, load):
    me = place[0]
    share = p1.shape[1]

    def mine(column, size):
        return x.at[:, pl.ds(pl.multiple_of(me * share + column, 128), size)]

    def theirs(column, size):
        return p1.at[:, column : column + size]

    out_ref[...] = pair_gram(me, ((0, mine), (1, theirs)), block, load, chunk)


def near_gram(place, x, p1, chunk=512):
    rows, share = p1.shape
    return pl.pallas_call(
        functools.partial(near_gram_kernel, chunk),
        out_shape=shape(rows, rows),
        in_specs=[SMEM, HBM, HBM],
        out_specs=VMEM,
        scratch_shapes=[pltpu.VMEM((2, rows, share), BF16), pltpu.SemaphoreType.DMA((2 * share // chunk,))],
        cost_estimate=cost(2 * rows * rows * share, 4 * rows * share),
        compiler_params=WHOLE,
        name="near_gram",
    )(place, x, p1)


def far_gram_kernel(chunk, place, near, p2, p3, keep_ref, give_ref, block, acc, load):
    me, core = place[0], place[1]
    sources = tuple((s, lambda column, size, p=p: p.at[:, column : column + size]) for s, p in ((2, p2), (3, p3)))
    acc[me // 2] = near[...]
    acc[1 - me // 2] = pair_gram(me, sources, block, load, chunk)
    part = keep_ref.shape[1]
    for s in range(GROUP):
        to = me ^ s
        pair, start = to // 2, (to % 2) * (CORES * part)
        keep_ref[s] = acc[pair, pl.ds(pl.multiple_of(start + core * part, part), part), :]
        give_ref[s] = acc[pair, pl.ds(pl.multiple_of(start + (1 - core) * part, part), part), :]


def far_gram(place, near, p2, p3, chunk=512):
    rows, share = p2.shape
    out = shape(GROUP, rows // (2 * CORES), rows)
    return pl.pallas_call(
        functools.partial(far_gram_kernel, chunk),
        out_shape=(out, out),
        in_specs=[SMEM, VMEM, HBM, HBM],
        out_specs=(VMEM, VMEM),
        scratch_shapes=[
            pltpu.VMEM((2, rows, share), BF16),
            pltpu.VMEM((GROUP // 2, rows, rows), F32),
            pltpu.SemaphoreType.DMA((2 * share // chunk,)),
        ],
        cost_estimate=cost(2 * rows * rows * share, 4 * rows * share),
        compiler_params=WHOLE,
        name="far_gram",
    )(place, near, p2, p3)


def fold(mine, theirs):
    return [mine[s] + theirs[s] for s in range(mine.shape[0])]


def total(arrays):
    return functools.reduce(jnp.add, arrays)


def merge_rows(stacked, w):
    lower = stacked[: w.shape[0]]
    return (lower.astype(F32) - dot(w, stacked)).astype(BF16)


def first_kernel(tile, *refs):
    place, tails, crosses, (x, p1, p2, p3), refs = refs[0], refs[1:9], refs[9:17], refs[17:21], refs[21:]
    m_ref, e_ref, f_ref, keep_ref, give_ref, cross, diag, inverse, w, block, m, acc, load, save = refs
    ahead = e_ref.shape[1]
    me, core = place[0], place[1]
    rows, share = p1.shape
    sources = [x.at[:, pl.ds(pl.multiple_of(me * share, share), share)], p1, p2, p3]
    loads = [
        pltpu.make_async_copy(source, block.at[pl.ds(pl.multiple_of((me ^ s) * rows, rows), rows)], load.at[s])
        for s, source in enumerate(sources)
    ]
    for copy in loads:
        copy.start()

    part, half = rows // (2 * CORES), rows // CORES
    for c in range(CORES):
        for s in range(GROUP):
            source, seat = me ^ s, core ^ c
            start = (source % 2) * (CORES * part) + seat * part
            cross[source // 2, pl.ds(pl.multiple_of(start, part), part), :] = crosses[c * GROUP + s][...]
            diag[source, pl.ds(pl.multiple_of(seat * half, half), half), :] = tails[c * GROUP + s][...]
    grams = [(diag[2 * j], cross[j], diag[2 * j + 1]) for j in range(GROUP // 2)]
    resolvent(grams, inverse, w)
    for copy in loads:
        copy.wait()

    acc[...] = jnp.zeros_like(acc)
    saves = []
    for k in range(share // tile):
        here = slice(k * tile, (k + 1) * tile)
        m0 = merge_rows(block[: 2 * rows, here], w[0])
        m1 = merge_rows(block[2 * rows :, here], w[1])
        m[:rows, here] = m0
        m[rows:, here] = m1
        saves.append(pltpu.make_async_copy(m.at[:, here], m_ref.at[:, here], save.at[k]))
        saves[-1].start()
        acc[0] += dot(m0, m0, NT)
        acc[1] += dot(m0, m1, NT)
        acc[2] += dot(m1, m1, NT)
    for i, ref in enumerate((e_ref, f_ref)):
        source = m.at[:, i * ahead : (i + 1) * ahead]
        saves.append(pltpu.make_async_copy(source, ref, save.at[share // tile + i]))
        saves[-1].start()
    part = rows // (GROUP * CORES)
    for s in range(GROUP):
        to = me ^ s
        for b in range(3):
            here = pl.ds(b * part, part)
            keep_ref[s, here, :] = acc[b, pl.ds(pl.multiple_of((to * CORES + core) * part, part), part), :]
            give_ref[s, here, :] = acc[b, pl.ds(pl.multiple_of((to * CORES + 1 - core) * part, part), part), :]
    for copy in saves:
        copy.wait()


def first(place, diagonals, crosses, x, pieces, ahead, tile=512):
    rows, share = pieces[0].shape
    pairs = GROUP // 2
    out = shape(GROUP, 3 * rows // (GROUP * CORES), rows)
    return pl.pallas_call(
        functools.partial(first_kernel, tile),
        out_shape=tuple(shape(pairs * rows, n, dtype=BF16) for n in (share, ahead, ahead)) + (out, out),
        in_specs=[SMEM] + [VMEM] * (4 * GROUP) + [HBM] * 4,
        out_specs=(ANY, ANY, ANY, VMEM, VMEM),
        scratch_shapes=[
            pltpu.VMEM((pairs, rows, rows), F32),
            pltpu.VMEM((GROUP, rows, rows), F32),
            pltpu.VMEM((pairs, rows, rows), F32),
            pltpu.VMEM((pairs, rows, 2 * rows), BF16),
            pltpu.VMEM((GROUP * rows, share), BF16),
            pltpu.VMEM((pairs * rows, share), BF16),
            pltpu.VMEM((3, rows, rows), F32),
            pltpu.SemaphoreType.DMA((GROUP,)),
            pltpu.SemaphoreType.DMA((share // tile + 2,)),
        ],
        cost_estimate=cost(2 * pairs * rows**3 * 40 + 14 * rows * rows * share, 12 * rows * share),
        name="first",
    )(place, *diagonals, *crosses, x, *pieces)


def second_kernel(*refs):
    place, bundles, m_ref, refs = refs[0], refs[1:9], refs[9], refs[10:]
    a_ref, b_ref, e_ref, w_ref, gram, inverse, m, load = refs
    me, core = place[0], place[1]
    rows = m.shape[0] // 2
    copy = pltpu.make_async_copy(m_ref, m, load)
    copy.start()
    part = rows // (GROUP * CORES)
    for c in range(CORES):
        for s in range(GROUP):
            seat = (me ^ s) * CORES + (core ^ c)
            for b in range(3):
                gram[b, pl.ds(pl.multiple_of(seat * part, part), part), :] = bundles[c * GROUP + s][b * part : (b + 1) * part]
    resolvent([(gram[0], gram[1], gram[2])], inverse, w_ref)
    copy.wait()
    start = 0
    for ref in (e_ref, a_ref, b_ref):
        here = slice(start, start + ref.shape[1])
        ref[...] = merge_rows(m[:, here], w_ref[0])
        start += ref.shape[1]


def second(place, bundles, m, ahead):
    rows, share = m.shape[0] // 2, m.shape[1]
    early, half = 2 * ahead, share // 2 - ahead
    return pl.pallas_call(
        second_kernel,
        out_shape=tuple(shape(rows, n, dtype=BF16) for n in (half, half, early)) + (shape(1, rows, 2 * rows, dtype=BF16),),
        in_specs=[SMEM] + [VMEM] * (2 * GROUP) + [ANY],
        out_specs=(VMEM,) * 4,
        scratch_shapes=[
            pltpu.VMEM((3, rows, rows), F32),
            pltpu.VMEM((1, rows, rows), F32),
            pltpu.VMEM(m.shape, BF16),
            pltpu.SemaphoreType.DMA,
        ],
        cost_estimate=cost(2 * rows**3 * 40 + 4 * rows * rows * share, 6 * rows * share),
        name="second",
    )(place, *bundles, m)


def late_kernel(share, place, w, a, b, e, *refs):
    early, (out, buffer, save) = refs[:-3], refs[-3:]
    me, ahead, half = place[0], e.shape[1] // 2, a.shape[1]
    saves = []

    def put(source, owner, column):
        target = out.at[:, pl.ds(pl.multiple_of(owner * share + column, 128), source.shape[1])]
        saves.append(pltpu.make_async_copy(source, target, save.at[len(saves)]))
        saves[-1].start()

    put(e, me, 0)
    put(a, me, 2 * ahead)
    put(b, me, 2 * ahead + half)
    for i, pair in enumerate(early):
        buffer[i] = merge_rows(pair[...], w[0])
        put(buffer.at[i], me ^ (i % (GROUP - 1) + 1), i // (GROUP - 1) * ahead)
    for copy in saves:
        copy.wait()


def late(place, w, a, b, e, early, share):
    rows, ahead = e.shape[0], e.shape[1] // 2
    return pl.pallas_call(
        functools.partial(late_kernel, share),
        out_shape=shape(rows, GROUP * share, dtype=BF16),
        in_specs=[SMEM] + [VMEM] * (4 + len(early)),
        out_specs=HBM,
        scratch_shapes=[pltpu.VMEM((len(early), rows, ahead), BF16), pltpu.SemaphoreType.DMA((len(early) + 3,))],
        cost_estimate=cost(4 * rows * rows * ahead * len(early), 6 * rows * ahead * len(early)),
        name="late",
    )(place, w, a, b, e, *early)


def put_kernel(spots, share, place, *refs):
    count = len(spots)
    blocks, out, buffers, load, save = refs[:count], refs[count + 1], refs[count + 2 : -2], refs[-2], refs[-1]
    loads, saves = [], []
    for i, ((s, column), block, buffer) in enumerate(zip(spots, blocks, buffers)):
        start = pl.multiple_of((place[0] ^ s) * share + column, 128)
        loads.append(pltpu.make_async_copy(block, buffer, load.at[i]))
        loads[-1].start()
        saves.append(pltpu.make_async_copy(buffer, out.at[:, pl.ds(start, block.shape[1])], save.at[i]))
    for load_copy, save_copy in zip(loads, saves):
        load_copy.wait()
        save_copy.start()
    for copy in saves:
        copy.wait()


def put(place, out, blocks, spots, share):
    size = sum(b.size for b in blocks)
    return pl.pallas_call(
        functools.partial(put_kernel, spots, share),
        out_shape=shape(*out.shape, dtype=out.dtype),
        in_specs=[SMEM] + [HBM] * (len(blocks) + 1),
        out_specs=HBM,
        scratch_shapes=[pltpu.VMEM(b.shape, b.dtype) for b in blocks] + [pltpu.SemaphoreType.DMA((len(blocks),))] * 2,
        input_output_aliases={1 + len(blocks): 0},
        cost_estimate=cost(0, 4 * size),
        compiler_params=WHOLE,
        name="put",
    )(place, *blocks, out)


PEERS = tuple(range(1, GROUP))


def over_chips(block):
    chips = lax.axis_size("feat") // CORES
    return total([block] + [send(block, "feat", CORES * s) for s in range(1, chips)])


def gather_group(bundle):
    mine = [bundle] + send_all([bundle] * len(PEERS), "dp", PEERS)
    return mine + [send(b, "feat", 1) for b in mine]


def run(sketches):
    x = sketches[0]
    rows, columns = x.shape
    share = columns // GROUP
    ahead = share // 8
    me = lax.axis_index("dp") % GROUP
    place = jnp.stack([me, lax.axis_index("feat") % CORES]).astype(jnp.int32)

    pieces, source = {}, x
    for s in PEERS:
        piece = lax.dynamic_slice(source, (0, (me ^ s) * share), (rows, share))
        source, piece = lax.optimization_barrier((source, piece))
        pieces[s] = send(piece, "dp", s)
    keep, give = own_gram(place, x)
    own = over_chips(total([keep, send(give, "feat", 1)]))
    near = near_gram(place, x, pieces[1])
    p2, p3, own, near = lax.optimization_barrier((pieces[2], pieces[3], own, near))

    keep, give = far_gram(place, near, p2, p3)
    parts = fold(keep, send(give, "feat", 1))
    parts, own = lax.optimization_barrier((parts, own))
    mine = total([parts[0]] + send_all(parts[1:], "dp", PEERS))
    diagonals = gather_group(own)
    crosses = gather_group(over_chips(mine))
    m, e, f, keep, give = first(place, diagonals, crosses, x, [pieces[1], p2, p3], ahead)

    parts = fold(keep, send(give, "feat", 1))
    parts, e = lax.optimization_barrier((parts, e))
    mine = total([parts[0]] + send_all(parts[1:], "dp", PEERS))
    early = send_all([e] * len(PEERS), "dp", PEERS)
    bundle = over_chips(mine)
    bundle, f = lax.optimization_barrier((bundle, f))
    bundles = gather_group(bundle)
    early += send_all([f] * len(PEERS), "dp", PEERS)
    a, b, e, w = second(place, bundles, m, ahead)

    ax, by = send(a, "dp", 1), send(b, "dp", 2)
    bx, ay = send(b, "dp", 1), send(a, "dp", 2)
    ad, bd = send(ax, "dp", 2), send(by, "dp", 1)
    left, right = 2 * ahead, ahead + share // 2
    out = late(place, w, a, b, e, early, share)
    out = put(place, out, [ax, by], ((1, left), (2, right)), share)
    out = put(place, out, [bx, ay], ((1, right), (2, left)), share)
    out = put(place, out, [ad, bd], ((3, left), (3, right)), share)
    return out[None]


def solution(mesh):
    spec = P("dp", None, "feat")
    return jax.shard_map(run, mesh=mesh, in_specs=(spec,), out_specs=spec, check_vma=False)
```

```python
import functools

import jax
import jax.numpy as jnp
from jax import lax
from jax.experimental import pallas as pl
from jax.experimental.pallas import tpu as pltpu
from jax.sharding import PartitionSpec as P


LEVELS = 2
GROUP = 2**LEVELS
CORES = 2
F32, BF16 = jnp.float32, jnp.bfloat16
NT = (((1,), (1,)), ((), ()))
NN = (((1,), (0,)), ((), ()))
VMEM = pl.BlockSpec(memory_space=pltpu.VMEM)
SMEM = pl.BlockSpec(memory_space=pltpu.SMEM)
ANY = pl.BlockSpec(memory_space=pl.ANY)
HBM = pl.BlockSpec(memory_space=pltpu.HBM)


def send(block, axis, shift):
    count = lax.axis_size(axis)
    return lax.ppermute(block, axis, [(i, i ^ shift) for i in range(count)])


def send_all(blocks, axis, shifts):
    return [send(b, axis, s) for b, s in zip(blocks, shifts)]


def dot(a, b, dims=NN):
    return lax.dot_general(a, b, dims, preferred_element_type=F32)


def shape(*dims, dtype=F32):
    return jax.ShapeDtypeStruct(dims, dtype)


WHOLE = pltpu.CompilerParams(vmem_limit_bytes=67_043_328)


def cost(flops, nbytes):
    return pl.CostEstimate(flops=int(flops), bytes_accessed=int(nbytes), transcendentals=0)


def halves(a):
    high = a.astype(BF16)
    return high, (a - high.astype(F32)).astype(BF16)


def product(a, b, dims=NN):
    (ah, al), (bh, bl) = a, b
    return dot(ah, bh, dims) + (dot(ah, bl, dims) + dot(al, bh, dims))


def eye_mask(n):
    return lax.broadcasted_iota(jnp.int32, (n, n), 0) == lax.broadcasted_iota(jnp.int32, (n, n), 1)


def invert(kernels, x_ref, limit):
    n = kernels[0].shape[0]
    mask = eye_mask(n)
    eye = jnp.where(mask, 1.0, 0.0)
    parts = [halves(k) for k in kernels]
    for j, k in enumerate(kernels):
        diag = jnp.where(mask, k, 0.0)
        row = 1.0 / jnp.sum(diag, axis=0, keepdims=True)
        col = 1.0 / jnp.sum(diag, axis=1, keepdims=True)
        scaled = jnp.where(mask, 0.0, k) * row
        spread = jnp.sum(scaled * (jnp.where(mask, 0.0, k) * col))
        bound = jnp.minimum(jnp.max(jnp.sum(jnp.abs(k), axis=1, keepdims=True)), limit)
        near = jnp.where(mask, row, -scaled * col)
        far = eye * (2.0 / (1.0 + bound))
        x_ref[j] = jnp.where(spread < 0.9, near, far)

    def step(state):
        count, _ = state
        worst = jnp.float32(0.0)
        for j, part in enumerate(parts):
            x = x_ref[j]
            xs = halves(x)
            rest = eye - product(part, xs)
            worst = jnp.maximum(worst, jnp.sum(rest * rest))
            x_ref[j] = x + dot(xs[0], rest.astype(BF16))
        return count + 1, worst

    lax.while_loop(lambda s: (s[0] < 24) & (s[1] > 1e-6), step, (jnp.int32(0), jnp.float32(1.0)))


def resolvent(grams, x_ref, out_ref):
    n = grams[0][0].shape[0]
    mask = eye_mask(n)
    eye = jnp.where(mask, 1.0, 0.0)
    scaled = []
    for a, b, d in grams:
        average = jnp.sum(jnp.where(mask, a + d, 0.0)) / (2 * n)
        scaled.append((eye + a / average, b / average, eye + d / average))
    limit = 1.0 + 2 * n
    invert([d for _, _, d in scaled], x_ref, limit)
    ties, schurs = [], []
    for j, (a, b, d) in enumerate(scaled):
        bs = halves(b)
        tie = halves(product(bs, halves(x_ref[j])))
        ties.append(tie)
        schurs.append(a - product(tie, bs, NT))
    invert(schurs, x_ref, limit)
    for j, tie in enumerate(ties):
        x = x_ref[j]
        out_ref[j, :, :n] = x.astype(BF16)
        out_ref[j, :, n:] = (-product(halves(x), tie)).astype(BF16)


def own_gram_kernel(place, x_ref, keep_ref, give_ref, acc):
    step = pl.program_id(0)
    core = place[1]
    half = keep_ref.shape[0]

    @pl.when(step == 0)
    def _():
        acc[...] = jnp.zeros_like(acc)

    acc[...] += dot(x_ref[...], x_ref[...], NT)

    @pl.when(step == pl.num_programs(0) - 1)
    def _():
        keep_ref[...] = acc[pl.ds(pl.multiple_of(core * half, half), half), :]
        give_ref[...] = acc[pl.ds(pl.multiple_of((1 - core) * half, half), half), :]


def own_gram(place, x, tile=2048):
    rows, columns = x.shape
    half = shape(rows // CORES, rows)
    spec = pl.BlockSpec((rows // CORES, rows), lambda k, place: (0, 0))
    return pl.pallas_call(
        own_gram_kernel,
        out_shape=(half, half),
        grid_spec=pltpu.PrefetchScalarGridSpec(
            num_scalar_prefetch=1,
            grid=(columns // tile,),
            in_specs=[pl.BlockSpec((rows, tile), lambda k, place: (0, k))],
            out_specs=(spec, spec),
            scratch_shapes=[pltpu.VMEM((rows, rows), F32)],
        ),
        cost_estimate=cost(2 * rows * rows * columns, 2 * rows * columns),
        name="own_gram",
    )(place, x)


def pair_gram(me, sources, block, load, chunk):
    rows, share = block.shape[1:]
    copies = []
    for k in range(share // chunk):
        here = slice(k * chunk, (k + 1) * chunk)
        for i, (s, source) in enumerate(sources):
            target = block.at[(me ^ s) % 2, :, here]
            copies.append(pltpu.make_async_copy(source(k * chunk, chunk), target, load.at[2 * k + i]))
            copies[-1].start()
    value = jnp.zeros((rows, rows), F32)
    for k in range(share // chunk):
        copies[2 * k].wait()
        copies[2 * k + 1].wait()
        here = slice(k * chunk, (k + 1) * chunk)
        value = value + dot(block[0, :, here], block[1, :, here], NT)
    return value


SHARES_X, SHARES_Y = (0, 2, 3), (0, 1, 3)


def near_gram_kernel(chunk, place, x, p1, out_ref, x_ref, y_ref, d_ref, block, pack, load, save):
    me = place[0]
    share, raw = p1.shape[1], d_ref.shape[1]

    def mine(column, size, t=0):
        return x.at[:, pl.ds(pl.multiple_of((me ^ t) * share + column, 128), size)]

    def theirs(column, size):
        return p1.at[:, column : column + size]

    packs = [pltpu.make_async_copy(mine(0, raw, t), pack.at[t], save.at[t]) for t in range(GROUP)]
    packs.append(pltpu.make_async_copy(theirs(0, raw), pack.at[GROUP], save.at[GROUP]))
    for copy in packs:
        copy.start()
    out_ref[...] = pair_gram(me, ((0, mine), (1, theirs)), block, load, chunk)
    for copy in packs:
        copy.wait()
    targets = [(t, x_ref.at[i]) for i, t in enumerate(SHARES_X)] + [(t, y_ref.at[i]) for i, t in enumerate(SHARES_Y)]
    targets += [(GROUP, y_ref.at[GROUP - 1]), (0, d_ref)]
    copies = [pltpu.make_async_copy(pack.at[t], target, save.at[i]) for i, (t, target) in enumerate(targets)]
    for copy in copies:
        copy.start()
    for copy in copies:
        copy.wait()


def near_gram(place, x, p1, raw, chunk=512):
    rows, share = p1.shape
    message = shape(GROUP, rows, raw, dtype=BF16)
    return pl.pallas_call(
        functools.partial(near_gram_kernel, chunk),
        out_shape=(shape(rows, rows), message, message, shape(rows, raw, dtype=BF16)),
        in_specs=[SMEM, HBM, HBM],
        out_specs=(VMEM, HBM, HBM, HBM),
        scratch_shapes=[
            pltpu.VMEM((2, rows, share), BF16),
            pltpu.VMEM((GROUP + 1, rows, raw), BF16),
            pltpu.SemaphoreType.DMA((2 * share // chunk,)),
            pltpu.SemaphoreType.DMA((2 * GROUP,)),
        ],
        cost_estimate=cost(2 * rows * rows * share, 4 * rows * share),
        compiler_params=WHOLE,
        name="near_gram",
    )(place, x, p1)


def far_gram_kernel(chunk, place, near, p2, p3, _, keep_ref, give_ref, x_ref, block, acc, load, save):
    me, core = place[0], place[1]
    sources = tuple((s, lambda column, size, p=p: p.at[:, column : column + size]) for s, p in ((2, p2), (3, p3)))
    acc[me // 2] = near[...]
    acc[1 - me // 2] = pair_gram(me, sources, block, load, chunk)
    copy = pltpu.make_async_copy(block.at[(me ^ 2) % 2, :, : x_ref.shape[2]], x_ref.at[GROUP - 1], save)
    copy.start()
    part = keep_ref.shape[1]
    for s in range(GROUP):
        to = me ^ s
        pair, start = to // 2, (to % 2) * (CORES * part)
        keep_ref[s] = acc[pair, pl.ds(pl.multiple_of(start + core * part, part), part), :]
        give_ref[s] = acc[pair, pl.ds(pl.multiple_of(start + (1 - core) * part, part), part), :]
    copy.wait()


def far_gram(place, near, p2, p3, message, chunk=512):
    rows, share = p2.shape
    out = shape(GROUP, rows // (2 * CORES), rows)
    return pl.pallas_call(
        functools.partial(far_gram_kernel, chunk),
        out_shape=(out, out, shape(*message.shape, dtype=BF16)),
        in_specs=[SMEM, VMEM, HBM, HBM, HBM],
        out_specs=(VMEM, VMEM, HBM),
        scratch_shapes=[
            pltpu.VMEM((2, rows, share), BF16),
            pltpu.VMEM((GROUP // 2, rows, rows), F32),
            pltpu.SemaphoreType.DMA((2 * share // chunk,)),
            pltpu.SemaphoreType.DMA,
        ],
        input_output_aliases={4: 2},
        cost_estimate=cost(2 * rows * rows * share, 4 * rows * share),
        compiler_params=WHOLE,
        name="far_gram",
    )(place, near, p2, p3, message)


def fold(mine, theirs):
    return [mine[s] + theirs[s] for s in range(mine.shape[0])]


def total(arrays):
    return functools.reduce(jnp.add, arrays)


def merge_rows(stacked, w):
    lower = stacked[: w.shape[0]]
    return (lower.astype(F32) - dot(w, stacked)).astype(BF16)


def first_kernel(raw, tile, *refs):
    place, tails, crosses, (x, p1, p2, p3), refs = refs[0], refs[1:9], refs[9:17], refs[17:21], refs[21:]
    m_ref, e_ref, f_ref, w, keep_ref, give_ref, cross, diag, inverse, block, m, acc, load, save = refs
    me, core = place[0], place[1]
    rows, share = p1.shape
    sources = [x.at[:, pl.ds(pl.multiple_of(me * share, share), share)], p1, p2, p3]
    loads = [
        pltpu.make_async_copy(source, block.at[pl.ds(pl.multiple_of((me ^ s) * rows, rows), rows)], load.at[s])
        for s, source in enumerate(sources)
    ]
    for copy in loads:
        copy.start()

    part, half = rows // (2 * CORES), rows // CORES
    for c in range(CORES):
        for s in range(GROUP):
            source, seat = me ^ s, core ^ c
            start = (source % 2) * (CORES * part) + seat * part
            cross[source // 2, pl.ds(pl.multiple_of(start, part), part), :] = crosses[c * GROUP + s][...]
            diag[source, pl.ds(pl.multiple_of(seat * half, half), half), :] = tails[c * GROUP + s][...]
    grams = [(diag[2 * j], cross[j], diag[2 * j + 1]) for j in range(GROUP // 2)]
    resolvent(grams, inverse, w)
    for copy in loads:
        copy.wait()

    acc[...] = jnp.zeros_like(acc)
    saves = []
    for k in range(share // tile):
        here = slice(k * tile, (k + 1) * tile)
        m0 = merge_rows(block[: 2 * rows, here], w[0])
        m1 = merge_rows(block[2 * rows :, here], w[1])
        m[:rows, here] = m0
        m[rows:, here] = m1
        saves.append(pltpu.make_async_copy(m.at[:, here], m_ref.at[:, here], save.at[k]))
        saves[-1].start()
        acc[0] += dot(m0, m0, NT)
        acc[1] += dot(m0, m1, NT)
        acc[2] += dot(m1, m1, NT)
    start = raw
    for i, ref in enumerate((e_ref, f_ref)):
        source = m.at[:, start : start + ref.shape[1]]
        saves.append(pltpu.make_async_copy(source, ref, save.at[share // tile + i]))
        saves[-1].start()
        start += ref.shape[1]
    part = rows // (GROUP * CORES)
    for s in range(GROUP):
        to = me ^ s
        for b in range(3):
            here = pl.ds(b * part, part)
            keep_ref[s, here, :] = acc[b, pl.ds(pl.multiple_of((to * CORES + core) * part, part), part), :]
            give_ref[s, here, :] = acc[b, pl.ds(pl.multiple_of((to * CORES + 1 - core) * part, part), part), :]
    for copy in saves:
        copy.wait()


def first(place, diagonals, crosses, x, pieces, raw, ahead, tile=512):
    rows, share = pieces[0].shape
    pairs = GROUP // 2
    out = shape(GROUP, 3 * rows // (GROUP * CORES), rows)
    return pl.pallas_call(
        functools.partial(first_kernel, raw, tile),
        out_shape=tuple(shape(pairs * rows, n, dtype=BF16) for n in (share, *ahead)) + (shape(pairs, rows, 2 * rows, dtype=BF16), out, out),
        in_specs=[SMEM] + [VMEM] * (4 * GROUP) + [HBM] * 4,
        out_specs=(ANY, ANY, ANY, VMEM, VMEM, VMEM),
        scratch_shapes=[
            pltpu.VMEM((pairs, rows, rows), F32),
            pltpu.VMEM((GROUP, rows, rows), F32),
            pltpu.VMEM((pairs, rows, rows), F32),
            pltpu.VMEM((GROUP * rows, share), BF16),
            pltpu.VMEM((pairs * rows, share), BF16),
            pltpu.VMEM((3, rows, rows), F32),
            pltpu.SemaphoreType.DMA((GROUP,)),
            pltpu.SemaphoreType.DMA((share // tile + 2,)),
        ],
        cost_estimate=cost(2 * pairs * rows**3 * 40 + 14 * rows * rows * share, 12 * rows * share),
        name="first",
    )(place, *diagonals, *crosses, x, *pieces)


def second_kernel(*refs):
    place, bundles, m_ref, refs = refs[0], refs[1:9], refs[9], refs[10:]
    a_ref, b_ref, e_ref, w_ref, gram, inverse, m, load = refs
    me, core = place[0], place[1]
    rows = m.shape[0] // 2
    copy = pltpu.make_async_copy(m_ref, m, load)
    copy.start()
    part = rows // (GROUP * CORES)
    for c in range(CORES):
        for s in range(GROUP):
            seat = (me ^ s) * CORES + (core ^ c)
            for b in range(3):
                gram[b, pl.ds(pl.multiple_of(seat * part, part), part), :] = bundles[c * GROUP + s][b * part : (b + 1) * part]
    resolvent([(gram[0], gram[1], gram[2])], inverse, w_ref)
    copy.wait()
    start = 0
    for ref in (e_ref, a_ref, b_ref):
        here = slice(start, start + ref.shape[1])
        ref[...] = merge_rows(m[:, here], w_ref[0])
        start += ref.shape[1]


def second(place, bundles, m, early):
    rows, share = m.shape[0] // 2, m.shape[1]
    half = (share - early) // 2
    return pl.pallas_call(
        second_kernel,
        out_shape=tuple(shape(rows, n, dtype=BF16) for n in (half, half, early)) + (shape(1, rows, 2 * rows, dtype=BF16),),
        in_specs=[SMEM] + [VMEM] * (2 * GROUP) + [ANY],
        out_specs=(VMEM,) * 4,
        scratch_shapes=[
            pltpu.VMEM((3, rows, rows), F32),
            pltpu.VMEM((1, rows, rows), F32),
            pltpu.VMEM(m.shape, BF16),
            pltpu.SemaphoreType.DMA,
        ],
        cost_estimate=cost(2 * rows**3 * 40 + 4 * rows * rows * share, 6 * rows * share),
        name="second",
    )(place, *bundles, m)


def late_kernel(share, raw, place, w, a, b, e, *refs):
    early, (out, buffer, save) = refs[:-3], refs[-3:]
    me, half = place[0], a.shape[1]
    saves = []

    def put(source, owner, column):
        target = out.at[:, pl.ds(pl.multiple_of(owner * share + column, 128), source.shape[1])]
        saves.append(pltpu.make_async_copy(source, target, save.at[len(saves)]))
        saves[-1].start()

    put(e, me, 0)
    put(a, me, e.shape[1])
    put(b, me, e.shape[1] + half)
    for i, pair in enumerate(early):
        s, size = i % (GROUP - 1), pair.shape[1]
        column = raw if i < GROUP - 1 else raw + early[0].shape[1]
        spot = buffer.at[s, :, column - raw : column - raw + size]
        spot[...] = merge_rows(pair[...], w[0])
        put(spot, me ^ (s + 1), column)
    for copy in saves:
        copy.wait()


def late(place, w, a, b, e, early, raw, share):
    rows, size = e.shape[0], e.shape[1] - raw
    return pl.pallas_call(
        functools.partial(late_kernel, share, raw),
        out_shape=shape(rows, GROUP * share, dtype=BF16),
        in_specs=[SMEM] + [VMEM] * (4 + len(early)),
        out_specs=HBM,
        scratch_shapes=[pltpu.VMEM((GROUP - 1, rows, size), BF16), pltpu.SemaphoreType.DMA((len(early) + 3,))],
        cost_estimate=cost(4 * rows * rows * size * (GROUP - 1), 6 * rows * size * (GROUP - 1)),
        name="late",
    )(place, w, a, b, e, *early)


def raw_merge_kernel(share, place, w0, w1, x, xs, ys, d, _, out, block, pair, buffer, load, save):
    me = place[0]
    rows, raw = d.shape
    saves = []
    sources = {}
    for v in range(1, GROUP):
        mine = x.at[:, pl.ds(pl.multiple_of((me ^ v) * share, 128), raw)]
        across = {1: xs.at[GROUP - 1], 2: ys.at[GROUP - 1], 3: d}[v]
        sources[v] = (mine, xs.at[SHARES_X.index(v ^ 1)], ys.at[SHARES_Y.index(v ^ 2)], across)
    loads = {}
    for v, group in sources.items():
        for s, source in enumerate(group):
            target = block.at[v - 1, pl.ds(pl.multiple_of((me ^ s) * rows, rows), rows)]
            loads[v, s] = pltpu.make_async_copy(source, target, load.at[(v - 1) * GROUP + s])
            loads[v, s].start()
    for v in sources:
        for s in range(GROUP):
            loads[v, s].wait()
        for j in range(GROUP // 2):
            pair[j * rows : (j + 1) * rows] = merge_rows(block[v - 1, 2 * j * rows : 2 * (j + 1) * rows], w0[j])
        buffer[v - 1] = merge_rows(pair[...], w1[0])
        target = out.at[:, pl.ds(pl.multiple_of((me ^ v) * share, 128), raw)]
        saves.append(pltpu.make_async_copy(buffer.at[v - 1], target, save.at[v - 1]))
        saves[-1].start()
    for copy in saves:
        copy.wait()


def raw_merge(place, w0, w1, x, messages, out, share):
    rows, raw = messages[2].shape
    return pl.pallas_call(
        functools.partial(raw_merge_kernel, share),
        out_shape=shape(*out.shape, dtype=BF16),
        in_specs=[SMEM, VMEM, VMEM] + [HBM] * 5,
        out_specs=HBM,
        scratch_shapes=[
            pltpu.VMEM((GROUP - 1, GROUP * rows, raw), BF16),
            pltpu.VMEM((2 * rows, raw), BF16),
            pltpu.VMEM((GROUP - 1, rows, raw), BF16),
            pltpu.SemaphoreType.DMA(((GROUP - 1) * GROUP,)),
            pltpu.SemaphoreType.DMA((GROUP - 1,)),
        ],
        input_output_aliases={7: 0},
        cost_estimate=cost(12 * rows * rows * raw * (GROUP - 1), 10 * rows * raw * (GROUP - 1)),
        compiler_params=WHOLE,
        name="raw_merge",
    )(place, w0, w1, x, *messages, out)


def put_kernel(spots, share, place, *refs):
    count = len(spots)
    blocks, out, buffers, load, save = refs[:count], refs[count + 1], refs[count + 2 : -2], refs[-2], refs[-1]
    loads, saves = [], []
    for i, ((s, column), block, buffer) in enumerate(zip(spots, blocks, buffers)):
        start = pl.multiple_of((place[0] ^ s) * share + column, 128)
        loads.append(pltpu.make_async_copy(block, buffer, load.at[i]))
        loads[-1].start()
        saves.append(pltpu.make_async_copy(buffer, out.at[:, pl.ds(start, block.shape[1])], save.at[i]))
    for load_copy, save_copy in zip(loads, saves):
        load_copy.wait()
        save_copy.start()
    for copy in saves:
        copy.wait()


def put(place, out, blocks, spots, share):
    size = sum(b.size for b in blocks)
    return pl.pallas_call(
        functools.partial(put_kernel, spots, share),
        out_shape=shape(*out.shape, dtype=out.dtype),
        in_specs=[SMEM] + [HBM] * (len(blocks) + 1),
        out_specs=HBM,
        scratch_shapes=[pltpu.VMEM(b.shape, b.dtype) for b in blocks] + [pltpu.SemaphoreType.DMA((len(blocks),))] * 2,
        input_output_aliases={1 + len(blocks): 0},
        cost_estimate=cost(0, 4 * size),
        compiler_params=WHOLE,
        name="put",
    )(place, *blocks, out)


PEERS = tuple(range(1, GROUP))


def over_chips(block):
    chips = lax.axis_size("feat") // CORES
    return total([block] + [send(block, "feat", CORES * s) for s in range(1, chips)])


def gather_group(bundle):
    mine = [bundle] + send_all([bundle] * len(PEERS), "dp", PEERS)
    return mine + [send(b, "feat", 1) for b in mine]


def run(sketches):
    x = sketches[0]
    rows, columns = x.shape
    share = columns // GROUP
    raw, ahead = 3 * share // 16, (3 * share // 16, share // 8)
    early = raw + sum(ahead)
    me = lax.axis_index("dp") % GROUP
    place = jnp.stack([me, lax.axis_index("feat") % CORES]).astype(jnp.int32)

    pieces, source = {}, x
    for s in PEERS:
        piece = lax.dynamic_slice(source, (0, (me ^ s) * share), (rows, share))
        source, piece = lax.optimization_barrier((source, piece))
        pieces[s] = send(piece, "dp", s)
    keep, give = own_gram(place, x)
    own = over_chips(total([keep, send(give, "feat", 1)]))
    near, to_x, to_y, to_d = near_gram(place, x, pieces[1], raw)
    p2, p3, own, near = lax.optimization_barrier((pieces[2], pieces[3], own, near))

    keep, give, to_x = far_gram(place, near, p2, p3, to_x)
    parts = fold(keep, send(give, "feat", 1))
    parts, own, to_d = lax.optimization_barrier((parts, own, to_d))
    mine = total([parts[0]] + send_all(parts[1:], "dp", PEERS))
    diagonals = gather_group(own)
    from_d = send(to_d, "dp", 3)
    bundle = over_chips(mine)
    bundle, to_x, to_y = lax.optimization_barrier((bundle, to_x, to_y))
    crosses = gather_group(bundle)
    messages = [send(to_x, "dp", 1), send(to_y, "dp", 2), from_d]
    m, e, f, w0, keep, give = first(place, diagonals, crosses, x, [pieces[1], p2, p3], raw, ahead)

    parts = fold(keep, send(give, "feat", 1))
    parts, e = lax.optimization_barrier((parts, e))
    mine = total([parts[0]] + send_all(parts[1:], "dp", PEERS))
    pairs = send_all([e] * len(PEERS), "dp", PEERS)
    bundle = over_chips(mine)
    bundle, f = lax.optimization_barrier((bundle, f))
    bundles = gather_group(bundle)
    pairs += send_all([f] * len(PEERS), "dp", PEERS)
    a, b, e, w1 = second(place, bundles, m, early)

    ax, by = send(a, "dp", 1), send(b, "dp", 2)
    bx, ay = send(b, "dp", 1), send(a, "dp", 2)
    ad, bd = send(ax, "dp", 2), send(by, "dp", 1)
    left, right = early, early + a.shape[1]
    out = late(place, w1, a, b, e, pairs, raw, share)
    out = raw_merge(place, w0, w1, x, messages, out, share)
    out = put(place, out, [ax, by, bx, ay], ((1, left), (2, right), (1, right), (2, left)), share)
    out = put(place, out, [ad, bd], ((3, left), (3, right)), share)
    return out[None]


def solution(mesh):
    spec = P("dp", None, "feat")
    return jax.shard_map(run, mesh=mesh, in_specs=(spec,), out_specs=spec, check_vma=False)
```

```python
import functools

import jax
import jax.numpy as jnp
from jax import lax
from jax.experimental import pallas as pl
from jax.experimental.pallas import tpu as pltpu
from jax.sharding import PartitionSpec as P


LEVELS = 2
GROUP = 2**LEVELS
CORES = 2
F32, BF16 = jnp.float32, jnp.bfloat16
NT = (((1,), (1,)), ((), ()))
NN = (((1,), (0,)), ((), ()))
VMEM = pl.BlockSpec(memory_space=pltpu.VMEM)
SMEM = pl.BlockSpec(memory_space=pltpu.SMEM)
ANY = pl.BlockSpec(memory_space=pl.ANY)
HBM = pl.BlockSpec(memory_space=pltpu.HBM)


def send(block, axis, shift):
    count = lax.axis_size(axis)
    return lax.ppermute(block, axis, [(i, i ^ shift) for i in range(count)])


def send_all(blocks, axis, shifts):
    return [send(b, axis, s) for b, s in zip(blocks, shifts)]


def dot(a, b, dims=NN):
    return lax.dot_general(a, b, dims, preferred_element_type=F32)


def shape(*dims, dtype=F32):
    return jax.ShapeDtypeStruct(dims, dtype)


WHOLE = pltpu.CompilerParams(vmem_limit_bytes=67_043_328)


def cost(flops, nbytes):
    return pl.CostEstimate(flops=int(flops), bytes_accessed=int(nbytes), transcendentals=0)


def halves(a):
    high = a.astype(BF16)
    return high, (a - high.astype(F32)).astype(BF16)


def product(a, b, dims=NN):
    (ah, al), (bh, bl) = a, b
    return dot(ah, bh, dims) + (dot(ah, bl, dims) + dot(al, bh, dims))


def eye_mask(n):
    return lax.broadcasted_iota(jnp.int32, (n, n), 0) == lax.broadcasted_iota(jnp.int32, (n, n), 1)


def invert(kernels, x_ref, limit):
    n = kernels[0].shape[0]
    mask = eye_mask(n)
    eye = jnp.where(mask, 1.0, 0.0)
    parts = [halves(k) for k in kernels]
    for j, k in enumerate(kernels):
        diag = jnp.where(mask, k, 0.0)
        row = 1.0 / jnp.sum(diag, axis=0, keepdims=True)
        col = 1.0 / jnp.sum(diag, axis=1, keepdims=True)
        scaled = jnp.where(mask, 0.0, k) * row
        spread = jnp.sum(scaled * (jnp.where(mask, 0.0, k) * col))
        bound = jnp.minimum(jnp.max(jnp.sum(jnp.abs(k), axis=1, keepdims=True)), limit)
        near = jnp.where(mask, row, -scaled * col)
        far = eye * (2.0 / (1.0 + bound))
        x_ref[j] = jnp.where(spread < 0.9, near, far)

    def step(state):
        count, _ = state
        worst = jnp.float32(0.0)
        for j, part in enumerate(parts):
            x = x_ref[j]
            xs = halves(x)
            rest = eye - product(part, xs)
            worst = jnp.maximum(worst, jnp.sum(rest * rest))
            x_ref[j] = x + dot(xs[0], rest.astype(BF16))
        return count + 1, worst

    lax.while_loop(lambda s: (s[0] < 24) & (s[1] > 1e-6), step, (jnp.int32(0), jnp.float32(1.0)))


def resolvent(grams, x_ref, out_ref):
    n = grams[0][0].shape[0]
    mask = eye_mask(n)
    eye = jnp.where(mask, 1.0, 0.0)
    scaled = []
    for a, b, d in grams:
        average = jnp.sum(jnp.where(mask, a + d, 0.0)) / (2 * n)
        scaled.append((eye + a / average, b / average, eye + d / average))
    limit = 1.0 + 2 * n
    invert([d for _, _, d in scaled], x_ref, limit)
    ties, schurs = [], []
    for j, (a, b, d) in enumerate(scaled):
        bs = halves(b)
        tie = halves(product(bs, halves(x_ref[j])))
        ties.append(tie)
        schurs.append(a - product(tie, bs, NT))
    invert(schurs, x_ref, limit)
    for j, tie in enumerate(ties):
        x = x_ref[j]
        out_ref[j, :, :n] = x.astype(BF16)
        out_ref[j, :, n:] = (-product(halves(x), tie)).astype(BF16)


def own_gram_kernel(place, x_ref, keep_ref, give_ref, acc):
    step = pl.program_id(0)
    core = place[1]
    half = keep_ref.shape[0]

    @pl.when(step == 0)
    def _():
        acc[...] = jnp.zeros_like(acc)

    acc[...] += dot(x_ref[...], x_ref[...], NT)

    @pl.when(step == pl.num_programs(0) - 1)
    def _():
        keep_ref[...] = acc[pl.ds(pl.multiple_of(core * half, half), half), :]
        give_ref[...] = acc[pl.ds(pl.multiple_of((1 - core) * half, half), half), :]


def own_gram(place, x, tile=2048):
    rows, columns = x.shape
    half = shape(rows // CORES, rows)
    spec = pl.BlockSpec((rows // CORES, rows), lambda k, place: (0, 0))
    return pl.pallas_call(
        own_gram_kernel,
        out_shape=(half, half),
        grid_spec=pltpu.PrefetchScalarGridSpec(
            num_scalar_prefetch=1,
            grid=(columns // tile,),
            in_specs=[pl.BlockSpec((rows, tile), lambda k, place: (0, k))],
            out_specs=(spec, spec),
            scratch_shapes=[pltpu.VMEM((rows, rows), F32)],
        ),
        cost_estimate=cost(2 * rows * rows * columns, 2 * rows * columns),
        name="own_gram",
    )(place, x)


def pair_gram(me, sources, block, load, chunk):
    rows, share = block.shape[1:]
    copies = []
    for k in range(share // chunk):
        here = slice(k * chunk, (k + 1) * chunk)
        for i, (s, source) in enumerate(sources):
            target = block.at[(me ^ s) % 2, :, here]
            copies.append(pltpu.make_async_copy(source(k * chunk, chunk), target, load.at[2 * k + i]))
            copies[-1].start()
    value = jnp.zeros((rows, rows), F32)
    for k in range(share // chunk):
        copies[2 * k].wait()
        copies[2 * k + 1].wait()
        here = slice(k * chunk, (k + 1) * chunk)
        value = value + dot(block[0, :, here], block[1, :, here], NT)
    return value


SHARES_X, SHARES_Y = (0, 2, 3), (0, 1, 3)


def near_gram_kernel(chunk, place, x, p1, out_ref, x_ref, y_ref, d_ref, block, pack, load, save):
    me = place[0]
    share, raw = p1.shape[1], d_ref.shape[1]

    def mine(column, size, t=0):
        return x.at[:, pl.ds(pl.multiple_of((me ^ t) * share + column, 128), size)]

    def theirs(column, size):
        return p1.at[:, column : column + size]

    packs = [pltpu.make_async_copy(mine(0, raw, t), pack.at[t], save.at[t]) for t in range(GROUP)]
    packs.append(pltpu.make_async_copy(theirs(0, raw), pack.at[GROUP], save.at[GROUP]))
    for copy in packs:
        copy.start()
    out_ref[...] = pair_gram(me, ((0, mine), (1, theirs)), block, load, chunk)
    for copy in packs:
        copy.wait()
    targets = [(t, x_ref.at[i]) for i, t in enumerate(SHARES_X)] + [(t, y_ref.at[i]) for i, t in enumerate(SHARES_Y)]
    targets += [(GROUP, y_ref.at[GROUP - 1]), (0, d_ref)]
    copies = [pltpu.make_async_copy(pack.at[t], target, save.at[i]) for i, (t, target) in enumerate(targets)]
    for copy in copies:
        copy.start()
    for copy in copies:
        copy.wait()


def near_gram(place, x, p1, raw, chunk=512):
    rows, share = p1.shape
    message = shape(GROUP, rows, raw, dtype=BF16)
    return pl.pallas_call(
        functools.partial(near_gram_kernel, chunk),
        out_shape=(shape(rows, rows), message, message, shape(rows, raw, dtype=BF16)),
        in_specs=[SMEM, HBM, HBM],
        out_specs=(VMEM, HBM, HBM, HBM),
        scratch_shapes=[
            pltpu.VMEM((2, rows, share), BF16),
            pltpu.VMEM((GROUP + 1, rows, raw), BF16),
            pltpu.SemaphoreType.DMA((2 * share // chunk,)),
            pltpu.SemaphoreType.DMA((2 * GROUP,)),
        ],
        cost_estimate=cost(2 * rows * rows * share, 4 * rows * share),
        compiler_params=WHOLE,
        name="near_gram",
    )(place, x, p1)


def far_gram_kernel(chunk, place, near, p2, p3, _, keep_out, give_out, x_ref, block, acc, keep_ref, give_ref, load, save):
    me, core = place[0], place[1]
    first_load = pltpu.make_async_copy(near, acc.at[me // 2], save.at[3])
    first_load.start()
    sources = tuple((s, lambda column, size, p=p: p.at[:, column : column + size]) for s, p in ((2, p2), (3, p3)))
    acc[1 - me // 2] = pair_gram(me, sources, block, load, chunk)
    copies = [pltpu.make_async_copy(block.at[(me ^ 2) % 2, :, : x_ref.shape[2]], x_ref.at[GROUP - 1], save.at[0])]
    copies[0].start()
    first_load.wait()
    part = keep_ref.shape[1]
    for s in range(GROUP):
        to = me ^ s
        pair, start = to // 2, (to % 2) * (CORES * part)
        keep_ref[s] = acc[pair, pl.ds(pl.multiple_of(start + core * part, part), part), :]
        give_ref[s] = acc[pair, pl.ds(pl.multiple_of(start + (1 - core) * part, part), part), :]
    for i, (source, target) in enumerate(((give_ref, give_out), (keep_ref, keep_out))):
        copies.append(pltpu.make_async_copy(source, target, save.at[1 + i]))
        copies[-1].start()
    for copy in copies:
        copy.wait()


def far_gram(place, near, p2, p3, message, chunk=512):
    rows, share = p2.shape
    out = shape(GROUP, rows // (2 * CORES), rows)
    return pl.pallas_call(
        functools.partial(far_gram_kernel, chunk),
        out_shape=(out, out, shape(*message.shape, dtype=BF16)),
        in_specs=[SMEM, HBM, HBM, HBM, HBM],
        out_specs=(HBM, HBM, HBM),
        scratch_shapes=[
            pltpu.VMEM((2, rows, share), BF16),
            pltpu.VMEM((GROUP // 2, rows, rows), F32),
            pltpu.VMEM(out.shape, F32),
            pltpu.VMEM(out.shape, F32),
            pltpu.SemaphoreType.DMA((2 * share // chunk,)),
            pltpu.SemaphoreType.DMA((4,)),
        ],
        input_output_aliases={4: 2},
        cost_estimate=cost(2 * rows * rows * share, 4 * rows * share),
        compiler_params=WHOLE,
        name="far_gram",
    )(place, near, p2, p3, message)


def fold(mine, theirs):
    return [mine[s] + theirs[s] for s in range(mine.shape[0])]


def total(arrays):
    return functools.reduce(jnp.add, arrays)


def merge_rows(stacked, w):
    lower = stacked[: w.shape[0]]
    return (lower.astype(F32) - dot(w, stacked)).astype(BF16)


def first_kernel(raw, tile, *refs):
    place, tails, crosses, (x, p1, p2, p3), refs = refs[0], refs[1:9], refs[9:17], refs[17:21], refs[21:]
    m_ref, e_ref, f_ref, w, keep_out, give_out, cross, diag, inverse, block, m, acc, keep_ref, give_ref, load, save = refs
    me, core = place[0], place[1]
    rows, share = p1.shape
    sources = [x.at[:, pl.ds(pl.multiple_of(me * share, share), share)], p1, p2, p3]
    loads = [
        pltpu.make_async_copy(source, block.at[pl.ds(pl.multiple_of((me ^ s) * rows, rows), rows)], load.at[s])
        for s, source in enumerate(sources)
    ]
    for copy in loads:
        copy.start()

    part, half = rows // (2 * CORES), rows // CORES
    for c in range(CORES):
        for s in range(GROUP):
            source, seat = me ^ s, core ^ c
            start = (source % 2) * (CORES * part) + seat * part
            cross[source // 2, pl.ds(pl.multiple_of(start, part), part), :] = crosses[c * GROUP + s][...]
            diag[source, pl.ds(pl.multiple_of(seat * half, half), half), :] = tails[c * GROUP + s][...]
    grams = [(diag[2 * j], cross[j], diag[2 * j + 1]) for j in range(GROUP // 2)]
    resolvent(grams, inverse, w)
    for copy in loads:
        copy.wait()

    acc[...] = jnp.zeros_like(acc)
    saves = []
    for k in range(share // tile):
        here = slice(k * tile, (k + 1) * tile)
        m0 = merge_rows(block[: 2 * rows, here], w[0])
        m1 = merge_rows(block[2 * rows :, here], w[1])
        m[:rows, here] = m0
        m[rows:, here] = m1
        saves.append(pltpu.make_async_copy(m.at[:, here], m_ref.at[:, here], save.at[k]))
        saves[-1].start()
        acc[0] += dot(m0, m0, NT)
        acc[1] += dot(m0, m1, NT)
        acc[2] += dot(m1, m1, NT)
    start = raw
    for i, ref in enumerate((e_ref, f_ref)):
        source = m.at[:, start : start + ref.shape[1]]
        saves.append(pltpu.make_async_copy(source, ref, save.at[share // tile + i]))
        saves[-1].start()
        start += ref.shape[1]
    lower = lax.broadcasted_iota(jnp.int32, (rows, rows), 0) >= lax.broadcasted_iota(jnp.int32, (rows, rows), 1)
    row = jnp.sum(jnp.where(eye_mask(rows), acc[2], 0.0), axis=0, keepdims=True)
    acc[2] = jnp.where(lower, acc[0], acc[2])
    part = rows // (GROUP * CORES)
    for s in range(GROUP):
        to = me ^ s
        for ref, seat in ((give_ref, to * CORES + 1 - core), (keep_ref, to * CORES + core)):
            here = pl.ds(pl.multiple_of(seat * part, part), part)
            ref[s, :part] = acc[1, here, :]
            ref[s, part : 2 * part] = acc[2, here, :]
            ref[s, 2 * part :] = jnp.broadcast_to(row, (8, rows))
    for i, (source, target) in enumerate(((give_ref, give_out), (keep_ref, keep_out))):
        saves.append(pltpu.make_async_copy(source, target, save.at[share // tile + 2 + i]))
        saves[-1].start()
    for copy in saves:
        copy.wait()


def first(place, diagonals, crosses, x, pieces, raw, ahead, tile=512):
    rows, share = pieces[0].shape
    pairs = GROUP // 2
    out = shape(GROUP, 2 * rows // (GROUP * CORES) + 8, rows)
    return pl.pallas_call(
        functools.partial(first_kernel, raw, tile),
        out_shape=tuple(shape(pairs * rows, n, dtype=BF16) for n in (share, *ahead)) + (shape(pairs, rows, 2 * rows, dtype=BF16), out, out),
        in_specs=[SMEM] + [VMEM] * (4 * GROUP) + [HBM] * 4,
        out_specs=(ANY, ANY, ANY, VMEM, ANY, ANY),
        scratch_shapes=[
            pltpu.VMEM((pairs, rows, rows), F32),
            pltpu.VMEM((GROUP, rows, rows), F32),
            pltpu.VMEM((pairs, rows, rows), F32),
            pltpu.VMEM((GROUP * rows, share), BF16),
            pltpu.VMEM((pairs * rows, share), BF16),
            pltpu.VMEM((3, rows, rows), F32),
            pltpu.VMEM(out.shape, F32),
            pltpu.VMEM(out.shape, F32),
            pltpu.SemaphoreType.DMA((GROUP,)),
            pltpu.SemaphoreType.DMA((share // tile + 4,)),
        ],
        cost_estimate=cost(2 * pairs * rows**3 * 40 + 14 * rows * rows * share, 12 * rows * share),
        name="first",
    )(place, *diagonals, *crosses, x, *pieces)


def second_kernel(*refs):
    place, bundles, m_ref, refs = refs[0], refs[1:9], refs[9], refs[10:]
    a_ref, b_ref, e_ref, w_ref, gram, inverse, m, load = refs
    me, core = place[0], place[1]
    rows = m.shape[0] // 2
    copy = pltpu.make_async_copy(m_ref, m, load)
    copy.start()
    part = rows // (GROUP * CORES)
    for c in range(CORES):
        for s in range(GROUP):
            seat = (me ^ s) * CORES + (core ^ c)
            for b in range(2):
                gram[b, pl.ds(pl.multiple_of(seat * part, part), part), :] = bundles[c * GROUP + s][b * part : (b + 1) * part]
    packed = gram[1]
    turned = packed.T
    lower = lax.broadcasted_iota(jnp.int32, (rows, rows), 0) >= lax.broadcasted_iota(jnp.int32, (rows, rows), 1)
    diagonal = jnp.broadcast_to(bundles[0][2 * part : 2 * part + 1], (rows, rows))
    upper_gram = jnp.where(eye_mask(rows), diagonal, jnp.where(lower, turned, packed))
    resolvent([(jnp.where(lower, packed, turned), gram[0], upper_gram)], inverse, w_ref)
    copy.wait()
    start = 0
    for ref in (e_ref, a_ref, b_ref):
        here = slice(start, start + ref.shape[1])
        ref[...] = merge_rows(m[:, here], w_ref[0])
        start += ref.shape[1]


def second(place, bundles, m, early):
    rows, share = m.shape[0] // 2, m.shape[1]
    half = (share - early) // 2
    return pl.pallas_call(
        second_kernel,
        out_shape=tuple(shape(rows, n, dtype=BF16) for n in (half, half, early)) + (shape(1, rows, 2 * rows, dtype=BF16),),
        in_specs=[SMEM] + [VMEM] * (2 * GROUP) + [ANY],
        out_specs=(VMEM,) * 4,
        scratch_shapes=[
            pltpu.VMEM((2, rows, rows), F32),
            pltpu.VMEM((1, rows, rows), F32),
            pltpu.VMEM(m.shape, BF16),
            pltpu.SemaphoreType.DMA,
        ],
        cost_estimate=cost(2 * rows**3 * 40 + 4 * rows * rows * share, 6 * rows * share),
        name="second",
    )(place, *bundles, m)


def late_kernel(share, raw, place, w, a, b, e, *refs):
    early, (out, buffer, save) = refs[:-3], refs[-3:]
    me, half = place[0], a.shape[1]
    saves = []

    def put(source, owner, column):
        target = out.at[:, pl.ds(pl.multiple_of(owner * share + column, 128), source.shape[1])]
        saves.append(pltpu.make_async_copy(source, target, save.at[len(saves)]))
        saves[-1].start()

    put(e, me, 0)
    put(a, me, e.shape[1])
    put(b, me, e.shape[1] + half)
    for i, pair in enumerate(early):
        s, size = i % (GROUP - 1), pair.shape[1]
        column = raw if i < GROUP - 1 else raw + early[0].shape[1]
        spot = buffer.at[s, :, column - raw : column - raw + size]
        spot[...] = merge_rows(pair[...], w[0])
        put(spot, me ^ (s + 1), column)
    for copy in saves:
        copy.wait()


def late(place, w, a, b, e, early, raw, share):
    rows, size = e.shape[0], e.shape[1] - raw
    return pl.pallas_call(
        functools.partial(late_kernel, share, raw),
        out_shape=shape(rows, GROUP * share, dtype=BF16),
        in_specs=[SMEM] + [VMEM] * (4 + len(early)),
        out_specs=HBM,
        scratch_shapes=[pltpu.VMEM((GROUP - 1, rows, size), BF16), pltpu.SemaphoreType.DMA((len(early) + 3,))],
        cost_estimate=cost(4 * rows * rows * size * (GROUP - 1), 6 * rows * size * (GROUP - 1)),
        name="late",
    )(place, w, a, b, e, *early)


def raw_merge_kernel(share, place, w0, w1, x, xs, ys, d, _, out, block, pair, buffer, load, save):
    me = place[0]
    rows, raw = d.shape
    saves = []
    sources = {}
    for v in range(1, GROUP):
        mine = x.at[:, pl.ds(pl.multiple_of((me ^ v) * share, 128), raw)]
        across = {1: xs.at[GROUP - 1], 2: ys.at[GROUP - 1], 3: d}[v]
        sources[v] = (mine, xs.at[SHARES_X.index(v ^ 1)], ys.at[SHARES_Y.index(v ^ 2)], across)
    loads = {}
    for v, group in sources.items():
        for s, source in enumerate(group):
            target = block.at[v - 1, pl.ds(pl.multiple_of((me ^ s) * rows, rows), rows)]
            loads[v, s] = pltpu.make_async_copy(source, target, load.at[(v - 1) * GROUP + s])
            loads[v, s].start()
    for v in sources:
        for s in range(GROUP):
            loads[v, s].wait()
        for j in range(GROUP // 2):
            pair[j * rows : (j + 1) * rows] = merge_rows(block[v - 1, 2 * j * rows : 2 * (j + 1) * rows], w0[j])
        buffer[v - 1] = merge_rows(pair[...], w1[0])
        target = out.at[:, pl.ds(pl.multiple_of((me ^ v) * share, 128), raw)]
        saves.append(pltpu.make_async_copy(buffer.at[v - 1], target, save.at[v - 1]))
        saves[-1].start()
    for copy in saves:
        copy.wait()


def raw_merge(place, w0, w1, x, messages, out, share):
    rows, raw = messages[2].shape
    return pl.pallas_call(
        functools.partial(raw_merge_kernel, share),
        out_shape=shape(*out.shape, dtype=BF16),
        in_specs=[SMEM, VMEM, VMEM] + [HBM] * 5,
        out_specs=HBM,
        scratch_shapes=[
            pltpu.VMEM((GROUP - 1, GROUP * rows, raw), BF16),
            pltpu.VMEM((2 * rows, raw), BF16),
            pltpu.VMEM((GROUP - 1, rows, raw), BF16),
            pltpu.SemaphoreType.DMA(((GROUP - 1) * GROUP,)),
            pltpu.SemaphoreType.DMA((GROUP - 1,)),
        ],
        input_output_aliases={7: 0},
        cost_estimate=cost(12 * rows * rows * raw * (GROUP - 1), 10 * rows * raw * (GROUP - 1)),
        compiler_params=WHOLE,
        name="raw_merge",
    )(place, w0, w1, x, *messages, out)


def put_kernel(spots, share, place, *refs):
    count = len(spots)
    blocks, out, buffers, load, save = refs[:count], refs[count + 1], refs[count + 2 : -2], refs[-2], refs[-1]
    loads, saves = [], []
    for i, ((s, column), block, buffer) in enumerate(zip(spots, blocks, buffers)):
        start = pl.multiple_of((place[0] ^ s) * share + column, 128)
        loads.append(pltpu.make_async_copy(block, buffer, load.at[i]))
        loads[-1].start()
        saves.append(pltpu.make_async_copy(buffer, out.at[:, pl.ds(start, block.shape[1])], save.at[i]))
    for load_copy, save_copy in zip(loads, saves):
        load_copy.wait()
        save_copy.start()
    for copy in saves:
        copy.wait()


def put(place, out, blocks, spots, share):
    size = sum(b.size for b in blocks)
    return pl.pallas_call(
        functools.partial(put_kernel, spots, share),
        out_shape=shape(*out.shape, dtype=out.dtype),
        in_specs=[SMEM] + [HBM] * (len(blocks) + 1),
        out_specs=HBM,
        scratch_shapes=[pltpu.VMEM(b.shape, b.dtype) for b in blocks] + [pltpu.SemaphoreType.DMA((len(blocks),))] * 2,
        input_output_aliases={1 + len(blocks): 0},
        cost_estimate=cost(0, 4 * size),
        compiler_params=WHOLE,
        name="put",
    )(place, *blocks, out)


PEERS = tuple(range(1, GROUP))


def over_chips(block):
    chips = lax.axis_size("feat") // CORES
    return total([block] + [send(block, "feat", CORES * s) for s in range(1, chips)])


def gather_group(bundle):
    mine = [bundle] + send_all([bundle] * len(PEERS), "dp", PEERS)
    return mine + [send(b, "feat", 1) for b in mine]


def run(sketches):
    x = sketches[0]
    rows, columns = x.shape
    share = columns // GROUP
    raw, ahead = 3 * share // 16, (3 * share // 16, share // 8)
    early = raw + sum(ahead)
    me = lax.axis_index("dp") % GROUP
    place = jnp.stack([me, lax.axis_index("feat") % CORES]).astype(jnp.int32)

    cuts, source = {}, x
    for s in PEERS:
        cuts[s] = lax.dynamic_slice(source, (0, (me ^ s) * share), (rows, share))
        if s == 2:
            source, cuts = lax.optimization_barrier((source, cuts))
    pieces = {s: send(cut, "dp", s) for s, cut in cuts.items()}
    keep, give = own_gram(place, x)
    own = over_chips(total([keep, send(give, "feat", 1)]))
    near, to_x, to_y, to_d = near_gram(place, x, pieces[1], raw)
    p2, p3, own, near = lax.optimization_barrier((pieces[2], pieces[3], own, near))

    keep, give, to_x = far_gram(place, near, p2, p3, to_x)
    parts = fold(keep, send(give, "feat", 1))
    parts, own, to_d = lax.optimization_barrier((parts, own, to_d))
    mine = total([parts[0]] + send_all(parts[1:], "dp", PEERS))
    diagonals = gather_group(own)
    from_d = send(to_d, "dp", 3)
    bundle = over_chips(mine)
    bundle, to_x, to_y = lax.optimization_barrier((bundle, to_x, to_y))
    crosses = gather_group(bundle)
    messages = [send(to_x, "dp", 1), send(to_y, "dp", 2), from_d]
    m, e, f, w0, keep, give = first(place, diagonals, crosses, x, [pieces[1], p2, p3], raw, ahead)

    parts = fold(keep, send(give, "feat", 1))
    parts, e = lax.optimization_barrier((parts, e))
    mine = total([parts[0]] + send_all(parts[1:], "dp", PEERS))
    pairs = send_all([e] * len(PEERS), "dp", PEERS)
    bundle = over_chips(mine)
    bundle, f = lax.optimization_barrier((bundle, f))
    bundles = gather_group(bundle)
    pairs += send_all([f] * len(PEERS), "dp", PEERS)
    a, b, e, w1 = second(place, bundles, m, early)

    ax, by = send(a, "dp", 1), send(b, "dp", 2)
    bx, ay = send(b, "dp", 1), send(a, "dp", 2)
    ad, bd = send(ax, "dp", 2), send(by, "dp", 1)
    left, right = early, early + a.shape[1]
    out = late(place, w1, a, b, e, pairs, raw, share)
    out = raw_merge(place, w0, w1, x, messages, out, share)
    out = put(place, out, [ax, by, bx, ay], ((1, left), (2, right), (1, right), (2, left)), share)
    for block, column in ((ad, left), (bd, right)):
        out = lax.dynamic_update_slice(out, block, (0, (me ^ 3) * share + column))
    return out[None]


def solution(mesh):
    spec = P("dp", None, "feat")
    return jax.shard_map(run, mesh=mesh, in_specs=(spec,), out_specs=spec, check_vma=False)
```

```python
import functools

import jax
import jax.numpy as jnp
from jax import lax
from jax.experimental import pallas as pl
from jax.experimental.pallas import tpu as pltpu
from jax.sharding import PartitionSpec as P


LEVELS = 2
GROUP = 2**LEVELS
CORES = 2
PEERS = tuple(range(1, GROUP))
F32, BF16 = jnp.float32, jnp.bfloat16
NT = (((1,), (1,)), ((), ()))
NN = (((1,), (0,)), ((), ()))
VMEM = pl.BlockSpec(memory_space=pltpu.VMEM)
SMEM = pl.BlockSpec(memory_space=pltpu.SMEM)
ANY = pl.BlockSpec(memory_space=pl.ANY)
HBM = pl.BlockSpec(memory_space=pltpu.HBM)


def send(block, axis, shift):
    count = lax.axis_size(axis)
    return lax.ppermute(block, axis, [(i, i ^ shift) for i in range(count)])


def send_all(blocks, axis, shifts):
    return [send(b, axis, s) for b, s in zip(blocks, shifts)]


def dot(a, b, dims=NN):
    return lax.dot_general(a, b, dims, preferred_element_type=F32)


def shape(*dims, dtype=F32):
    return jax.ShapeDtypeStruct(dims, dtype)


WHOLE = pltpu.CompilerParams(vmem_limit_bytes=67_043_328)


def cost(flops, nbytes):
    return pl.CostEstimate(flops=int(flops), bytes_accessed=int(nbytes), transcendentals=0)


def halves(a):
    high = a.astype(BF16)
    return high, (a - high.astype(F32)).astype(BF16)


def product(a, b, dims=NN):
    (ah, al), (bh, bl) = a, b
    return dot(ah, bh, dims) + (dot(ah, bl, dims) + dot(al, bh, dims))


def eye_mask(n):
    return lax.broadcasted_iota(jnp.int32, (n, n), 0) == lax.broadcasted_iota(jnp.int32, (n, n), 1)


def invert(kernels, x_ref, limit):
    n = kernels[0].shape[0]
    mask = eye_mask(n)
    eye = jnp.where(mask, 1.0, 0.0)
    parts = [halves(k) for k in kernels]
    for j, k in enumerate(kernels):
        diag = jnp.where(mask, k, 0.0)
        row = 1.0 / jnp.sum(diag, axis=0, keepdims=True)
        col = 1.0 / jnp.sum(diag, axis=1, keepdims=True)
        scaled = jnp.where(mask, 0.0, k) * row
        spread = jnp.sum(scaled * (jnp.where(mask, 0.0, k) * col))
        bound = jnp.minimum(jnp.max(jnp.sum(jnp.abs(k), axis=0, keepdims=True)), limit)
        near = jnp.where(mask, row, -scaled * col)
        far = eye * (2.0 / (1.0 + bound))
        x_ref[j] = jnp.where(spread < 0.9, near, far)

    def step():
        worst = jnp.float32(0.0)
        for j, part in enumerate(parts):
            x = x_ref[j]
            xs = halves(x)
            rest = eye - product(part, xs)
            worst = jnp.maximum(worst, jnp.sum(rest * rest))
            x_ref[j] = x + dot(xs[0], rest.astype(BF16))
        return worst

    step()
    lax.while_loop(lambda s: (s[0] < 24) & (s[1] > 1e-6), lambda s: (s[0] + 1, step()), (jnp.int32(2), step()))


def resolvent(grams, x_ref, out_ref):
    n = grams[0][0].shape[0]
    mask = eye_mask(n)
    eye = jnp.where(mask, 1.0, 0.0)
    scaled = []
    for a, b, d in grams:
        average = jnp.sum(jnp.where(mask, a + d, 0.0)) / (2 * n)
        scaled.append((eye + a / average, b / average, eye + d / average))
    limit = 1.0 + 2 * n
    invert([d for _, _, d in scaled], x_ref, limit)
    ties, schurs = [], []
    for j, (a, b, d) in enumerate(scaled):
        bs = halves(b)
        tie = halves(product(bs, halves(x_ref[j])))
        ties.append(tie)
        schurs.append(a - product(tie, bs, NT))
    invert(schurs, x_ref, limit)
    for j, tie in enumerate(ties):
        x = x_ref[j]
        out_ref[j, :, :n] = x.astype(BF16)
        out_ref[j, :, n:] = (-product(halves(x), tie)).astype(BF16)


def own_gram_kernel(place, x_ref, keep_ref, give_ref, acc):
    step = pl.program_id(0)
    core = place[1]
    half = keep_ref.shape[0]

    @pl.when(step == 0)
    def _():
        acc[...] = jnp.zeros_like(acc)

    acc[...] += dot(x_ref[...], x_ref[...], NT)

    @pl.when(step == pl.num_programs(0) - 1)
    def _():
        keep_ref[...] = acc[pl.ds(pl.multiple_of(core * half, half), half), :]
        give_ref[...] = acc[pl.ds(pl.multiple_of((1 - core) * half, half), half), :]


def own_gram(place, x, tile=2048):
    rows, columns = x.shape
    half = shape(rows // CORES, rows)
    spec = pl.BlockSpec((rows // CORES, rows), lambda k, place: (0, 0))
    return pl.pallas_call(
        own_gram_kernel,
        out_shape=(half, half),
        grid_spec=pltpu.PrefetchScalarGridSpec(
            num_scalar_prefetch=1,
            grid=(columns // tile,),
            in_specs=[pl.BlockSpec((rows, tile), lambda k, place: (0, k))],
            out_specs=(spec, spec),
            scratch_shapes=[pltpu.VMEM((rows, rows), F32)],
        ),
        cost_estimate=cost(2 * rows * rows * columns, 2 * rows * columns),
        name="own_gram",
    )(place, x)


def pair_gram(me, sources, block, load, chunk):
    rows, share = block.shape[1:]
    copies = []
    for k in range(share // chunk):
        here = slice(k * chunk, (k + 1) * chunk)
        for i, (s, source) in enumerate(sources):
            target = block.at[(me ^ s) % 2, :, here]
            copies.append(pltpu.make_async_copy(source(k * chunk, chunk), target, load.at[2 * k + i]))
            copies[-1].start()
    value = jnp.zeros((rows, rows), F32)
    for k in range(share // chunk):
        copies[2 * k].wait()
        copies[2 * k + 1].wait()
        here = slice(k * chunk, (k + 1) * chunk)
        value = value + dot(block[0, :, here], block[1, :, here], NT)
    return value


SHARES_X, SHARES_Y = (0, 2, 3), (0, 1, 3)


def near_gram_kernel(chunk, place, x, p1, out_ref, x_ref, y_ref, d_ref, block, pack, load, save):
    me = place[0]
    share, raw = p1.shape[1], d_ref.shape[1]

    def mine(column, size, t=0):
        return x.at[:, pl.ds(pl.multiple_of((me ^ t) * share + column, 128), size)]

    def theirs(column, size):
        return p1.at[:, column : column + size]

    packs = [pltpu.make_async_copy(mine(0, raw, t), pack.at[t], save.at[t]) for t in range(GROUP)]
    packs.append(pltpu.make_async_copy(theirs(0, raw), pack.at[GROUP], save.at[GROUP]))
    for copy in packs:
        copy.start()
    out_ref[...] = pair_gram(me, ((0, mine), (1, theirs)), block, load, chunk)
    for copy in packs:
        copy.wait()
    targets = [(t, x_ref.at[i]) for i, t in enumerate(SHARES_X)] + [(t, y_ref.at[i]) for i, t in enumerate(SHARES_Y)]
    targets += [(GROUP, y_ref.at[GROUP - 1]), (0, d_ref)]
    copies = [pltpu.make_async_copy(pack.at[t], target, save.at[i]) for i, (t, target) in enumerate(targets)]
    for copy in copies:
        copy.start()
    for copy in copies:
        copy.wait()


def near_gram(place, x, p1, raw, chunk=512):
    rows, share = p1.shape
    message = shape(GROUP, rows, raw, dtype=BF16)
    return pl.pallas_call(
        functools.partial(near_gram_kernel, chunk),
        out_shape=(shape(rows, rows), message, message, shape(rows, raw, dtype=BF16)),
        in_specs=[SMEM, HBM, HBM],
        out_specs=(VMEM, HBM, HBM, HBM),
        scratch_shapes=[
            pltpu.VMEM((2, rows, share), BF16),
            pltpu.VMEM((GROUP + 1, rows, raw), BF16),
            pltpu.SemaphoreType.DMA((2 * share // chunk,)),
            pltpu.SemaphoreType.DMA((2 * GROUP,)),
        ],
        cost_estimate=cost(2 * rows * rows * share, 4 * rows * share),
        compiler_params=WHOLE,
        name="near_gram",
    )(place, x, p1)


def far_gram_kernel(chunk, place, near, p2, p3, _, keep_out, give_out, x_ref, block, acc, keep_ref, give_ref, load, save):
    me, core = place[0], place[1]
    first_load = pltpu.make_async_copy(near, acc.at[me // 2], save.at[3])
    first_load.start()
    sources = tuple((s, lambda column, size, p=p: p.at[:, column : column + size]) for s, p in ((2, p2), (3, p3)))
    acc[1 - me // 2] = pair_gram(me, sources, block, load, chunk)
    copies = [pltpu.make_async_copy(block.at[(me ^ 2) % 2, :, : x_ref.shape[2]], x_ref.at[GROUP - 1], save.at[0])]
    copies[0].start()
    first_load.wait()
    part = keep_ref.shape[1]
    for s in range(GROUP):
        to = me ^ s
        pair, start = to // 2, (to % 2) * (CORES * part)
        keep_ref[s] = acc[pair, pl.ds(pl.multiple_of(start + core * part, part), part), :]
        give_ref[s] = acc[pair, pl.ds(pl.multiple_of(start + (1 - core) * part, part), part), :]
    for i, (source, target) in enumerate(((give_ref, give_out), (keep_ref, keep_out))):
        copies.append(pltpu.make_async_copy(source, target, save.at[1 + i]))
        copies[-1].start()
    for copy in copies:
        copy.wait()


def far_gram(place, near, p2, p3, message, chunk=512):
    rows, share = p2.shape
    out = shape(GROUP, rows // (2 * CORES), rows)
    return pl.pallas_call(
        functools.partial(far_gram_kernel, chunk),
        out_shape=(out, out, shape(*message.shape, dtype=BF16)),
        in_specs=[SMEM, HBM, HBM, HBM, HBM],
        out_specs=(HBM, HBM, HBM),
        scratch_shapes=[
            pltpu.VMEM((2, rows, share), BF16),
            pltpu.VMEM((GROUP // 2, rows, rows), F32),
            pltpu.VMEM(out.shape, F32),
            pltpu.VMEM(out.shape, F32),
            pltpu.SemaphoreType.DMA((2 * share // chunk,)),
            pltpu.SemaphoreType.DMA((4,)),
        ],
        input_output_aliases={4: 2},
        cost_estimate=cost(2 * rows * rows * share, 4 * rows * share),
        compiler_params=WHOLE,
        name="far_gram",
    )(place, near, p2, p3, message)


def fold(mine, theirs):
    return [mine[s] + theirs[s] for s in range(mine.shape[0])]


def total(arrays):
    return functools.reduce(jnp.add, arrays)


def merge_rows(stacked, w):
    lower = stacked[: w.shape[0]]
    return (lower.astype(F32) - dot(w, stacked)).astype(BF16)


def first_kernel(raw, tile, *refs):
    place, tails, crosses, (x, p1, p2, p3), refs = refs[0], refs[1:9], refs[9:17], refs[17:21], refs[21:]
    m_ref, e_ref, f_ref, w_out, keep_out, give_out, cross, diag, inverse, block, m, acc, keep_ref, give_ref, w, load, save = refs
    me, core = place[0], place[1]
    rows, share = p1.shape
    sources = [x.at[:, pl.ds(pl.multiple_of(me * share, share), share)], p1, p2, p3]
    loads = [
        pltpu.make_async_copy(source, block.at[pl.ds(pl.multiple_of((me ^ s) * rows, rows), rows)], load.at[s])
        for s, source in enumerate(sources)
    ]
    for copy in loads:
        copy.start()

    part, half = rows // (2 * CORES), rows // CORES
    for c in range(CORES):
        for s in range(GROUP):
            source, seat = me ^ s, core ^ c
            start = (source % 2) * (CORES * part) + seat * part
            cross[source // 2, pl.ds(pl.multiple_of(start, part), part), :] = crosses[c * GROUP + s][...]
            diag[source, pl.ds(pl.multiple_of(seat * half, half), half), :] = tails[c * GROUP + s][...]
    grams = [(diag[2 * j], cross[j], diag[2 * j + 1]) for j in range(GROUP // 2)]
    resolvent(grams, inverse, w)
    for copy in loads:
        copy.wait()

    acc[...] = jnp.zeros_like(acc)
    saves = [pltpu.make_async_copy(w, w_out, save.at[share // tile + 4])]
    saves[0].start()
    for k in range(share // tile):
        here = slice(k * tile, (k + 1) * tile)
        m0 = merge_rows(block[: 2 * rows, here], w[0])
        m1 = merge_rows(block[2 * rows :, here], w[1])
        m[:rows, here] = m0
        m[rows:, here] = m1
        saves.append(pltpu.make_async_copy(m.at[:, here], m_ref.at[:, here], save.at[k]))
        saves[-1].start()
        acc[0] += dot(m0, m0, NT)
        acc[1] += dot(m0, m1, NT)
        acc[2] += dot(m1, m1, NT)
    start = raw
    for i, ref in enumerate((e_ref, f_ref)):
        source = m.at[:, start : start + ref.shape[1]]
        saves.append(pltpu.make_async_copy(source, ref, save.at[share // tile + i]))
        saves[-1].start()
        start += ref.shape[1]
    lower = lax.broadcasted_iota(jnp.int32, (rows, rows), 0) >= lax.broadcasted_iota(jnp.int32, (rows, rows), 1)
    row = jnp.sum(jnp.where(eye_mask(rows), acc[2], 0.0), axis=0, keepdims=True)
    acc[2] = jnp.where(lower, acc[0], acc[2])
    part = rows // (GROUP * CORES)
    for s in range(GROUP):
        to = me ^ s
        for ref, seat in ((give_ref, to * CORES + 1 - core), (keep_ref, to * CORES + core)):
            here = pl.ds(pl.multiple_of(seat * part, part), part)
            ref[s, :part] = acc[1, here, :]
            ref[s, part : 2 * part] = acc[2, here, :]
            ref[s, 2 * part :] = jnp.broadcast_to(row, (8, rows))
    for i, (source, target) in enumerate(((give_ref, give_out), (keep_ref, keep_out))):
        saves.append(pltpu.make_async_copy(source, target, save.at[share // tile + 2 + i]))
        saves[-1].start()
    for copy in saves:
        copy.wait()


def first(place, diagonals, crosses, x, pieces, raw, ahead, tile=512):
    rows, share = pieces[0].shape
    pairs = GROUP // 2
    out = shape(GROUP, 2 * rows // (GROUP * CORES) + 8, rows)
    return pl.pallas_call(
        functools.partial(first_kernel, raw, tile),
        out_shape=tuple(shape(pairs * rows, n, dtype=BF16) for n in (share, *ahead)) + (shape(pairs, rows, 2 * rows, dtype=BF16), out, out),
        in_specs=[SMEM] + [VMEM] * (4 * GROUP) + [HBM] * 4,
        out_specs=(ANY,) * 6,
        scratch_shapes=[
            pltpu.VMEM((pairs, rows, rows), F32),
            pltpu.VMEM((GROUP, rows, rows), F32),
            pltpu.VMEM((pairs, rows, rows), F32),
            pltpu.VMEM((GROUP * rows, share), BF16),
            pltpu.VMEM((pairs * rows, share), BF16),
            pltpu.VMEM((3, rows, rows), F32),
            pltpu.VMEM(out.shape, F32),
            pltpu.VMEM(out.shape, F32),
            pltpu.VMEM((pairs, rows, 2 * rows), BF16),
            pltpu.SemaphoreType.DMA((GROUP,)),
            pltpu.SemaphoreType.DMA((share // tile + 5,)),
        ],
        cost_estimate=cost(2 * pairs * rows**3 * 40 + 14 * rows * rows * share, 12 * rows * share),
        name="first",
    )(place, *diagonals, *crosses, x, *pieces)


def second_kernel(*refs):
    place, bundles, m_ref, refs = refs[0], refs[1:9], refs[9], refs[10:]
    a_ref, b_ref, e_ref, w_out, gram, inverse, m, w_ref, merged, load, save = refs
    me, core = place[0], place[1]
    rows = m.shape[0] // 2
    copy = pltpu.make_async_copy(m_ref, m, load)
    copy.start()
    part = rows // (GROUP * CORES)
    for c in range(CORES):
        for s in range(GROUP):
            seat = (me ^ s) * CORES + (core ^ c)
            for b in range(2):
                gram[b, pl.ds(pl.multiple_of(seat * part, part), part), :] = bundles[c * GROUP + s][b * part : (b + 1) * part]
    packed = gram[1]
    turned = packed.T
    lower = lax.broadcasted_iota(jnp.int32, (rows, rows), 0) >= lax.broadcasted_iota(jnp.int32, (rows, rows), 1)
    diagonal = jnp.broadcast_to(bundles[0][2 * part : 2 * part + 1], (rows, rows))
    upper_gram = jnp.where(eye_mask(rows), diagonal, jnp.where(lower, turned, packed))
    resolvent([(jnp.where(lower, packed, turned), gram[0], upper_gram)], inverse, w_ref)
    copy.wait()
    saves = []
    early, half = e_ref.shape[1], a_ref.shape[1]
    for i, (ref, start) in enumerate(((a_ref, early), (b_ref, early + half), (e_ref, 0))):
        here = slice(start, start + ref.shape[1])
        merged[:, here] = merge_rows(m[:, here], w_ref[0])
        saves.append(pltpu.make_async_copy(merged.at[:, here], ref, save.at[i]))
        saves[-1].start()
    saves.append(pltpu.make_async_copy(w_ref, w_out, save.at[3]))
    saves[-1].start()
    for save_copy in saves:
        save_copy.wait()


def second(place, bundles, m, early):
    rows, share = m.shape[0] // 2, m.shape[1]
    half = (share - early) // 2
    return pl.pallas_call(
        second_kernel,
        out_shape=tuple(shape(rows, n, dtype=BF16) for n in (half, half, early)) + (shape(1, rows, 2 * rows, dtype=BF16),),
        in_specs=[SMEM] + [VMEM] * (2 * GROUP) + [ANY],
        out_specs=(ANY,) * 4,
        scratch_shapes=[
            pltpu.VMEM((2, rows, rows), F32),
            pltpu.VMEM((1, rows, rows), F32),
            pltpu.VMEM(m.shape, BF16),
            pltpu.VMEM((1, rows, 2 * rows), BF16),
            pltpu.VMEM((rows, share), BF16),
            pltpu.SemaphoreType.DMA,
            pltpu.SemaphoreType.DMA((4,)),
        ],
        cost_estimate=cost(2 * rows**3 * 40 + 4 * rows * rows * share, 6 * rows * share),
        name="second",
    )(place, *bundles, m)


def raw_first_kernel(share, place, w, x, xs, ys, d, out, block, pair, load, save):
    me = place[0]
    rows, raw = d.shape
    saves, loads, sources = [], {}, {}
    for v in PEERS:
        mine = x.at[:, pl.ds(pl.multiple_of((me ^ v) * share, 128), raw)]
        across = {1: xs.at[GROUP - 1], 2: ys.at[GROUP - 1], 3: d}[v]
        sources[v] = (mine, xs.at[SHARES_X.index(v ^ 1)], ys.at[SHARES_Y.index(v ^ 2)], across)
    for v, group in sources.items():
        for s, source in enumerate(group):
            target = block.at[v - 1, pl.ds(pl.multiple_of((me ^ s) * rows, rows), rows)]
            loads[v, s] = pltpu.make_async_copy(source, target, load.at[(v - 1) * GROUP + s])
            loads[v, s].start()
    for v in PEERS:
        for s in range(GROUP):
            loads[v, s].wait()
        for j in range(GROUP // 2):
            pair[v - 1, j * rows : (j + 1) * rows] = merge_rows(block[v - 1, 2 * j * rows : 2 * (j + 1) * rows], w[j])
        saves.append(pltpu.make_async_copy(pair.at[v - 1], out.at[v - 1], save.at[v - 1]))
        saves[-1].start()
    for copy in saves:
        copy.wait()


def raw_first(place, w, x, messages, share):
    rows, raw = messages[2].shape
    pairs = (GROUP - 1, 2 * rows, raw)
    return pl.pallas_call(
        functools.partial(raw_first_kernel, share),
        out_shape=shape(*pairs, dtype=BF16),
        in_specs=[SMEM, VMEM] + [HBM] * 4,
        out_specs=HBM,
        scratch_shapes=[
            pltpu.VMEM((GROUP - 1, GROUP * rows, raw), BF16),
            pltpu.VMEM(pairs, BF16),
            pltpu.SemaphoreType.DMA(((GROUP - 1) * GROUP,)),
            pltpu.SemaphoreType.DMA((GROUP - 1,)),
        ],
        cost_estimate=cost(8 * rows * rows * raw * (GROUP - 1), 12 * rows * raw * (GROUP - 1)),
        compiler_params=WHOLE,
        name="raw_first",
    )(place, w, x, *messages)


def late_kernel(share, raw, place, w, a, b, e, raws, *refs):
    early, (out, buffer, save) = refs[:-3], refs[-3:]
    me, half = place[0], a.shape[1]
    saves = []

    def put(source, owner, column):
        target = out.at[:, pl.ds(pl.multiple_of(owner * share + column, 128), source.shape[1])]
        saves.append(pltpu.make_async_copy(source, target, save.at[len(saves)]))
        saves[-1].start()

    put(e, me, 0)
    put(a, me, e.shape[1])
    put(b, me, e.shape[1] + half)
    work = [(raws.at[s - 1], s, 0) for s in PEERS]
    work += [(pair, s, raw) for pair, s in zip(early, PEERS)]
    work += [(pair, s, raw + early[0].shape[1]) for pair, s in zip(early[len(PEERS) :], PEERS)]
    for pair, s, column in work:
        spot = buffer.at[s - 1, :, column : column + pair.shape[1]]
        spot[...] = merge_rows(pair[...], w[0])
        put(spot, me ^ s, column)
    for copy in saves:
        copy.wait()


def late(place, w, a, b, e, raws, early, share):
    rows, size = e.shape
    return pl.pallas_call(
        functools.partial(late_kernel, share, raws.shape[2]),
        out_shape=shape(rows, GROUP * share, dtype=BF16),
        in_specs=[SMEM] + [VMEM] * (5 + len(early)),
        out_specs=HBM,
        scratch_shapes=[pltpu.VMEM((GROUP - 1, rows, size), BF16), pltpu.SemaphoreType.DMA((len(early) + GROUP + 2,))],
        cost_estimate=cost(4 * rows * rows * size * (GROUP - 1), 6 * rows * size * (GROUP - 1)),
        name="late",
    )(place, w, a, b, e, raws, *early)


def put_kernel(spots, share, place, *refs):
    count = len(spots)
    blocks, out, buffers, load, save = refs[:count], refs[count + 1], refs[count + 2 : -2], refs[-2], refs[-1]
    loads, saves = [], []
    for i, ((s, column), block, buffer) in enumerate(zip(spots, blocks, buffers)):
        start = pl.multiple_of((place[0] ^ s) * share + column, 128)
        loads.append(pltpu.make_async_copy(block, buffer, load.at[i]))
        loads[-1].start()
        saves.append(pltpu.make_async_copy(buffer, out.at[:, pl.ds(start, block.shape[1])], save.at[i]))
    for load_copy, save_copy in zip(loads, saves):
        load_copy.wait()
        save_copy.start()
    for copy in saves:
        copy.wait()


def put(place, out, blocks, spots, share):
    size = sum(b.size for b in blocks)
    return pl.pallas_call(
        functools.partial(put_kernel, spots, share),
        out_shape=shape(*out.shape, dtype=out.dtype),
        in_specs=[SMEM] + [HBM] * (len(blocks) + 1),
        out_specs=HBM,
        scratch_shapes=[pltpu.VMEM(b.shape, b.dtype) for b in blocks] + [pltpu.SemaphoreType.DMA((len(blocks),))] * 2,
        input_output_aliases={1 + len(blocks): 0},
        cost_estimate=cost(0, 4 * size),
        compiler_params=WHOLE,
        name="put",
    )(place, *blocks, out)


def over_chips(block):
    chips = lax.axis_size("feat") // CORES
    return total([block] + [send(block, "feat", CORES * s) for s in range(1, chips)])


def gather_group(bundle):
    mine = [bundle] + send_all([bundle] * len(PEERS), "dp", PEERS)
    return mine + [send(b, "feat", 1) for b in mine]


def run(sketches):
    x = sketches[0]
    rows, columns = x.shape
    share = columns // GROUP
    raw, ahead = 3 * share // 16, (3 * share // 16, share // 8)
    early = raw + sum(ahead)
    me = lax.axis_index("dp") % GROUP
    place = jnp.stack([me, lax.axis_index("feat") % CORES]).astype(jnp.int32)

    cuts, source = {}, x
    for s in PEERS:
        cuts[s] = lax.dynamic_slice(source, (0, (me ^ s) * share), (rows, share))
        if s == 2:
            source, cuts = lax.optimization_barrier((source, cuts))
    pieces = {s: send(cut, "dp", s) for s, cut in cuts.items()}
    keep, give = own_gram(place, x)
    own = over_chips(total([keep, send(give, "feat", 1)]))
    near, to_x, to_y, to_d = near_gram(place, x, pieces[1], raw)
    p2, p3, own, near = lax.optimization_barrier((pieces[2], pieces[3], own, near))

    keep, give, to_x = far_gram(place, near, p2, p3, to_x)
    parts = fold(keep, send(give, "feat", 1))
    parts, own, to_d = lax.optimization_barrier((parts, own, to_d))
    mine = total([parts[0]] + send_all(parts[1:], "dp", PEERS))
    diagonals = gather_group(own)
    from_d = send(to_d, "dp", 3)
    bundle = over_chips(mine)
    bundle, to_x, to_y = lax.optimization_barrier((bundle, to_x, to_y))
    crosses = gather_group(bundle)
    messages = [send(to_x, "dp", 1), send(to_y, "dp", 2), from_d]
    m, e, f, w0, keep, give = first(place, diagonals, crosses, x, [pieces[1], p2, p3], raw, ahead)

    parts = fold(keep, send(give, "feat", 1))
    parts, e = lax.optimization_barrier((parts, e))
    mine = total([parts[0]] + send_all(parts[1:], "dp", PEERS))
    pairs = send_all([e] * len(PEERS), "dp", PEERS)
    raws = raw_first(place, w0, x, messages, share)
    bundle = over_chips(mine)
    bundle, f = lax.optimization_barrier((bundle, f))
    bundles = gather_group(bundle)
    pairs += send_all([f] * len(PEERS), "dp", PEERS)
    a, b, e, w1 = second(place, bundles, m, early)

    ax, by = send(a, "dp", 1), send(b, "dp", 2)
    bx, ay = send(b, "dp", 1), send(a, "dp", 2)
    ad, bd = send(ax, "dp", 2), send(by, "dp", 1)
    left, right = early, early + a.shape[1]
    out = late(place, w1, a, b, e, raws, pairs, share)
    out = put(place, out, [ax, by, bx, ay], ((1, left), (2, right), (1, right), (2, left)), share)
    out = put(place, out, [ad, bd], ((3, left), (3, right)), share)
    return out[None]


def solution(mesh):
    spec = P("dp", None, "feat")
    return jax.shard_map(run, mesh=mesh, in_specs=(spec,), out_specs=spec, check_vma=False)
```

```python
import functools

import jax
import jax.numpy as jnp
from jax import lax
from jax.experimental import pallas as pl
from jax.experimental.pallas import tpu as pltpu
from jax.sharding import PartitionSpec as P


LEVELS = 2
GROUP = 2**LEVELS
CORES = 2
PEERS = tuple(range(1, GROUP))
F32, BF16 = jnp.float32, jnp.bfloat16
NT = (((1,), (1,)), ((), ()))
NN = (((1,), (0,)), ((), ()))
VMEM = pl.BlockSpec(memory_space=pltpu.VMEM)
SMEM = pl.BlockSpec(memory_space=pltpu.SMEM)
ANY = pl.BlockSpec(memory_space=pl.ANY)
HBM = pl.BlockSpec(memory_space=pltpu.HBM)


def send(block, axis, shift):
    count = lax.axis_size(axis)
    return lax.ppermute(block, axis, [(i, i ^ shift) for i in range(count)])


def send_all(blocks, axis, shifts):
    return [send(b, axis, s) for b, s in zip(blocks, shifts)]


def dot(a, b, dims=NN):
    return lax.dot_general(a, b, dims, preferred_element_type=F32)


def shape(*dims, dtype=F32):
    return jax.ShapeDtypeStruct(dims, dtype)


WHOLE = pltpu.CompilerParams(vmem_limit_bytes=67_043_328)


def cost(flops, nbytes):
    return pl.CostEstimate(flops=int(flops), bytes_accessed=int(nbytes), transcendentals=0)


def halves(a):
    high = a.astype(BF16)
    return high, (a - high.astype(F32)).astype(BF16)


def product(a, b, dims=NN):
    (ah, al), (bh, bl) = a, b
    return dot(ah, bh, dims) + (dot(ah, bl, dims) + dot(al, bh, dims))


def eye_mask(n):
    return lax.broadcasted_iota(jnp.int32, (n, n), 0) == lax.broadcasted_iota(jnp.int32, (n, n), 1)


def invert(kernels, x_ref, limit):
    n = kernels[0].shape[0]
    mask = eye_mask(n)
    eye = jnp.where(mask, 1.0, 0.0)
    parts = [halves(k) for k in kernels]
    for j, k in enumerate(kernels):
        diag = jnp.where(mask, k, 0.0)
        row = 1.0 / jnp.sum(diag, axis=0, keepdims=True)
        col = 1.0 / jnp.sum(diag, axis=1, keepdims=True)
        scaled = jnp.where(mask, 0.0, k) * row
        spread = jnp.sum(scaled * (jnp.where(mask, 0.0, k) * col))
        bound = jnp.minimum(jnp.max(jnp.sum(jnp.abs(k), axis=0, keepdims=True)), limit)
        near = jnp.where(mask, row, -scaled * col)
        far = eye * (2.0 / (1.0 + bound))
        x_ref[j] = jnp.where(spread < 0.9, near, far)

    def step():
        worst = jnp.float32(0.0)
        for j, part in enumerate(parts):
            x = x_ref[j]
            xs = halves(x)
            rest = eye - product(part, xs)
            worst = jnp.maximum(worst, jnp.sum(rest * rest))
            x_ref[j] = x + dot(xs[0], rest.astype(BF16))
        return worst

    step()
    lax.while_loop(lambda s: (s[0] < 24) & (s[1] > 1e-6), lambda s: (s[0] + 1, step()), (jnp.int32(2), step()))


def resolvent(grams, x_ref, out_ref):
    n = grams[0][0].shape[0]
    mask = eye_mask(n)
    eye = jnp.where(mask, 1.0, 0.0)
    scaled = []
    for a, b, d in grams:
        average = jnp.sum(jnp.where(mask, a + d, 0.0)) / (2 * n)
        scaled.append((eye + a / average, b / average, eye + d / average))
    limit = 1.0 + 2 * n
    invert([d for _, _, d in scaled], x_ref, limit)
    ties, schurs = [], []
    for j, (a, b, d) in enumerate(scaled):
        bs = halves(b)
        tie = halves(product(bs, halves(x_ref[j])))
        ties.append(tie)
        schurs.append(a - product(tie, bs, NT))
    invert(schurs, x_ref, limit)
    for j, tie in enumerate(ties):
        x = x_ref[j]
        out_ref[j, :, :n] = x.astype(BF16)
        out_ref[j, :, n:] = (-product(halves(x), tie)).astype(BF16)


def own_gram_kernel(place, x_ref, keep_ref, give_ref, acc):
    step = pl.program_id(0)
    core = place[1]
    half = keep_ref.shape[0]

    @pl.when(step == 0)
    def _():
        acc[...] = jnp.zeros_like(acc)

    acc[...] += dot(x_ref[...], x_ref[...], NT)

    @pl.when(step == pl.num_programs(0) - 1)
    def _():
        keep_ref[...] = acc[pl.ds(pl.multiple_of(core * half, half), half), :]
        give_ref[...] = acc[pl.ds(pl.multiple_of((1 - core) * half, half), half), :]


def own_gram(place, x, tile=2048):
    rows, columns = x.shape
    half = shape(rows // CORES, rows)
    spec = pl.BlockSpec((rows // CORES, rows), lambda k, place: (0, 0))
    return pl.pallas_call(
        own_gram_kernel,
        out_shape=(half, half),
        grid_spec=pltpu.PrefetchScalarGridSpec(
            num_scalar_prefetch=1,
            grid=(columns // tile,),
            in_specs=[pl.BlockSpec((rows, tile), lambda k, place: (0, k))],
            out_specs=(spec, spec),
            scratch_shapes=[pltpu.VMEM((rows, rows), F32)],
        ),
        cost_estimate=cost(2 * rows * rows * columns, 2 * rows * columns),
        name="own_gram",
    )(place, x)


def pair_gram(me, sources, block, load, chunk):
    rows, share = block.shape[1:]
    copies = []
    for k in range(share // chunk):
        here = slice(k * chunk, (k + 1) * chunk)
        for i, (s, source) in enumerate(sources):
            target = block.at[(me ^ s) % 2, :, here]
            copies.append(pltpu.make_async_copy(source(k * chunk, chunk), target, load.at[2 * k + i]))
            copies[-1].start()
    value = jnp.zeros((rows, rows), F32)
    for k in range(share // chunk):
        copies[2 * k].wait()
        copies[2 * k + 1].wait()
        here = slice(k * chunk, (k + 1) * chunk)
        value = value + dot(block[0, :, here], block[1, :, here], NT)
    return value


SHARES_X, SHARES_Y = (0, 2, 3), (0, 1, 3)


def near_gram_kernel(chunk, place, x, p1, out_ref, x_ref, y_ref, d_ref, block, pack, load, save):
    me = place[0]
    share, raw = p1.shape[1], d_ref.shape[1]

    def mine(column, size, t=0):
        return x.at[:, pl.ds(pl.multiple_of((me ^ t) * share + column, 128), size)]

    def theirs(column, size):
        return p1.at[:, column : column + size]

    packs = [pltpu.make_async_copy(mine(0, raw, t), pack.at[t], save.at[t]) for t in range(GROUP)]
    packs.append(pltpu.make_async_copy(theirs(0, raw), pack.at[GROUP], save.at[GROUP]))
    for copy in packs:
        copy.start()
    out_ref[...] = pair_gram(me, ((0, mine), (1, theirs)), block, load, chunk)
    for copy in packs:
        copy.wait()
    targets = [(t, x_ref.at[i]) for i, t in enumerate(SHARES_X)] + [(t, y_ref.at[i]) for i, t in enumerate(SHARES_Y)]
    targets += [(GROUP, y_ref.at[GROUP - 1]), (0, d_ref)]
    copies = [pltpu.make_async_copy(pack.at[t], target, save.at[i]) for i, (t, target) in enumerate(targets)]
    for copy in copies:
        copy.start()
    for copy in copies:
        copy.wait()


def near_gram(place, x, p1, raw, chunk=512):
    rows, share = p1.shape
    message = shape(GROUP, rows, raw, dtype=BF16)
    return pl.pallas_call(
        functools.partial(near_gram_kernel, chunk),
        out_shape=(shape(rows, rows), message, message, shape(rows, raw, dtype=BF16)),
        in_specs=[SMEM, HBM, HBM],
        out_specs=(VMEM, HBM, HBM, HBM),
        scratch_shapes=[
            pltpu.VMEM((2, rows, share), BF16),
            pltpu.VMEM((GROUP + 1, rows, raw), BF16),
            pltpu.SemaphoreType.DMA((2 * share // chunk,)),
            pltpu.SemaphoreType.DMA((2 * GROUP,)),
        ],
        cost_estimate=cost(2 * rows * rows * share, 4 * rows * share),
        compiler_params=WHOLE,
        name="near_gram",
    )(place, x, p1)


def far_gram_kernel(chunk, place, near, p2, p3, _, keep_out, give_out, x_ref, block, acc, keep_ref, give_ref, load, save):
    me, core = place[0], place[1]
    first_load = pltpu.make_async_copy(near, acc.at[me // 2], save.at[3])
    first_load.start()
    sources = tuple((s, lambda column, size, p=p: p.at[:, column : column + size]) for s, p in ((2, p2), (3, p3)))
    acc[1 - me // 2] = pair_gram(me, sources, block, load, chunk)
    copies = [pltpu.make_async_copy(block.at[(me ^ 2) % 2, :, : x_ref.shape[2]], x_ref.at[GROUP - 1], save.at[0])]
    copies[0].start()
    first_load.wait()
    part = keep_ref.shape[1]
    for s in range(GROUP):
        to = me ^ s
        pair, start = to // 2, (to % 2) * (CORES * part)
        keep_ref[s] = acc[pair, pl.ds(pl.multiple_of(start + core * part, part), part), :]
        give_ref[s] = acc[pair, pl.ds(pl.multiple_of(start + (1 - core) * part, part), part), :]
    for i, (source, target) in enumerate(((give_ref, give_out), (keep_ref, keep_out))):
        copies.append(pltpu.make_async_copy(source, target, save.at[1 + i]))
        copies[-1].start()
    for copy in copies:
        copy.wait()


def far_gram(place, near, p2, p3, message, chunk=512):
    rows, share = p2.shape
    out = shape(GROUP, rows // (2 * CORES), rows)
    return pl.pallas_call(
        functools.partial(far_gram_kernel, chunk),
        out_shape=(out, out, shape(*message.shape, dtype=BF16)),
        in_specs=[SMEM, HBM, HBM, HBM, HBM],
        out_specs=(HBM, HBM, HBM),
        scratch_shapes=[
            pltpu.VMEM((2, rows, share), BF16),
            pltpu.VMEM((GROUP // 2, rows, rows), F32),
            pltpu.VMEM(out.shape, F32),
            pltpu.VMEM(out.shape, F32),
            pltpu.SemaphoreType.DMA((2 * share // chunk,)),
            pltpu.SemaphoreType.DMA((4,)),
        ],
        input_output_aliases={4: 2},
        cost_estimate=cost(2 * rows * rows * share, 4 * rows * share),
        compiler_params=WHOLE,
        name="far_gram",
    )(place, near, p2, p3, message)


def fold(mine, theirs):
    return [mine[s] + theirs[s] for s in range(mine.shape[0])]


def total(arrays):
    return functools.reduce(jnp.add, arrays)


def merge_rows(stacked, w):
    lower = stacked[: w.shape[0]]
    return (lower.astype(F32) - dot(w, stacked)).astype(BF16)


def first_kernel(raw, tile, *refs):
    place, tails, crosses, (x, p1, p2, p3), refs = refs[0], refs[1:9], refs[9:17], refs[17:21], refs[21:]
    m_ref, e_ref, f_ref, w_out, keep_out, give_out, cross, diag, inverse, block, m, acc, keep_ref, give_ref, w, load, save = refs
    me, core = place[0], place[1]
    rows, share = p1.shape
    sources = [x.at[:, pl.ds(pl.multiple_of(me * share, share), share)], p1, p2, p3]
    loads = [
        pltpu.make_async_copy(source, block.at[pl.ds(pl.multiple_of((me ^ s) * rows, rows), rows)], load.at[s])
        for s, source in enumerate(sources)
    ]
    for copy in loads:
        copy.start()

    part, half = rows // (2 * CORES), rows // CORES
    for c in range(CORES):
        for s in range(GROUP):
            source, seat = me ^ s, core ^ c
            start = (source % 2) * (CORES * part) + seat * part
            cross[source // 2, pl.ds(pl.multiple_of(start, part), part), :] = crosses[c * GROUP + s][...]
            diag[source, pl.ds(pl.multiple_of(seat * half, half), half), :] = tails[c * GROUP + s][...]
    grams = [(diag[2 * j], cross[j], diag[2 * j + 1]) for j in range(GROUP // 2)]
    resolvent(grams, inverse, w)
    for copy in loads:
        copy.wait()

    acc[...] = jnp.zeros_like(acc)
    saves = [pltpu.make_async_copy(w, w_out, save.at[share // tile + 4])]
    saves[0].start()
    for k in range(share // tile):
        here = slice(k * tile, (k + 1) * tile)
        m0 = merge_rows(block[: 2 * rows, here], w[0])
        m1 = merge_rows(block[2 * rows :, here], w[1])
        m[:rows, here] = m0
        m[rows:, here] = m1
        saves.append(pltpu.make_async_copy(m.at[:, here], m_ref.at[:, here], save.at[k]))
        saves[-1].start()
        acc[0] += dot(m0, m0, NT)
        acc[1] += dot(m0, m1, NT)
        acc[2] += dot(m1, m1, NT)
    start = raw
    for i, ref in enumerate((e_ref, f_ref)):
        source = m.at[:, start : start + ref.shape[1]]
        saves.append(pltpu.make_async_copy(source, ref, save.at[share // tile + i]))
        saves[-1].start()
        start += ref.shape[1]
    lower = lax.broadcasted_iota(jnp.int32, (rows, rows), 0) >= lax.broadcasted_iota(jnp.int32, (rows, rows), 1)
    row = jnp.sum(jnp.where(eye_mask(rows), acc[2], 0.0), axis=0, keepdims=True)
    acc[2] = jnp.where(lower, acc[0], acc[2])
    part = rows // (GROUP * CORES)
    for s in range(GROUP):
        to = me ^ s
        for ref, seat in ((give_ref, to * CORES + 1 - core), (keep_ref, to * CORES + core)):
            here = pl.ds(pl.multiple_of(seat * part, part), part)
            ref[s, :part] = acc[1, here, :]
            ref[s, part : 2 * part] = acc[2, here, :]
            ref[s, 2 * part :] = jnp.broadcast_to(row, (8, rows))
    for i, (source, target) in enumerate(((give_ref, give_out), (keep_ref, keep_out))):
        saves.append(pltpu.make_async_copy(source, target, save.at[share // tile + 2 + i]))
        saves[-1].start()
    for copy in saves:
        copy.wait()


def first(place, diagonals, crosses, x, pieces, raw, ahead, tile=512):
    rows, share = pieces[0].shape
    pairs = GROUP // 2
    out = shape(GROUP, 2 * rows // (GROUP * CORES) + 8, rows)
    return pl.pallas_call(
        functools.partial(first_kernel, raw, tile),
        out_shape=tuple(shape(pairs * rows, n, dtype=BF16) for n in (share, *ahead)) + (shape(pairs, rows, 2 * rows, dtype=BF16), out, out),
        in_specs=[SMEM] + [VMEM] * (4 * GROUP) + [HBM] * 4,
        out_specs=(ANY,) * 6,
        scratch_shapes=[
            pltpu.VMEM((pairs, rows, rows), F32),
            pltpu.VMEM((GROUP, rows, rows), F32),
            pltpu.VMEM((pairs, rows, rows), F32),
            pltpu.VMEM((GROUP * rows, share), BF16),
            pltpu.VMEM((pairs * rows, share), BF16),
            pltpu.VMEM((3, rows, rows), F32),
            pltpu.VMEM(out.shape, F32),
            pltpu.VMEM(out.shape, F32),
            pltpu.VMEM((pairs, rows, 2 * rows), BF16),
            pltpu.SemaphoreType.DMA((GROUP,)),
            pltpu.SemaphoreType.DMA((share // tile + 5,)),
        ],
        cost_estimate=cost(2 * pairs * rows**3 * 40 + 14 * rows * rows * share, 12 * rows * share),
        name="first",
    )(place, *diagonals, *crosses, x, *pieces)


def second_kernel(*refs):
    place, bundles, m_ref, refs = refs[0], refs[1:9], refs[9], refs[10:]
    a_ref, b_ref, e_ref, w_out, gram, inverse, m, w_ref, merged, load, save = refs
    me, core = place[0], place[1]
    rows = m.shape[0] // 2
    copy = pltpu.make_async_copy(m_ref, m, load)
    copy.start()
    part = rows // (GROUP * CORES)
    for c in range(CORES):
        for s in range(GROUP):
            seat = (me ^ s) * CORES + (core ^ c)
            for b in range(2):
                gram[b, pl.ds(pl.multiple_of(seat * part, part), part), :] = bundles[c * GROUP + s][b * part : (b + 1) * part]
    packed = gram[1]
    turned = packed.T
    lower = lax.broadcasted_iota(jnp.int32, (rows, rows), 0) >= lax.broadcasted_iota(jnp.int32, (rows, rows), 1)
    diagonal = jnp.broadcast_to(bundles[0][2 * part : 2 * part + 1], (rows, rows))
    upper_gram = jnp.where(eye_mask(rows), diagonal, jnp.where(lower, turned, packed))
    resolvent([(jnp.where(lower, packed, turned), gram[0], upper_gram)], inverse, w_ref)
    copy.wait()
    saves = []
    early, half = e_ref.shape[1], a_ref.shape[1]
    for i, (ref, start) in enumerate(((a_ref, early), (b_ref, early + half), (e_ref, 0))):
        here = slice(start, start + ref.shape[1])
        merged[:, here] = merge_rows(m[:, here], w_ref[0])
        saves.append(pltpu.make_async_copy(merged.at[:, here], ref, save.at[i]))
        saves[-1].start()
    saves.append(pltpu.make_async_copy(w_ref, w_out, save.at[3]))
    saves[-1].start()
    for save_copy in saves:
        save_copy.wait()


def second(place, bundles, m, early):
    rows, share = m.shape[0] // 2, m.shape[1]
    half = (share - early) // 2
    return pl.pallas_call(
        second_kernel,
        out_shape=tuple(shape(rows, n, dtype=BF16) for n in (half, half, early)) + (shape(1, rows, 2 * rows, dtype=BF16),),
        in_specs=[SMEM] + [VMEM] * (2 * GROUP) + [ANY],
        out_specs=(ANY,) * 4,
        scratch_shapes=[
            pltpu.VMEM((2, rows, rows), F32),
            pltpu.VMEM((1, rows, rows), F32),
            pltpu.VMEM(m.shape, BF16),
            pltpu.VMEM((1, rows, 2 * rows), BF16),
            pltpu.VMEM((rows, share), BF16),
            pltpu.SemaphoreType.DMA,
            pltpu.SemaphoreType.DMA((4,)),
        ],
        cost_estimate=cost(2 * rows**3 * 40 + 4 * rows * rows * share, 6 * rows * share),
        name="second",
    )(place, *bundles, m)


def raw_first_kernel(share, place, w, x, xs, ys, d, out, block, pair, load, save):
    me = place[0]
    rows, raw = d.shape
    saves, loads, sources = [], {}, {}
    for v in PEERS:
        mine = x.at[:, pl.ds(pl.multiple_of((me ^ v) * share, 128), raw)]
        across = {1: xs.at[GROUP - 1], 2: ys.at[GROUP - 1], 3: d}[v]
        sources[v] = (mine, xs.at[SHARES_X.index(v ^ 1)], ys.at[SHARES_Y.index(v ^ 2)], across)
    for v, group in sources.items():
        for s, source in enumerate(group):
            target = block.at[v - 1, pl.ds(pl.multiple_of((me ^ s) * rows, rows), rows)]
            loads[v, s] = pltpu.make_async_copy(source, target, load.at[(v - 1) * GROUP + s])
            loads[v, s].start()
    for v in PEERS:
        for s in range(GROUP):
            loads[v, s].wait()
        for j in range(GROUP // 2):
            pair[v - 1, j * rows : (j + 1) * rows] = merge_rows(block[v - 1, 2 * j * rows : 2 * (j + 1) * rows], w[j])
        saves.append(pltpu.make_async_copy(pair.at[v - 1], out.at[v - 1], save.at[v - 1]))
        saves[-1].start()
    for copy in saves:
        copy.wait()


def raw_first(place, w, x, messages, share):
    rows, raw = messages[2].shape
    pairs = (GROUP - 1, 2 * rows, raw)
    return pl.pallas_call(
        functools.partial(raw_first_kernel, share),
        out_shape=shape(*pairs, dtype=BF16),
        in_specs=[SMEM, VMEM] + [HBM] * 4,
        out_specs=HBM,
        scratch_shapes=[
            pltpu.VMEM((GROUP - 1, GROUP * rows, raw), BF16),
            pltpu.VMEM(pairs, BF16),
            pltpu.SemaphoreType.DMA(((GROUP - 1) * GROUP,)),
            pltpu.SemaphoreType.DMA((GROUP - 1,)),
        ],
        cost_estimate=cost(8 * rows * rows * raw * (GROUP - 1), 12 * rows * raw * (GROUP - 1)),
        compiler_params=WHOLE,
        name="raw_first",
    )(place, w, x, *messages)


def late_kernel(share, raw, place, w, a, b, e, raws, *refs):
    early, (out, buffer, save) = refs[:-3], refs[-3:]
    me, half = place[0], a.shape[1]
    saves = []

    def put(source, owner, column):
        target = out.at[:, pl.ds(pl.multiple_of(owner * share + column, 128), source.shape[1])]
        saves.append(pltpu.make_async_copy(source, target, save.at[len(saves)]))
        saves[-1].start()

    put(e, me, 0)
    put(a, me, e.shape[1])
    put(b, me, e.shape[1] + half)
    work = [(raws.at[s - 1], s, 0) for s in PEERS]
    work += [(pair, s, raw) for pair, s in zip(early, PEERS)]
    work += [(pair, s, raw + early[0].shape[1]) for pair, s in zip(early[len(PEERS) :], PEERS)]
    for pair, s, column in work:
        spot = buffer.at[s - 1, :, column : column + pair.shape[1]]
        spot[...] = merge_rows(pair[...], w[0])
        put(spot, me ^ s, column)
    for copy in saves:
        copy.wait()


def late(place, w, a, b, e, raws, early, share):
    rows, size = e.shape
    return pl.pallas_call(
        functools.partial(late_kernel, share, raws.shape[2]),
        out_shape=shape(rows, GROUP * share, dtype=BF16),
        in_specs=[SMEM] + [VMEM] * (5 + len(early)),
        out_specs=HBM,
        scratch_shapes=[pltpu.VMEM((GROUP - 1, rows, size), BF16), pltpu.SemaphoreType.DMA((len(early) + GROUP + 2,))],
        cost_estimate=cost(4 * rows * rows * size * (GROUP - 1), 6 * rows * size * (GROUP - 1)),
        name="late",
    )(place, w, a, b, e, raws, *early)


def put_kernel(spots, share, place, *refs):
    count = len(spots)
    blocks, out, buffers, load, save = refs[:count], refs[count + 1], refs[count + 2 : -2], refs[-2], refs[-1]
    loads, saves = [], []
    for i, ((s, column), block, buffer) in enumerate(zip(spots, blocks, buffers)):
        start = pl.multiple_of((place[0] ^ s) * share + column, 128)
        loads.append(pltpu.make_async_copy(block, buffer, load.at[i]))
        loads[-1].start()
        saves.append(pltpu.make_async_copy(buffer, out.at[:, pl.ds(start, block.shape[1])], save.at[i]))
    for load_copy, save_copy in zip(loads, saves):
        load_copy.wait()
        save_copy.start()
    for copy in saves:
        copy.wait()


def put(place, out, blocks, spots, share):
    size = sum(b.size for b in blocks)
    return pl.pallas_call(
        functools.partial(put_kernel, spots, share),
        out_shape=shape(*out.shape, dtype=out.dtype),
        in_specs=[SMEM] + [HBM] * (len(blocks) + 1),
        out_specs=HBM,
        scratch_shapes=[pltpu.VMEM(b.shape, b.dtype) for b in blocks] + [pltpu.SemaphoreType.DMA((len(blocks),))] * 2,
        input_output_aliases={1 + len(blocks): 0},
        cost_estimate=cost(0, 4 * size),
        compiler_params=WHOLE,
        name="put",
    )(place, *blocks, out)


def over_chips(block):
    chips = lax.axis_size("feat") // CORES
    return total([block] + [send(block, "feat", CORES * s) for s in range(1, chips)])


def gather_group(bundle):
    mine = [bundle] + send_all([bundle] * len(PEERS), "dp", PEERS)
    return mine + [send(b, "feat", 1) for b in mine]


def run(sketches):
    x = sketches[0]
    rows, columns = x.shape
    share = columns // GROUP
    raw, ahead = 3 * share // 16, (3 * share // 16, share // 8)
    early = raw + sum(ahead)
    me = lax.axis_index("dp") % GROUP
    place = jnp.stack([me, lax.axis_index("feat") % CORES]).astype(jnp.int32)

    cuts, source = {}, x
    for s in PEERS:
        cuts[s] = lax.dynamic_slice(source, (0, (me ^ s) * share), (rows, share))
        if s == 2:
            source, cuts = lax.optimization_barrier((source, cuts))
    pieces = {s: send(cut, "dp", s) for s, cut in cuts.items()}
    keep, give = own_gram(place, x)
    own = over_chips(total([keep, send(give, "feat", 1)]))
    near, to_x, to_y, to_d = near_gram(place, x, pieces[1], raw)
    p2, p3, own, near = lax.optimization_barrier((pieces[2], pieces[3], own, near))

    keep, give, to_x = far_gram(place, near, p2, p3, to_x)
    parts = fold(keep, send(give, "feat", 1))
    parts, own, to_d = lax.optimization_barrier((parts, own, to_d))
    mine = total([parts[0]] + send_all(parts[1:], "dp", PEERS))
    diagonals = gather_group(own)
    from_d = send(to_d, "dp", 3)
    bundle = over_chips(mine)
    bundle, to_x, to_y = lax.optimization_barrier((bundle, to_x, to_y))
    crosses = gather_group(bundle)
    messages = [send(to_x, "dp", 1), send(to_y, "dp", 2), from_d]
    m, e, f, w0, keep, give = first(place, diagonals, crosses, x, [pieces[1], p2, p3], raw, ahead)

    parts = fold(keep, send(give, "feat", 1))
    parts, e, f = lax.optimization_barrier((parts, e, f))
    mine = total([parts[0]] + send_all(parts[1:], "dp", PEERS))
    pairs_a, pairs_b = [[send(block, "dp", s) for s in (1, 2)] for block in (e, f)]
    raws = raw_first(place, w0, x, messages, share)
    bundles = gather_group(over_chips(mine))
    pairs = pairs_a + [send(pairs_a[0], "dp", 2)] + pairs_b + [send(pairs_b[1], "dp", 1)]
    a, b, e, w1 = second(place, bundles, m, early)

    ax, by = send(a, "dp", 1), send(b, "dp", 2)
    bx, ay = send(b, "dp", 1), send(a, "dp", 2)
    ad, bd = send(ax, "dp", 2), send(by, "dp", 1)
    left, right = early, early + a.shape[1]
    out = late(place, w1, a, b, e, raws, pairs, share)
    out = put(place, out, [ax, by, bx, ay], ((1, left), (2, right), (1, right), (2, left)), share)
    out = put(place, out, [ad, bd], ((3, left), (3, right)), share)
    return out[None]


def solution(mesh):
    spec = P("dp", None, "feat")
    return jax.shard_map(run, mesh=mesh, in_specs=(spec,), out_specs=spec, check_vma=False)
```

```python
import functools

import jax
import jax.numpy as jnp
from jax import lax
from jax.experimental import pallas as pl
from jax.experimental.pallas import tpu as pltpu
from jax.sharding import PartitionSpec as P


LEVELS = 2
GROUP = 2**LEVELS
CORES = 2
PEERS = tuple(range(1, GROUP))
F32, BF16 = jnp.float32, jnp.bfloat16
NT = (((1,), (1,)), ((), ()))
NN = (((1,), (0,)), ((), ()))
VMEM = pl.BlockSpec(memory_space=pltpu.VMEM)
SMEM = pl.BlockSpec(memory_space=pltpu.SMEM)
ANY = pl.BlockSpec(memory_space=pl.ANY)
HBM = pl.BlockSpec(memory_space=pltpu.HBM)


def send(block, axis, shift):
    count = lax.axis_size(axis)
    return lax.ppermute(block, axis, [(i, i ^ shift) for i in range(count)])


def send_all(blocks, axis, shifts):
    return [send(b, axis, s) for b, s in zip(blocks, shifts)]


def dot(a, b, dims=NN):
    return lax.dot_general(a, b, dims, preferred_element_type=F32)


def shape(*dims, dtype=F32):
    return jax.ShapeDtypeStruct(dims, dtype)


WHOLE = pltpu.CompilerParams(vmem_limit_bytes=67_043_328)


def cost(flops, nbytes):
    return pl.CostEstimate(flops=int(flops), bytes_accessed=int(nbytes), transcendentals=0)


def halves(a):
    high = a.astype(BF16)
    return high, (a - high.astype(F32)).astype(BF16)


def product(a, b, dims=NN):
    (ah, al), (bh, bl) = a, b
    return dot(ah, bh, dims) + (dot(ah, bl, dims) + dot(al, bh, dims))


def eye_mask(n):
    return lax.broadcasted_iota(jnp.int32, (n, n), 0) == lax.broadcasted_iota(jnp.int32, (n, n), 1)


def invert(kernels, x_ref, limit):
    n = kernels[0].shape[0]
    mask = eye_mask(n)
    eye = jnp.where(mask, 1.0, 0.0)
    parts = [halves(k) for k in kernels]
    for j, k in enumerate(kernels):
        diag = jnp.where(mask, k, 0.0)
        row = 1.0 / jnp.sum(diag, axis=0, keepdims=True)
        col = 1.0 / jnp.sum(diag, axis=1, keepdims=True)
        scaled = jnp.where(mask, 0.0, k) * row
        spread = jnp.sum(scaled * (jnp.where(mask, 0.0, k) * col))
        bound = jnp.minimum(jnp.max(jnp.sum(jnp.abs(k), axis=0, keepdims=True)), limit)
        near = jnp.where(mask, row, -scaled * col)
        far = eye * (2.0 / (1.0 + bound))
        x_ref[j] = jnp.where(spread < 0.9, near, far)

    def step():
        worst = jnp.float32(0.0)
        for j, part in enumerate(parts):
            x = x_ref[j]
            xs = halves(x)
            rest = eye - product(part, xs)
            worst = jnp.maximum(worst, jnp.sum(rest * rest))
            x_ref[j] = x + dot(xs[0], rest.astype(BF16))
        return worst

    step()
    lax.while_loop(lambda s: (s[0] < 24) & (s[1] > 1e-6), lambda s: (s[0] + 1, step()), (jnp.int32(2), step()))


def resolvent(grams, x_ref, out_ref):
    n = grams[0][0].shape[0]
    mask = eye_mask(n)
    eye = jnp.where(mask, 1.0, 0.0)
    scaled = []
    for a, b, d in grams:
        average = jnp.sum(jnp.where(mask, a + d, 0.0)) / (2 * n)
        scaled.append((eye + a / average, b / average, eye + d / average))
    limit = 1.0 + 2 * n
    invert([d for _, _, d in scaled], x_ref, limit)
    ties, schurs = [], []
    for j, (a, b, d) in enumerate(scaled):
        bs = halves(b)
        tie = halves(product(bs, halves(x_ref[j])))
        ties.append(tie)
        schurs.append(a - product(tie, bs, NT))
    invert(schurs, x_ref, limit)
    for j, tie in enumerate(ties):
        x = x_ref[j]
        out_ref[j, :, :n] = x.astype(BF16)
        out_ref[j, :, n:] = (-product(halves(x), tie)).astype(BF16)


def own_gram_kernel(place, x_ref, keep_ref, give_ref, acc):
    step = pl.program_id(0)
    core = place[1]
    half = keep_ref.shape[0]

    @pl.when(step == 0)
    def _():
        acc[...] = jnp.zeros_like(acc)

    acc[...] += dot(x_ref[...], x_ref[...], NT)

    @pl.when(step == pl.num_programs(0) - 1)
    def _():
        keep_ref[...] = acc[pl.ds(pl.multiple_of(core * half, half), half), :]
        give_ref[...] = acc[pl.ds(pl.multiple_of((1 - core) * half, half), half), :]


def own_gram(place, x, tile=2048):
    rows, columns = x.shape
    half = shape(rows // CORES, rows)
    spec = pl.BlockSpec((rows // CORES, rows), lambda k, place: (0, 0))
    return pl.pallas_call(
        own_gram_kernel,
        out_shape=(half, half),
        grid_spec=pltpu.PrefetchScalarGridSpec(
            num_scalar_prefetch=1,
            grid=(columns // tile,),
            in_specs=[pl.BlockSpec((rows, tile), lambda k, place: (0, k))],
            out_specs=(spec, spec),
            scratch_shapes=[pltpu.VMEM((rows, rows), F32)],
        ),
        cost_estimate=cost(2 * rows * rows * columns, 2 * rows * columns),
        name="own_gram",
    )(place, x)


def pair_gram(me, sources, block, load, chunk):
    rows, share = block.shape[1:]
    copies = []
    for k in range(share // chunk):
        here = slice(k * chunk, (k + 1) * chunk)
        for i, (s, source) in enumerate(sources):
            target = block.at[(me ^ s) % 2, :, here]
            copies.append(pltpu.make_async_copy(source(k * chunk, chunk), target, load.at[2 * k + i]))
            copies[-1].start()
    value = jnp.zeros((rows, rows), F32)
    for k in range(share // chunk):
        copies[2 * k].wait()
        copies[2 * k + 1].wait()
        here = slice(k * chunk, (k + 1) * chunk)
        value = value + dot(block[0, :, here], block[1, :, here], NT)
    return value


SHARES_X, SHARES_Y = (0, 2, 3), (0, 1, 3)


def near_gram_kernel(chunk, place, x, p1, out_ref, x_ref, y_ref, d_ref, block, pack, load, save):
    me = place[0]
    share, raw = p1.shape[1], d_ref.shape[1]

    def mine(column, size, t=0):
        return x.at[:, pl.ds(pl.multiple_of((me ^ t) * share + column, 128), size)]

    def theirs(column, size):
        return p1.at[:, column : column + size]

    packs = [pltpu.make_async_copy(mine(0, raw, t), pack.at[t], save.at[t]) for t in range(GROUP)]
    packs.append(pltpu.make_async_copy(theirs(0, raw), pack.at[GROUP], save.at[GROUP]))
    for copy in packs:
        copy.start()
    out_ref[...] = pair_gram(me, ((0, mine), (1, theirs)), block, load, chunk)
    for copy in packs:
        copy.wait()
    targets = [(t, x_ref.at[i]) for i, t in enumerate(SHARES_X)] + [(t, y_ref.at[i]) for i, t in enumerate(SHARES_Y)]
    targets += [(GROUP, y_ref.at[GROUP - 1]), (0, d_ref)]
    copies = [pltpu.make_async_copy(pack.at[t], target, save.at[i]) for i, (t, target) in enumerate(targets)]
    for copy in copies:
        copy.start()
    for copy in copies:
        copy.wait()


def near_gram(place, x, p1, raw, chunk=512):
    rows, share = p1.shape
    message = shape(GROUP, rows, raw, dtype=BF16)
    return pl.pallas_call(
        functools.partial(near_gram_kernel, chunk),
        out_shape=(shape(rows, rows), message, message, shape(rows, raw, dtype=BF16)),
        in_specs=[SMEM, HBM, HBM],
        out_specs=(VMEM, HBM, HBM, HBM),
        scratch_shapes=[
            pltpu.VMEM((2, rows, share), BF16),
            pltpu.VMEM((GROUP + 1, rows, raw), BF16),
            pltpu.SemaphoreType.DMA((2 * share // chunk,)),
            pltpu.SemaphoreType.DMA((2 * GROUP,)),
        ],
        cost_estimate=cost(2 * rows * rows * share, 4 * rows * share),
        compiler_params=WHOLE,
        name="near_gram",
    )(place, x, p1)


def far_gram_kernel(chunk, place, near, p2, p3, _, keep_out, give_out, x_ref, block, acc, keep_ref, give_ref, load, save):
    me, core = place[0], place[1]
    first_load = pltpu.make_async_copy(near, acc.at[me // 2], save.at[3])
    first_load.start()
    sources = tuple((s, lambda column, size, p=p: p.at[:, column : column + size]) for s, p in ((2, p2), (3, p3)))
    acc[1 - me // 2] = pair_gram(me, sources, block, load, chunk)
    copies = [pltpu.make_async_copy(block.at[(me ^ 2) % 2, :, : x_ref.shape[2]], x_ref.at[GROUP - 1], save.at[0])]
    copies[0].start()
    first_load.wait()
    part = keep_ref.shape[1]
    for s in range(GROUP):
        to = me ^ s
        pair, start = to // 2, (to % 2) * (CORES * part)
        keep_ref[s] = acc[pair, pl.ds(pl.multiple_of(start + core * part, part), part), :]
        give_ref[s] = acc[pair, pl.ds(pl.multiple_of(start + (1 - core) * part, part), part), :]
    for i, (source, target) in enumerate(((give_ref, give_out), (keep_ref, keep_out))):
        copies.append(pltpu.make_async_copy(source, target, save.at[1 + i]))
        copies[-1].start()
    for copy in copies:
        copy.wait()


def far_gram(place, near, p2, p3, message, chunk=512):
    rows, share = p2.shape
    out = shape(GROUP, rows // (2 * CORES), rows)
    return pl.pallas_call(
        functools.partial(far_gram_kernel, chunk),
        out_shape=(out, out, shape(*message.shape, dtype=BF16)),
        in_specs=[SMEM, HBM, HBM, HBM, HBM],
        out_specs=(HBM, HBM, HBM),
        scratch_shapes=[
            pltpu.VMEM((2, rows, share), BF16),
            pltpu.VMEM((GROUP // 2, rows, rows), F32),
            pltpu.VMEM(out.shape, F32),
            pltpu.VMEM(out.shape, F32),
            pltpu.SemaphoreType.DMA((2 * share // chunk,)),
            pltpu.SemaphoreType.DMA((4,)),
        ],
        input_output_aliases={4: 2},
        cost_estimate=cost(2 * rows * rows * share, 4 * rows * share),
        compiler_params=WHOLE,
        name="far_gram",
    )(place, near, p2, p3, message)


def fold(mine, theirs):
    return [mine[s] + theirs[s] for s in range(mine.shape[0])]


def total(arrays):
    return functools.reduce(jnp.add, arrays)


def merge_rows(stacked, w):
    lower = stacked[: w.shape[0]]
    return (lower.astype(F32) - dot(w, stacked)).astype(BF16)


def first_kernel(raw, tile, *refs):
    place, tails, crosses, (x, p1, p2, p3), refs = refs[0], refs[1:9], refs[9:17], refs[17:21], refs[21:]
    m_ref, e_ref, f_ref, w_out, keep_out, give_out, cross, diag, inverse, block, m, acc, keep_ref, give_ref, w, load, save = refs
    me, core = place[0], place[1]
    rows, share = p1.shape
    sources = [x.at[:, pl.ds(pl.multiple_of(me * share, share), share)], p1, p2, p3]
    loads = [
        pltpu.make_async_copy(source, block.at[pl.ds(pl.multiple_of((me ^ s) * rows, rows), rows)], load.at[s])
        for s, source in enumerate(sources)
    ]
    for copy in loads:
        copy.start()

    part, half = rows // (2 * CORES), rows // CORES
    for c in range(CORES):
        for s in range(GROUP):
            source, seat = me ^ s, core ^ c
            start = (source % 2) * (CORES * part) + seat * part
            cross[source // 2, pl.ds(pl.multiple_of(start, part), part), :] = crosses[c * GROUP + s][...]
            diag[source, pl.ds(pl.multiple_of(seat * half, half), half), :] = tails[c * GROUP + s][...]
    grams = [(diag[2 * j], cross[j], diag[2 * j + 1]) for j in range(GROUP // 2)]
    resolvent(grams, inverse, w)
    for copy in loads:
        copy.wait()

    acc[...] = jnp.zeros_like(acc)
    saves = [pltpu.make_async_copy(w, w_out, save.at[share // tile + 4])]
    saves[0].start()
    for k in range(share // tile):
        here = slice(k * tile, (k + 1) * tile)
        m0 = merge_rows(block[: 2 * rows, here], w[0])
        m1 = merge_rows(block[2 * rows :, here], w[1])
        m[:rows, here] = m0
        m[rows:, here] = m1
        saves.append(pltpu.make_async_copy(m.at[:, here], m_ref.at[:, here], save.at[k]))
        saves[-1].start()
        acc[0] += dot(m0, m0, NT)
        acc[1] += dot(m0, m1, NT)
        acc[2] += dot(m1, m1, NT)
    start = raw
    for i, ref in enumerate((e_ref, f_ref)):
        source = m.at[:, start : start + ref.shape[1]]
        saves.append(pltpu.make_async_copy(source, ref, save.at[share // tile + i]))
        saves[-1].start()
        start += ref.shape[1]
    lower = lax.broadcasted_iota(jnp.int32, (rows, rows), 0) >= lax.broadcasted_iota(jnp.int32, (rows, rows), 1)
    row = jnp.sum(jnp.where(eye_mask(rows), acc[2], 0.0), axis=0, keepdims=True)
    acc[2] = jnp.where(lower, acc[0], acc[2])
    part = rows // (GROUP * CORES)
    for s in range(GROUP):
        to = me ^ s
        for ref, seat in ((give_ref, to * CORES + 1 - core), (keep_ref, to * CORES + core)):
            here = pl.ds(pl.multiple_of(seat * part, part), part)
            ref[s, :part] = acc[1, here, :]
            ref[s, part : 2 * part] = acc[2, here, :]
            ref[s, 2 * part :] = jnp.broadcast_to(row, (8, rows))
    for i, (source, target) in enumerate(((give_ref, give_out), (keep_ref, keep_out))):
        saves.append(pltpu.make_async_copy(source, target, save.at[share // tile + 2 + i]))
        saves[-1].start()
    for copy in saves:
        copy.wait()


def first(place, diagonals, crosses, x, pieces, raw, ahead, tile=512):
    rows, share = pieces[0].shape
    pairs = GROUP // 2
    out = shape(GROUP, 2 * rows // (GROUP * CORES) + 8, rows)
    return pl.pallas_call(
        functools.partial(first_kernel, raw, tile),
        out_shape=tuple(shape(pairs * rows, n, dtype=BF16) for n in (share, *ahead)) + (shape(pairs, rows, 2 * rows, dtype=BF16), out, out),
        in_specs=[SMEM] + [VMEM] * (4 * GROUP) + [HBM] * 4,
        out_specs=(ANY,) * 6,
        scratch_shapes=[
            pltpu.VMEM((pairs, rows, rows), F32),
            pltpu.VMEM((GROUP, rows, rows), F32),
            pltpu.VMEM((pairs, rows, rows), F32),
            pltpu.VMEM((GROUP * rows, share), BF16),
            pltpu.VMEM((pairs * rows, share), BF16),
            pltpu.VMEM((3, rows, rows), F32),
            pltpu.VMEM(out.shape, F32),
            pltpu.VMEM(out.shape, F32),
            pltpu.VMEM((pairs, rows, 2 * rows), BF16),
            pltpu.SemaphoreType.DMA((GROUP,)),
            pltpu.SemaphoreType.DMA((share // tile + 5,)),
        ],
        cost_estimate=cost(2 * pairs * rows**3 * 40 + 14 * rows * rows * share, 12 * rows * share),
        name="first",
    )(place, *diagonals, *crosses, x, *pieces)


def second_kernel(*refs):
    place, bundles, m_ref, refs = refs[0], refs[1:9], refs[9], refs[10:]
    a_ref, b_ref, w_out, gram, inverse, m, w_ref, merged, load, save = refs
    me, core = place[0], place[1]
    rows = m.shape[0] // 2
    copy = pltpu.make_async_copy(m_ref.at[:, m_ref.shape[1] - m.shape[1] :], m, load)
    copy.start()
    part = rows // (GROUP * CORES)
    for c in range(CORES):
        for s in range(GROUP):
            seat = (me ^ s) * CORES + (core ^ c)
            for b in range(2):
                gram[b, pl.ds(pl.multiple_of(seat * part, part), part), :] = bundles[c * GROUP + s][b * part : (b + 1) * part]
    packed = gram[1]
    turned = packed.T
    lower = lax.broadcasted_iota(jnp.int32, (rows, rows), 0) >= lax.broadcasted_iota(jnp.int32, (rows, rows), 1)
    diagonal = jnp.broadcast_to(bundles[0][2 * part : 2 * part + 1], (rows, rows))
    upper_gram = jnp.where(eye_mask(rows), diagonal, jnp.where(lower, turned, packed))
    resolvent([(jnp.where(lower, packed, turned), gram[0], upper_gram)], inverse, w_ref)
    copy.wait()
    saves = [pltpu.make_async_copy(w_ref, w_out, save.at[2])]
    saves[0].start()
    half = a_ref.shape[1]
    for i, ref in enumerate((a_ref, b_ref)):
        here = slice(i * half, (i + 1) * half)
        merged[:, here] = merge_rows(m[:, here], w_ref[0])
        saves.append(pltpu.make_async_copy(merged.at[:, here], ref, save.at[i]))
        saves[-1].start()
    for save_copy in saves:
        save_copy.wait()


def second(place, bundles, m, early):
    rows, share = m.shape[0] // 2, m.shape[1]
    half = (share - early) // 2
    return pl.pallas_call(
        second_kernel,
        out_shape=(shape(rows, half, dtype=BF16),) * 2 + (shape(1, rows, 2 * rows, dtype=BF16),),
        in_specs=[SMEM] + [VMEM] * (2 * GROUP) + [ANY],
        out_specs=(ANY,) * 3,
        scratch_shapes=[
            pltpu.VMEM((2, rows, rows), F32),
            pltpu.VMEM((1, rows, rows), F32),
            pltpu.VMEM((2 * rows, 2 * half), BF16),
            pltpu.VMEM((1, rows, 2 * rows), BF16),
            pltpu.VMEM((rows, 2 * half), BF16),
            pltpu.SemaphoreType.DMA,
            pltpu.SemaphoreType.DMA((3,)),
        ],
        cost_estimate=cost(2 * rows**3 * 40 + 8 * rows * rows * half, 6 * rows * share),
        name="second",
    )(place, *bundles, m)


def raw_merge_kernel(share, place, w0, w1, x, xs, ys, d, _, out, block, pair, buffer, load, save):
    me = place[0]
    rows, raw = d.shape
    saves = []
    sources = {}
    for v in PEERS:
        mine = x.at[:, pl.ds(pl.multiple_of((me ^ v) * share, 128), raw)]
        across = {1: xs.at[GROUP - 1], 2: ys.at[GROUP - 1], 3: d}[v]
        sources[v] = (mine, xs.at[SHARES_X.index(v ^ 1)], ys.at[SHARES_Y.index(v ^ 2)], across)
    loads = {}
    for v, group in sources.items():
        for s, source in enumerate(group):
            target = block.at[v - 1, pl.ds(pl.multiple_of((me ^ s) * rows, rows), rows)]
            loads[v, s] = pltpu.make_async_copy(source, target, load.at[(v - 1) * GROUP + s])
            loads[v, s].start()
    for v in sources:
        for s in range(GROUP):
            loads[v, s].wait()
        for j in range(GROUP // 2):
            pair[j * rows : (j + 1) * rows] = merge_rows(block[v - 1, 2 * j * rows : 2 * (j + 1) * rows], w0[j])
        buffer[v - 1] = merge_rows(pair[...], w1[0])
        target = out.at[:, pl.ds(pl.multiple_of((me ^ v) * share, 128), raw)]
        saves.append(pltpu.make_async_copy(buffer.at[v - 1], target, save.at[v - 1]))
        saves[-1].start()
    for copy in saves:
        copy.wait()


def raw_merge(place, w0, w1, x, messages, out, share):
    rows, raw = messages[2].shape
    return pl.pallas_call(
        functools.partial(raw_merge_kernel, share),
        out_shape=shape(*out.shape, dtype=BF16),
        in_specs=[SMEM, VMEM, VMEM] + [HBM] * 5,
        out_specs=HBM,
        scratch_shapes=[
            pltpu.VMEM((GROUP - 1, GROUP * rows, raw), BF16),
            pltpu.VMEM((2 * rows, raw), BF16),
            pltpu.VMEM((GROUP - 1, rows, raw), BF16),
            pltpu.SemaphoreType.DMA(((GROUP - 1) * GROUP,)),
            pltpu.SemaphoreType.DMA((GROUP - 1,)),
        ],
        input_output_aliases={7: 0},
        cost_estimate=cost(12 * rows * rows * raw * (GROUP - 1), 10 * rows * raw * (GROUP - 1)),
        compiler_params=WHOLE,
        name="raw_merge",
    )(place, w0, w1, x, *messages, out)


def late_kernel(share, raw, place, w, a, b, m, *refs):
    early, (out, mine, own, buffer, load, save) = refs[:-6], refs[-6:]
    me, size, half = place[0], mine.shape[1], a.shape[1]
    copy = pltpu.make_async_copy(m.at[:, :size], mine, load)
    copy.start()
    saves = []

    def put(source, owner, column):
        target = out.at[:, pl.ds(pl.multiple_of(owner * share + column, 128), source.shape[1])]
        saves.append(pltpu.make_async_copy(source, target, save.at[len(saves)]))
        saves[-1].start()

    put(a, me, size)
    put(b, me, size + half)
    work = [(pair, s, raw) for pair, s in zip(early, PEERS)]
    work += [(pair, s, raw + early[0].shape[1]) for pair, s in zip(early[len(PEERS) :], PEERS)]
    for pair, s, column in work:
        spot = buffer.at[s - 1, :, column - raw : column - raw + pair.shape[1]]
        spot[...] = merge_rows(pair[...], w[0])
        put(spot, me ^ s, column)
    copy.wait()
    own[...] = merge_rows(mine[...], w[0])
    put(own, me, 0)
    for copy in saves:
        copy.wait()


def late(place, w, a, b, m, pairs, raw, share):
    rows, size = a.shape[0], share - 2 * a.shape[1]
    return pl.pallas_call(
        functools.partial(late_kernel, share, raw),
        out_shape=shape(rows, GROUP * share, dtype=BF16),
        in_specs=[SMEM] + [VMEM] * 3 + [HBM] + [VMEM] * len(pairs),
        out_specs=HBM,
        scratch_shapes=[
            pltpu.VMEM((2 * rows, size), BF16),
            pltpu.VMEM((rows, size), BF16),
            pltpu.VMEM((GROUP - 1, rows, size - raw), BF16),
            pltpu.SemaphoreType.DMA,
            pltpu.SemaphoreType.DMA((len(pairs) + 3,)),
        ],
        cost_estimate=cost(4 * rows * rows * size * GROUP, 6 * rows * size * GROUP),
        name="late",
    )(place, w, a, b, m, *pairs)


def put_kernel(spots, share, place, *refs):
    count = len(spots)
    blocks, out, buffers, load, save = refs[:count], refs[count + 1], refs[count + 2 : -2], refs[-2], refs[-1]
    loads, saves = [], []
    for i, ((s, column), block, buffer) in enumerate(zip(spots, blocks, buffers)):
        start = pl.multiple_of((place[0] ^ s) * share + column, 128)
        loads.append(pltpu.make_async_copy(block, buffer, load.at[i]))
        loads[-1].start()
        saves.append(pltpu.make_async_copy(buffer, out.at[:, pl.ds(start, block.shape[1])], save.at[i]))
    for load_copy, save_copy in zip(loads, saves):
        load_copy.wait()
        save_copy.start()
    for copy in saves:
        copy.wait()


def put(place, out, blocks, spots, share):
    size = sum(b.size for b in blocks)
    return pl.pallas_call(
        functools.partial(put_kernel, spots, share),
        out_shape=shape(*out.shape, dtype=out.dtype),
        in_specs=[SMEM] + [HBM] * (len(blocks) + 1),
        out_specs=HBM,
        scratch_shapes=[pltpu.VMEM(b.shape, b.dtype) for b in blocks] + [pltpu.SemaphoreType.DMA((len(blocks),))] * 2,
        input_output_aliases={1 + len(blocks): 0},
        cost_estimate=cost(0, 4 * size),
        compiler_params=WHOLE,
        name="put",
    )(place, *blocks, out)


def over_chips(block):
    chips = lax.axis_size("feat") // CORES
    return total([block] + [send(block, "feat", CORES * s) for s in range(1, chips)])


def gather_group(bundle):
    mine = [bundle] + send_all([bundle] * len(PEERS), "dp", PEERS)
    return mine + [send(b, "feat", 1) for b in mine]


def run(sketches):
    x = sketches[0]
    rows, columns = x.shape
    share = columns // GROUP
    raw, ahead = 3 * share // 16, (3 * share // 16, share // 8)
    early = raw + sum(ahead)
    me = lax.axis_index("dp") % GROUP
    place = jnp.stack([me, lax.axis_index("feat") % CORES]).astype(jnp.int32)

    cuts, source = {}, x
    for s in PEERS:
        cuts[s] = lax.dynamic_slice(source, (0, (me ^ s) * share), (rows, share))
        if s == 2:
            source, cuts = lax.optimization_barrier((source, cuts))
    pieces = {s: send(cut, "dp", s) for s, cut in cuts.items()}
    keep, give = own_gram(place, x)
    own = over_chips(total([keep, send(give, "feat", 1)]))
    near, to_x, to_y, to_d = near_gram(place, x, pieces[1], raw)
    p2, p3, own, near = lax.optimization_barrier((pieces[2], pieces[3], own, near))

    keep, give, to_x = far_gram(place, near, p2, p3, to_x)
    parts = fold(keep, send(give, "feat", 1))
    parts, own, to_d = lax.optimization_barrier((parts, own, to_d))
    mine = total([parts[0]] + send_all(parts[1:], "dp", PEERS))
    diagonals = gather_group(own)
    from_d = send(to_d, "dp", 3)
    bundle = over_chips(mine)
    bundle, to_x, to_y = lax.optimization_barrier((bundle, to_x, to_y))
    crosses = gather_group(bundle)
    messages = [send(to_x, "dp", 1), send(to_y, "dp", 2), from_d]
    m, e, f, w0, keep, give = first(place, diagonals, crosses, x, [pieces[1], p2, p3], raw, ahead)

    parts = fold(keep, send(give, "feat", 1))
    parts, e, f = lax.optimization_barrier((parts, e, f))
    mine = total([parts[0]] + send_all(parts[1:], "dp", PEERS))
    pairs_a, pairs_b = [[send(block, "dp", s) for s in (1, 2)] for block in (e, f)]
    bundles = gather_group(over_chips(mine))
    pairs = pairs_a + [send(pairs_a[0], "dp", 2)] + pairs_b + [send(pairs_b[1], "dp", 1)]
    a, b, w1 = second(place, bundles, m, early)

    ax, by = send(a, "dp", 1), send(b, "dp", 2)
    bx, ay = send(b, "dp", 1), send(a, "dp", 2)
    ad, bd = send(ax, "dp", 2), send(by, "dp", 1)
    left, right = early, early + a.shape[1]
    out = late(place, w1, a, b, m, pairs, raw, share)
    out = raw_merge(place, w0, w1, x, messages, out, share)
    out = put(place, out, [ax, by, bx, ay], ((1, left), (2, right), (1, right), (2, left)), share)
    out = put(place, out, [ad, bd], ((3, left), (3, right)), share)
    return out[None]


def solution(mesh):
    spec = P("dp", None, "feat")
    return jax.shard_map(run, mesh=mesh, in_specs=(spec,), out_specs=spec, check_vma=False)
```

```python
import functools

import jax
import jax.numpy as jnp
from jax import lax
from jax.experimental import pallas as pl
from jax.experimental.pallas import tpu as pltpu
from jax.sharding import PartitionSpec as P


LEVELS = 2
GROUP = 2**LEVELS
CORES = 2
PEERS = tuple(range(1, GROUP))
F32, BF16 = jnp.float32, jnp.bfloat16
NT = (((1,), (1,)), ((), ()))
NN = (((1,), (0,)), ((), ()))
VMEM = pl.BlockSpec(memory_space=pltpu.VMEM)
SMEM = pl.BlockSpec(memory_space=pltpu.SMEM)
ANY = pl.BlockSpec(memory_space=pl.ANY)
HBM = pl.BlockSpec(memory_space=pltpu.HBM)


def send(block, axis, shift):
    count = lax.axis_size(axis)
    return lax.ppermute(block, axis, [(i, i ^ shift) for i in range(count)])


def send_all(blocks, axis, shifts):
    return [send(b, axis, s) for b, s in zip(blocks, shifts)]


def dot(a, b, dims=NN):
    return lax.dot_general(a, b, dims, preferred_element_type=F32)


def shape(*dims, dtype=F32):
    return jax.ShapeDtypeStruct(dims, dtype)


WHOLE = pltpu.CompilerParams(vmem_limit_bytes=67_043_328)


def cost(flops, nbytes):
    return pl.CostEstimate(flops=int(flops), bytes_accessed=int(nbytes), transcendentals=0)


def halves(a):
    high = a.astype(BF16)
    return high, (a - high.astype(F32)).astype(BF16)


def product(a, b, dims=NN):
    (ah, al), (bh, bl) = a, b
    return dot(ah, bh, dims) + (dot(ah, bl, dims) + dot(al, bh, dims))


def eye_mask(n):
    return lax.broadcasted_iota(jnp.int32, (n, n), 0) == lax.broadcasted_iota(jnp.int32, (n, n), 1)


def invert(kernels, x_ref, limit):
    n = kernels[0].shape[0]
    mask = eye_mask(n)
    eye = jnp.where(mask, 1.0, 0.0)
    parts = [halves(k) for k in kernels]
    for j, k in enumerate(kernels):
        diag = jnp.where(mask, k, 0.0)
        row = 1.0 / jnp.sum(diag, axis=0, keepdims=True)
        col = 1.0 / jnp.sum(diag, axis=1, keepdims=True)
        scaled = jnp.where(mask, 0.0, k) * row
        spread = jnp.sum(scaled * (jnp.where(mask, 0.0, k) * col))
        bound = jnp.minimum(jnp.max(jnp.sum(jnp.abs(k), axis=0, keepdims=True)), limit)
        near = jnp.where(mask, row, -scaled * col)
        far = eye * (2.0 / (1.0 + bound))
        x_ref[j] = jnp.where(spread < 0.9, near, far)

    def step():
        worst = jnp.float32(0.0)
        for j, part in enumerate(parts):
            x = x_ref[j]
            xs = halves(x)
            rest = eye - product(part, xs)
            worst = jnp.maximum(worst, jnp.sum(rest * rest))
            x_ref[j] = x + dot(xs[0], rest.astype(BF16))
        return worst

    step()
    lax.while_loop(lambda s: (s[0] < 24) & (s[1] > 1e-6), lambda s: (s[0] + 1, step()), (jnp.int32(2), step()))


def resolvent(grams, x_ref, out_ref, ready=lambda: None):
    n = grams[0][0].shape[0]
    mask = eye_mask(n)
    eye = jnp.where(mask, 1.0, 0.0)
    scales = [(2 * n) / jnp.sum(jnp.where(mask, a + d, 0.0)) for a, _, d in grams]
    limit = 1.0 + 2 * n
    invert([eye + d * scale for (_, _, d), scale in zip(grams, scales)], x_ref, limit)
    ready()
    ties, schurs = [], []
    for j, ((a, b, _), scale) in enumerate(zip(grams, scales)):
        bs = halves(b[...] * scale)
        tie = halves(product(bs, halves(x_ref[j])))
        ties.append(tie)
        schurs.append(eye + a * scale - product(tie, bs, NT))
    invert(schurs, x_ref, limit)
    for j, tie in enumerate(ties):
        x = x_ref[j]
        out_ref[j, :, :n] = x.astype(BF16)
        out_ref[j, :, n:] = (-product(halves(x), tie)).astype(BF16)


def own_gram_kernel(place, x_ref, keep_ref, give_ref, acc):
    step = pl.program_id(0)
    core = place[1]
    half = keep_ref.shape[0]

    @pl.when(step == 0)
    def _():
        acc[...] = jnp.zeros_like(acc)

    acc[...] += dot(x_ref[...], x_ref[...], NT)

    @pl.when(step == pl.num_programs(0) - 1)
    def _():
        keep_ref[...] = acc[pl.ds(pl.multiple_of(core * half, half), half), :]
        give_ref[...] = acc[pl.ds(pl.multiple_of((1 - core) * half, half), half), :]


def own_gram(place, x, tile=2048):
    rows, columns = x.shape
    half = shape(rows // CORES, rows)
    spec = pl.BlockSpec((rows // CORES, rows), lambda k, place: (0, 0))
    return pl.pallas_call(
        own_gram_kernel,
        out_shape=(half, half),
        grid_spec=pltpu.PrefetchScalarGridSpec(
            num_scalar_prefetch=1,
            grid=(columns // tile,),
            in_specs=[pl.BlockSpec((rows, tile), lambda k, place: (0, k))],
            out_specs=(spec, spec),
            scratch_shapes=[pltpu.VMEM((rows, rows), F32)],
        ),
        cost_estimate=cost(2 * rows * rows * columns, 2 * rows * columns),
        name="own_gram",
    )(place, x)


def pair_gram(me, sources, block, load, chunk):
    rows, share = block.shape[1:]
    copies = []
    for k in range(share // chunk):
        here = slice(k * chunk, (k + 1) * chunk)
        for i, (s, source) in enumerate(sources):
            target = block.at[(me ^ s) % 2, :, here]
            copies.append(pltpu.make_async_copy(source(k * chunk, chunk), target, load.at[2 * k + i]))
            copies[-1].start()
    value = jnp.zeros((rows, rows), F32)
    for k in range(share // chunk):
        copies[2 * k].wait()
        copies[2 * k + 1].wait()
        here = slice(k * chunk, (k + 1) * chunk)
        value = value + dot(block[0, :, here], block[1, :, here], NT)
    return value


SHARES_X, SHARES_Y = (0, 2, 3), (0, 1, 3)


def near_gram_kernel(chunk, place, x, p1, out_ref, x_ref, y_ref, d_ref, block, pack, load, save):
    me = place[0]
    share, raw = p1.shape[1], d_ref.shape[1]

    def mine(column, size, t=0):
        return x.at[:, pl.ds(pl.multiple_of((me ^ t) * share + column, 128), size)]

    def theirs(column, size):
        return p1.at[:, column : column + size]

    packs = [pltpu.make_async_copy(mine(0, raw, t), pack.at[t], save.at[t]) for t in range(GROUP)]
    packs.append(pltpu.make_async_copy(theirs(0, raw), pack.at[GROUP], save.at[GROUP]))
    for copy in packs:
        copy.start()
    out_ref[...] = pair_gram(me, ((0, mine), (1, theirs)), block, load, chunk)
    for copy in packs:
        copy.wait()
    targets = [(t, x_ref.at[i]) for i, t in enumerate(SHARES_X)] + [(t, y_ref.at[i]) for i, t in enumerate(SHARES_Y)]
    targets += [(GROUP, y_ref.at[GROUP - 1]), (0, d_ref)]
    copies = [pltpu.make_async_copy(pack.at[t], target, save.at[i]) for i, (t, target) in enumerate(targets)]
    for copy in copies:
        copy.start()
    for copy in copies:
        copy.wait()


def near_gram(place, x, p1, raw, chunk=512):
    rows, share = p1.shape
    message = shape(GROUP, rows, raw, dtype=BF16)
    return pl.pallas_call(
        functools.partial(near_gram_kernel, chunk),
        out_shape=(shape(rows, rows), message, message, shape(rows, raw, dtype=BF16)),
        in_specs=[SMEM, HBM, HBM],
        out_specs=(VMEM, HBM, HBM, HBM),
        scratch_shapes=[
            pltpu.VMEM((2, rows, share), BF16),
            pltpu.VMEM((GROUP + 1, rows, raw), BF16),
            pltpu.SemaphoreType.DMA((2 * share // chunk,)),
            pltpu.SemaphoreType.DMA((2 * GROUP,)),
        ],
        cost_estimate=cost(2 * rows * rows * share, 4 * rows * share),
        compiler_params=WHOLE,
        name="near_gram",
    )(place, x, p1)


def far_gram_kernel(chunk, place, near, p2, p3, _, keep_out, give_out, x_ref, block, acc, keep_ref, give_ref, load, save):
    me, core = place[0], place[1]
    first_load = pltpu.make_async_copy(near, acc.at[me // 2], save.at[3])
    first_load.start()
    sources = tuple((s, lambda column, size, p=p: p.at[:, column : column + size]) for s, p in ((2, p2), (3, p3)))
    acc[1 - me // 2] = pair_gram(me, sources, block, load, chunk)
    copies = [pltpu.make_async_copy(block.at[(me ^ 2) % 2, :, : x_ref.shape[2]], x_ref.at[GROUP - 1], save.at[0])]
    copies[0].start()
    first_load.wait()
    part = keep_ref.shape[1]
    for s in range(GROUP):
        to = me ^ s
        pair, start = to // 2, (to % 2) * (CORES * part)
        keep_ref[s] = acc[pair, pl.ds(pl.multiple_of(start + core * part, part), part), :]
        give_ref[s] = acc[pair, pl.ds(pl.multiple_of(start + (1 - core) * part, part), part), :]
    for i, (source, target) in enumerate(((give_ref, give_out), (keep_ref, keep_out))):
        copies.append(pltpu.make_async_copy(source, target, save.at[1 + i]))
        copies[-1].start()
    for copy in copies:
        copy.wait()


def far_gram(place, near, p2, p3, message, chunk=512):
    rows, share = p2.shape
    out = shape(GROUP, rows // (2 * CORES), rows)
    return pl.pallas_call(
        functools.partial(far_gram_kernel, chunk),
        out_shape=(out, out, shape(*message.shape, dtype=BF16)),
        in_specs=[SMEM, HBM, HBM, HBM, HBM],
        out_specs=(HBM, HBM, HBM),
        scratch_shapes=[
            pltpu.VMEM((2, rows, share), BF16),
            pltpu.VMEM((GROUP // 2, rows, rows), F32),
            pltpu.VMEM(out.shape, F32),
            pltpu.VMEM(out.shape, F32),
            pltpu.SemaphoreType.DMA((2 * share // chunk,)),
            pltpu.SemaphoreType.DMA((4,)),
        ],
        input_output_aliases={4: 2},
        cost_estimate=cost(2 * rows * rows * share, 4 * rows * share),
        compiler_params=WHOLE,
        name="far_gram",
    )(place, near, p2, p3, message)


def fold(mine, theirs):
    return [mine[s] + theirs[s] for s in range(mine.shape[0])]


def total(arrays):
    return functools.reduce(jnp.add, arrays)


def merge_rows(stacked, w):
    lower = stacked[: w.shape[0]]
    return (lower.astype(F32) - dot(w, stacked)).astype(BF16)


def first_kernel(raw, tile, *refs):
    place, tails, crosses, (x, p1, p2, p3), refs = refs[0], refs[1:9], refs[9:17], refs[17:21], refs[21:]
    m_ref, e_ref, f_ref, w_out, keep_out, give_out, cross, diag, inverse, block, m, acc, keep_ref, give_ref, w, load, save = refs
    me, core = place[0], place[1]
    rows, share = p1.shape
    sources = [x.at[:, pl.ds(pl.multiple_of(me * share, share), share)], p1, p2, p3]
    loads = [
        pltpu.make_async_copy(source, block.at[pl.ds(pl.multiple_of((me ^ s) * rows, rows), rows)], load.at[s])
        for s, source in enumerate(sources)
    ]
    part, half = rows // (2 * CORES), rows // CORES
    squares, places = [], []
    for c in range(CORES):
        for s in range(GROUP):
            source, seat, i = me ^ s, core ^ c, c * GROUP + s
            start = (source % 2) * (CORES * part) + seat * part
            target = cross.at[source // 2, pl.ds(pl.multiple_of(start, part), part)]
            places.append(pltpu.make_async_copy(crosses[i], target, load.at[GROUP + i]))
            target = diag.at[source, pl.ds(pl.multiple_of(seat * half, half), half)]
            squares.append(pltpu.make_async_copy(tails[i], target, load.at[3 * GROUP + i]))
    for copy in squares + places + loads:
        copy.start()
    for copy in squares:
        copy.wait()

    def ready():
        for copy in places:
            copy.wait()

    grams = [(diag[2 * j], cross.at[j], diag[2 * j + 1]) for j in range(GROUP // 2)]
    resolvent(grams, inverse, w, ready)
    for copy in loads:
        copy.wait()

    acc[...] = jnp.zeros_like(acc)
    saves = [pltpu.make_async_copy(w, w_out, save.at[share // tile + 4])]
    saves[0].start()
    for k in range(share // tile):
        here = slice(k * tile, (k + 1) * tile)
        m0 = merge_rows(block[: 2 * rows, here], w[0])
        m1 = merge_rows(block[2 * rows :, here], w[1])
        m[:rows, here] = m0
        m[rows:, here] = m1
        saves.append(pltpu.make_async_copy(m.at[:, here], m_ref.at[:, here], save.at[k]))
        saves[-1].start()
        acc[0] += dot(m0, m0, NT)
        acc[1] += dot(m0, m1, NT)
        acc[2] += dot(m1, m1, NT)
    start = raw
    for i, ref in enumerate((e_ref, f_ref)):
        source = m.at[:, start : start + ref.shape[1]]
        saves.append(pltpu.make_async_copy(source, ref, save.at[share // tile + i]))
        saves[-1].start()
        start += ref.shape[1]
    lower = lax.broadcasted_iota(jnp.int32, (rows, rows), 0) >= lax.broadcasted_iota(jnp.int32, (rows, rows), 1)
    row = jnp.sum(jnp.where(eye_mask(rows), acc[2], 0.0), axis=0, keepdims=True)
    acc[2] = jnp.where(lower, acc[0], acc[2])
    part = rows // (GROUP * CORES)
    for s in range(GROUP):
        to = me ^ s
        for ref, seat in ((give_ref, to * CORES + 1 - core), (keep_ref, to * CORES + core)):
            here = pl.ds(pl.multiple_of(seat * part, part), part)
            ref[s, :part] = acc[1, here, :]
            ref[s, part : 2 * part] = acc[2, here, :]
            ref[s, 2 * part :] = jnp.broadcast_to(row, (8, rows))
    for i, (source, target) in enumerate(((give_ref, give_out), (keep_ref, keep_out))):
        saves.append(pltpu.make_async_copy(source, target, save.at[share // tile + 2 + i]))
        saves[-1].start()
    for copy in saves:
        copy.wait()


def first(place, diagonals, crosses, x, pieces, raw, ahead, tile=512):
    rows, share = pieces[0].shape
    pairs = GROUP // 2
    out = shape(GROUP, 2 * rows // (GROUP * CORES) + 8, rows)
    return pl.pallas_call(
        functools.partial(first_kernel, raw, tile),
        out_shape=tuple(shape(pairs * rows, n, dtype=BF16) for n in (share, *ahead)) + (shape(pairs, rows, 2 * rows, dtype=BF16), out, out),
        in_specs=[SMEM] + [HBM] * (4 * GROUP + 4),
        out_specs=(ANY,) * 6,
        scratch_shapes=[
            pltpu.VMEM((pairs, rows, rows), F32),
            pltpu.VMEM((GROUP, rows, rows), F32),
            pltpu.VMEM((pairs, rows, rows), F32),
            pltpu.VMEM((GROUP * rows, share), BF16),
            pltpu.VMEM((pairs * rows, share), BF16),
            pltpu.VMEM((3, rows, rows), F32),
            pltpu.VMEM(out.shape, F32),
            pltpu.VMEM(out.shape, F32),
            pltpu.VMEM((pairs, rows, 2 * rows), BF16),
            pltpu.SemaphoreType.DMA((5 * GROUP,)),
            pltpu.SemaphoreType.DMA((share // tile + 5,)),
        ],
        cost_estimate=cost(2 * pairs * rows**3 * 40 + 14 * rows * rows * share, 12 * rows * share),
        compiler_params=WHOLE,
        name="first",
    )(place, *diagonals, *crosses, x, *pieces)


def second_kernel(*refs):
    place, bundles, m_ref, refs = refs[0], refs[1:9], refs[9], refs[10:]
    a_ref, b_ref, w_out, gram, inverse, m, w_ref, merged, load, save = refs
    me, core = place[0], place[1]
    rows = m.shape[0] // 2
    copy = pltpu.make_async_copy(m_ref.at[:, m_ref.shape[1] - m.shape[1] :], m, load)
    copy.start()
    part = rows // (GROUP * CORES)
    for c in range(CORES):
        for s in range(GROUP):
            seat = (me ^ s) * CORES + (core ^ c)
            for b in range(2):
                gram[b, pl.ds(pl.multiple_of(seat * part, part), part), :] = bundles[c * GROUP + s][b * part : (b + 1) * part]
    packed = gram[1]
    turned = packed.T
    lower = lax.broadcasted_iota(jnp.int32, (rows, rows), 0) >= lax.broadcasted_iota(jnp.int32, (rows, rows), 1)
    diagonal = jnp.broadcast_to(bundles[0][2 * part : 2 * part + 1], (rows, rows))
    upper_gram = jnp.where(eye_mask(rows), diagonal, jnp.where(lower, turned, packed))
    resolvent([(jnp.where(lower, packed, turned), gram.at[0], upper_gram)], inverse, w_ref)
    copy.wait()
    saves = [pltpu.make_async_copy(w_ref, w_out, save.at[2])]
    saves[0].start()
    half = a_ref.shape[1]
    for i, ref in enumerate((a_ref, b_ref)):
        here = slice(i * half, (i + 1) * half)
        merged[:, here] = merge_rows(m[:, here], w_ref[0])
        saves.append(pltpu.make_async_copy(merged.at[:, here], ref, save.at[i]))
        saves[-1].start()
    for save_copy in saves:
        save_copy.wait()


def second(place, bundles, m, early):
    rows, share = m.shape[0] // 2, m.shape[1]
    half = (share - early) // 2
    return pl.pallas_call(
        second_kernel,
        out_shape=(shape(rows, half, dtype=BF16),) * 2 + (shape(1, rows, 2 * rows, dtype=BF16),),
        in_specs=[SMEM] + [VMEM] * (2 * GROUP) + [ANY],
        out_specs=(ANY,) * 3,
        scratch_shapes=[
            pltpu.VMEM((2, rows, rows), F32),
            pltpu.VMEM((1, rows, rows), F32),
            pltpu.VMEM((2 * rows, 2 * half), BF16),
            pltpu.VMEM((1, rows, 2 * rows), BF16),
            pltpu.VMEM((rows, 2 * half), BF16),
            pltpu.SemaphoreType.DMA,
            pltpu.SemaphoreType.DMA((3,)),
        ],
        cost_estimate=cost(2 * rows**3 * 40 + 8 * rows * rows * half, 6 * rows * share),
        name="second",
    )(place, *bundles, m)


def raw_merge_kernel(share, place, w0, w1, x, xs, ys, d, _, out, block, pair, buffer, load, save):
    me = place[0]
    rows, raw = d.shape
    saves = []
    sources = {}
    for v in PEERS:
        mine = x.at[:, pl.ds(pl.multiple_of((me ^ v) * share, 128), raw)]
        across = {1: xs.at[GROUP - 1], 2: ys.at[GROUP - 1], 3: d}[v]
        sources[v] = (mine, xs.at[SHARES_X.index(v ^ 1)], ys.at[SHARES_Y.index(v ^ 2)], across)
    loads = {}
    for v, group in sources.items():
        for s, source in enumerate(group):
            target = block.at[v - 1, pl.ds(pl.multiple_of((me ^ s) * rows, rows), rows)]
            loads[v, s] = pltpu.make_async_copy(source, target, load.at[(v - 1) * GROUP + s])
            loads[v, s].start()
    for v in sources:
        for s in range(GROUP):
            loads[v, s].wait()
        for j in range(GROUP // 2):
            pair[j * rows : (j + 1) * rows] = merge_rows(block[v - 1, 2 * j * rows : 2 * (j + 1) * rows], w0[j])
        buffer[v - 1] = merge_rows(pair[...], w1[0])
        target = out.at[:, pl.ds(pl.multiple_of((me ^ v) * share, 128), raw)]
        saves.append(pltpu.make_async_copy(buffer.at[v - 1], target, save.at[v - 1]))
        saves[-1].start()
    for copy in saves:
        copy.wait()


def raw_merge(place, w0, w1, x, messages, out, share):
    rows, raw = messages[2].shape
    return pl.pallas_call(
        functools.partial(raw_merge_kernel, share),
        out_shape=shape(*out.shape, dtype=BF16),
        in_specs=[SMEM, VMEM, VMEM] + [HBM] * 5,
        out_specs=HBM,
        scratch_shapes=[
            pltpu.VMEM((GROUP - 1, GROUP * rows, raw), BF16),
            pltpu.VMEM((2 * rows, raw), BF16),
            pltpu.VMEM((GROUP - 1, rows, raw), BF16),
            pltpu.SemaphoreType.DMA(((GROUP - 1) * GROUP,)),
            pltpu.SemaphoreType.DMA((GROUP - 1,)),
        ],
        input_output_aliases={7: 0},
        cost_estimate=cost(12 * rows * rows * raw * (GROUP - 1), 10 * rows * raw * (GROUP - 1)),
        compiler_params=WHOLE,
        name="raw_merge",
    )(place, w0, w1, x, *messages, out)


def late_kernel(share, raw, place, w, a, b, m, *refs):
    early, (out, mine, own, buffer, load, save) = refs[:-6], refs[-6:]
    me, size, half = place[0], mine.shape[1], a.shape[1]
    copy = pltpu.make_async_copy(m.at[:, :size], mine, load)
    copy.start()
    saves = []

    def put(source, owner, column):
        target = out.at[:, pl.ds(pl.multiple_of(owner * share + column, 128), source.shape[1])]
        saves.append(pltpu.make_async_copy(source, target, save.at[len(saves)]))
        saves[-1].start()

    put(a, me, size)
    put(b, me, size + half)
    work = [(pair, s, raw) for pair, s in zip(early, PEERS)]
    work += [(pair, s, raw + early[0].shape[1]) for pair, s in zip(early[len(PEERS) :], PEERS)]
    for pair, s, column in work:
        spot = buffer.at[s - 1, :, column - raw : column - raw + pair.shape[1]]
        spot[...] = merge_rows(pair[...], w[0])
        put(spot, me ^ s, column)
    copy.wait()
    own[...] = merge_rows(mine[...], w[0])
    put(own, me, 0)
    for copy in saves:
        copy.wait()


def late(place, w, a, b, m, pairs, raw, share):
    rows, size = a.shape[0], share - 2 * a.shape[1]
    return pl.pallas_call(
        functools.partial(late_kernel, share, raw),
        out_shape=shape(rows, GROUP * share, dtype=BF16),
        in_specs=[SMEM] + [VMEM] * 3 + [HBM] + [VMEM] * len(pairs),
        out_specs=HBM,
        scratch_shapes=[
            pltpu.VMEM((2 * rows, size), BF16),
            pltpu.VMEM((rows, size), BF16),
            pltpu.VMEM((GROUP - 1, rows, size - raw), BF16),
            pltpu.SemaphoreType.DMA,
            pltpu.SemaphoreType.DMA((len(pairs) + 3,)),
        ],
        cost_estimate=cost(4 * rows * rows * size * GROUP, 6 * rows * size * GROUP),
        name="late",
    )(place, w, a, b, m, *pairs)


def put_kernel(spots, share, place, *refs):
    count = len(spots)
    blocks, out, buffers, load, save = refs[:count], refs[count + 1], refs[count + 2 : -2], refs[-2], refs[-1]
    loads, saves = [], []
    for i, ((s, column), block, buffer) in enumerate(zip(spots, blocks, buffers)):
        start = pl.multiple_of((place[0] ^ s) * share + column, 128)
        loads.append(pltpu.make_async_copy(block, buffer, load.at[i]))
        loads[-1].start()
        saves.append(pltpu.make_async_copy(buffer, out.at[:, pl.ds(start, block.shape[1])], save.at[i]))
    for load_copy, save_copy in zip(loads, saves):
        load_copy.wait()
        save_copy.start()
    for copy in saves:
        copy.wait()


def put(place, out, blocks, spots, share):
    size = sum(b.size for b in blocks)
    return pl.pallas_call(
        functools.partial(put_kernel, spots, share),
        out_shape=shape(*out.shape, dtype=out.dtype),
        in_specs=[SMEM] + [HBM] * (len(blocks) + 1),
        out_specs=HBM,
        scratch_shapes=[pltpu.VMEM(b.shape, b.dtype) for b in blocks] + [pltpu.SemaphoreType.DMA((len(blocks),))] * 2,
        input_output_aliases={1 + len(blocks): 0},
        cost_estimate=cost(0, 4 * size),
        compiler_params=WHOLE,
        name="put",
    )(place, *blocks, out)


def over_chips(block):
    chips = lax.axis_size("feat") // CORES
    return total([block] + [send(block, "feat", CORES * s) for s in range(1, chips)])


def gather_group(bundle):
    mine = [bundle] + send_all([bundle] * len(PEERS), "dp", PEERS)
    return mine + [send(b, "feat", 1) for b in mine]


def run(sketches):
    x = sketches[0]
    rows, columns = x.shape
    share = columns // GROUP
    raw, ahead = 3 * share // 16, (3 * share // 16, share // 8)
    early = raw + sum(ahead)
    me = lax.axis_index("dp") % GROUP
    place = jnp.stack([me, lax.axis_index("feat") % CORES]).astype(jnp.int32)

    cuts, source = {}, x
    for s in PEERS:
        cuts[s] = lax.dynamic_slice(source, (0, (me ^ s) * share), (rows, share))
        if s == 2:
            source, cuts = lax.optimization_barrier((source, cuts))
    pieces = {s: send(cut, "dp", s) for s, cut in cuts.items()}
    keep, give = own_gram(place, x)
    own = over_chips(total([keep, send(give, "feat", 1)]))
    near, to_x, to_y, to_d = near_gram(place, x, pieces[1], raw)
    p2, p3, own, near = lax.optimization_barrier((pieces[2], pieces[3], own, near))

    keep, give, to_x = far_gram(place, near, p2, p3, to_x)
    parts = fold(keep, send(give, "feat", 1))
    parts, own, to_d = lax.optimization_barrier((parts, own, to_d))
    mine = total([parts[0]] + send_all(parts[1:], "dp", PEERS))
    diagonals = gather_group(own)
    from_d = send(to_d, "dp", 3)
    bundle = over_chips(mine)
    bundle, to_x, to_y = lax.optimization_barrier((bundle, to_x, to_y))
    crosses = gather_group(bundle)
    messages = [send(to_x, "dp", 1), send(to_y, "dp", 2), from_d]
    m, e, f, w0, keep, give = first(place, diagonals, crosses, x, [pieces[1], p2, p3], raw, ahead)

    parts = fold(keep, send(give, "feat", 1))
    parts, e, f = lax.optimization_barrier((parts, e, f))
    mine = total([parts[0]] + send_all(parts[1:], "dp", PEERS))
    pairs_a, pairs_b = [[send(block, "dp", s) for s in (1, 2)] for block in (e, f)]
    bundles = gather_group(over_chips(mine))
    pairs = pairs_a + [send(pairs_a[0], "dp", 2)] + pairs_b + [send(pairs_b[1], "dp", 1)]
    a, b, w1 = second(place, bundles, m, early)

    ax, by = send(a, "dp", 1), send(b, "dp", 2)
    bx, ay = send(b, "dp", 1), send(a, "dp", 2)
    ad, bd = send(ax, "dp", 2), send(by, "dp", 1)
    left, right = early, early + a.shape[1]
    out = late(place, w1, a, b, m, pairs, raw, share)
    out = raw_merge(place, w0, w1, x, messages, out, share)
    out = put(place, out, [ax, by, bx, ay], ((1, left), (2, right), (1, right), (2, left)), share)
    out = put(place, out, [ad, bd], ((3, left), (3, right)), share)
    return out[None]


def solution(mesh):
    spec = P("dp", None, "feat")
    return jax.shard_map(run, mesh=mesh, in_specs=(spec,), out_specs=spec, check_vma=False)
```

```python
import functools

import jax
import jax.numpy as jnp
from jax import lax
from jax.experimental import pallas as pl
from jax.experimental.pallas import tpu as pltpu
from jax.sharding import PartitionSpec as P


LEVELS = 2
GROUP = 2**LEVELS
CORES = 2
PEERS = tuple(range(1, GROUP))
F32, BF16 = jnp.float32, jnp.bfloat16
NT = (((1,), (1,)), ((), ()))
NN = (((1,), (0,)), ((), ()))
VMEM = pl.BlockSpec(memory_space=pltpu.VMEM)
SMEM = pl.BlockSpec(memory_space=pltpu.SMEM)
ANY = pl.BlockSpec(memory_space=pl.ANY)
HBM = pl.BlockSpec(memory_space=pltpu.HBM)


def send(block, axis, shift):
    count = lax.axis_size(axis)
    return lax.ppermute(block, axis, [(i, i ^ shift) for i in range(count)])


def send_all(blocks, axis, shifts):
    return [send(b, axis, s) for b, s in zip(blocks, shifts)]


def dot(a, b, dims=NN):
    return lax.dot_general(a, b, dims, preferred_element_type=F32)


def shape(*dims, dtype=F32):
    return jax.ShapeDtypeStruct(dims, dtype)


WHOLE = pltpu.CompilerParams(vmem_limit_bytes=67_043_328)


def cost(flops, nbytes):
    return pl.CostEstimate(flops=int(flops), bytes_accessed=int(nbytes), transcendentals=0)


def halves(a):
    high = a.astype(BF16)
    return high, (a - high.astype(F32)).astype(BF16)


def product(a, b, dims=NN):
    (ah, al), (bh, bl) = a, b
    return dot(ah, bh, dims) + (dot(ah, bl, dims) + dot(al, bh, dims))


def eye_mask(n):
    return lax.broadcasted_iota(jnp.int32, (n, n), 0) == lax.broadcasted_iota(jnp.int32, (n, n), 1)


def invert(kernels, x_ref, limit):
    n = kernels[0].shape[0]
    mask = eye_mask(n)
    eye = jnp.where(mask, 1.0, 0.0)
    parts = [halves(k) for k in kernels]
    spreads = []
    for j, k in enumerate(kernels):
        diag = jnp.where(mask, k, 0.0)
        row = 1.0 / jnp.sum(diag, axis=0, keepdims=True)
        col = 1.0 / jnp.sum(diag, axis=1, keepdims=True)
        scaled = jnp.where(mask, 0.0, k) * row
        spreads.append(jnp.sum(scaled * (jnp.where(mask, 0.0, k) * col)))
        x_ref[j] = jnp.where(mask, row, -scaled * col)

    def step(update=lambda xs, rest: dot(xs[0], rest.astype(BF16))):
        worst = jnp.float32(0.0)
        for j, part in enumerate(parts):
            x = x_ref[j]
            xs = halves(x)
            rest = eye - product(part, xs)
            worst = jnp.maximum(worst, jnp.sum(rest * rest))
            x_ref[j] = x + update(xs, rest)
        return worst

    step()
    worst = step()
    wide = functools.reduce(jnp.maximum, spreads) >= 0.9

    def more(state):
        count, _ = state
        for j, k in enumerate(kernels):

            @pl.when((count == 0) & (spreads[j] >= 0.9))
            def _():
                bound = jnp.minimum(jnp.max(jnp.sum(jnp.abs(k), axis=0, keepdims=True)), limit)
                x_ref[j] = eye * (2.0 / (1.0 + bound))

        return count + 1, step(lambda xs, rest: product(xs, halves(rest)))

    lax.while_loop(lambda s: (s[0] < 24) & ((s[1] > 1e-6) | ((s[0] == 0) & wide)), more, (jnp.int32(0), worst))


def resolvent(grams, x_ref, out_ref):
    n = grams[0][0].shape[0]
    mask = eye_mask(n)
    eye = jnp.where(mask, 1.0, 0.0)
    scaled = []
    for a, b, d in grams:
        scale = (2 * n) / jnp.sum(jnp.where(mask, a + d, 0.0))
        scaled.append((eye + a * scale, b * scale, eye + d * scale))
    limit = 1.0 + 2 * n
    invert([d for _, _, d in scaled], x_ref, limit)
    ties, schurs = [], []
    for j, (a, b, d) in enumerate(scaled):
        bs = halves(b)
        tie = halves(product(bs, halves(x_ref[j])))
        ties.append(tie)
        schurs.append(a - product(tie, bs, NT))
    invert(schurs, x_ref, limit)
    for j, tie in enumerate(ties):
        x = x_ref[j]
        out_ref[j, :, :n] = x.astype(BF16)
        out_ref[j, :, n:] = (-product(halves(x), tie)).astype(BF16)


def own_gram_kernel(place, x_ref, keep_ref, give_ref, acc):
    step = pl.program_id(0)
    core = place[1]
    half = keep_ref.shape[0]

    @pl.when(step == 0)
    def _():
        acc[...] = jnp.zeros_like(acc)

    acc[...] += dot(x_ref[...], x_ref[...], NT)

    @pl.when(step == pl.num_programs(0) - 1)
    def _():
        keep_ref[...] = acc[pl.ds(pl.multiple_of(core * half, half), half), :]
        give_ref[...] = acc[pl.ds(pl.multiple_of((1 - core) * half, half), half), :]


def own_gram(place, x, tile=2048):
    rows, columns = x.shape
    half = shape(rows // CORES, rows)
    spec = pl.BlockSpec((rows // CORES, rows), lambda k, place: (0, 0))
    return pl.pallas_call(
        own_gram_kernel,
        out_shape=(half, half),
        grid_spec=pltpu.PrefetchScalarGridSpec(
            num_scalar_prefetch=1,
            grid=(columns // tile,),
            in_specs=[pl.BlockSpec((rows, tile), lambda k, place: (0, k))],
            out_specs=(spec, spec),
            scratch_shapes=[pltpu.VMEM((rows, rows), F32)],
        ),
        cost_estimate=cost(2 * rows * rows * columns, 2 * rows * columns),
        name="own_gram",
    )(place, x)


def pair_gram(me, sources, block, load, chunk):
    rows, share = block.shape[1:]
    copies = []
    for k in range(share // chunk):
        here = slice(k * chunk, (k + 1) * chunk)
        for i, (s, source) in enumerate(sources):
            target = block.at[(me ^ s) % 2, :, here]
            copies.append(pltpu.make_async_copy(source(k * chunk, chunk), target, load.at[2 * k + i]))
            copies[-1].start()
    value = jnp.zeros((rows, rows), F32)
    for k in range(share // chunk):
        copies[2 * k].wait()
        copies[2 * k + 1].wait()
        here = slice(k * chunk, (k + 1) * chunk)
        value = value + dot(block[0, :, here], block[1, :, here], NT)
    return value


SHARES_X, SHARES_Y = (0, 2, 3), (0, 1, 3)


def near_gram_kernel(chunk, place, x, p1, out_ref, x_ref, y_ref, d_ref, block, pack, load, save):
    me = place[0]
    share, raw = p1.shape[1], d_ref.shape[1]

    def mine(column, size, t=0):
        return x.at[:, pl.ds(pl.multiple_of((me ^ t) * share + column, 128), size)]

    def theirs(column, size):
        return p1.at[:, column : column + size]

    packs = [pltpu.make_async_copy(mine(0, raw, t), pack.at[t], save.at[t]) for t in range(GROUP)]
    packs.append(pltpu.make_async_copy(theirs(0, raw), pack.at[GROUP], save.at[GROUP]))
    for copy in packs:
        copy.start()
    out_ref[...] = pair_gram(me, ((0, mine), (1, theirs)), block, load, chunk)
    for copy in packs:
        copy.wait()
    targets = [(t, x_ref.at[i]) for i, t in enumerate(SHARES_X)] + [(t, y_ref.at[i]) for i, t in enumerate(SHARES_Y)]
    targets += [(GROUP, y_ref.at[GROUP - 1]), (0, d_ref)]
    copies = [pltpu.make_async_copy(pack.at[t], target, save.at[i]) for i, (t, target) in enumerate(targets)]
    for copy in copies:
        copy.start()
    for copy in copies:
        copy.wait()


def near_gram(place, x, p1, raw, chunk=512):
    rows, share = p1.shape
    message = shape(GROUP, rows, raw, dtype=BF16)
    return pl.pallas_call(
        functools.partial(near_gram_kernel, chunk),
        out_shape=(shape(rows, rows), message, message, shape(rows, raw, dtype=BF16)),
        in_specs=[SMEM, HBM, HBM],
        out_specs=(VMEM, HBM, HBM, HBM),
        scratch_shapes=[
            pltpu.VMEM((2, rows, share), BF16),
            pltpu.VMEM((GROUP + 1, rows, raw), BF16),
            pltpu.SemaphoreType.DMA((2 * share // chunk,)),
            pltpu.SemaphoreType.DMA((2 * GROUP,)),
        ],
        cost_estimate=cost(2 * rows * rows * share, 4 * rows * share),
        compiler_params=WHOLE,
        name="near_gram",
    )(place, x, p1)


def far_gram_kernel(chunk, place, near, p2, p3, _, keep_out, give_out, x_ref, block, acc, keep_ref, give_ref, load, save):
    me, core = place[0], place[1]
    first_load = pltpu.make_async_copy(near, acc.at[me // 2], save.at[3])
    first_load.start()
    sources = tuple((s, lambda column, size, p=p: p.at[:, column : column + size]) for s, p in ((2, p2), (3, p3)))
    acc[1 - me // 2] = pair_gram(me, sources, block, load, chunk)
    copies = [pltpu.make_async_copy(block.at[(me ^ 2) % 2, :, : x_ref.shape[2]], x_ref.at[GROUP - 1], save.at[0])]
    copies[0].start()
    first_load.wait()
    part = keep_ref.shape[1]
    for s in range(GROUP):
        to = me ^ s
        pair, start = to // 2, (to % 2) * (CORES * part)
        keep_ref[s] = acc[pair, pl.ds(pl.multiple_of(start + core * part, part), part), :]
        give_ref[s] = acc[pair, pl.ds(pl.multiple_of(start + (1 - core) * part, part), part), :]
    for i, (source, target) in enumerate(((give_ref, give_out), (keep_ref, keep_out))):
        copies.append(pltpu.make_async_copy(source, target, save.at[1 + i]))
        copies[-1].start()
    for copy in copies:
        copy.wait()


def far_gram(place, near, p2, p3, message, chunk=512):
    rows, share = p2.shape
    out = shape(GROUP, rows // (2 * CORES), rows)
    return pl.pallas_call(
        functools.partial(far_gram_kernel, chunk),
        out_shape=(out, out, shape(*message.shape, dtype=BF16)),
        in_specs=[SMEM, HBM, HBM, HBM, HBM],
        out_specs=(HBM, HBM, HBM),
        scratch_shapes=[
            pltpu.VMEM((2, rows, share), BF16),
            pltpu.VMEM((GROUP // 2, rows, rows), F32),
            pltpu.VMEM(out.shape, F32),
            pltpu.VMEM(out.shape, F32),
            pltpu.SemaphoreType.DMA((2 * share // chunk,)),
            pltpu.SemaphoreType.DMA((4,)),
        ],
        input_output_aliases={4: 2},
        cost_estimate=cost(2 * rows * rows * share, 4 * rows * share),
        compiler_params=WHOLE,
        name="far_gram",
    )(place, near, p2, p3, message)


def fold(mine, theirs):
    return [mine[s] + theirs[s] for s in range(mine.shape[0])]


def total(arrays):
    return functools.reduce(jnp.add, arrays)


def merge_rows(stacked, w):
    lower = stacked[: w.shape[0]]
    return (lower.astype(F32) - dot(w, stacked)).astype(BF16)


def first_kernel(raw, tile, *refs):
    place, tails, crosses, (x, p1, p2, p3), refs = refs[0], refs[1:9], refs[9:17], refs[17:21], refs[21:]
    m_ref, e_ref, f_ref, w_out, keep_out, give_out, cross, diag, inverse, block, m, acc, keep_ref, give_ref, w, load, save = refs
    me, core = place[0], place[1]
    rows, share = p1.shape
    sources = [x.at[:, pl.ds(pl.multiple_of(me * share, share), share)], p1, p2, p3]
    loads = [
        pltpu.make_async_copy(source, block.at[pl.ds(pl.multiple_of((me ^ s) * rows, rows), rows)], load.at[s])
        for s, source in enumerate(sources)
    ]
    for copy in loads:
        copy.start()

    part, half = rows // (2 * CORES), rows // CORES
    for c in range(CORES):
        for s in range(GROUP):
            source, seat = me ^ s, core ^ c
            start = (source % 2) * (CORES * part) + seat * part
            cross[source // 2, pl.ds(pl.multiple_of(start, part), part), :] = crosses[c * GROUP + s][...]
            diag[source, pl.ds(pl.multiple_of(seat * half, half), half), :] = tails[c * GROUP + s][...]
    grams = [(diag[2 * j], cross[j], diag[2 * j + 1]) for j in range(GROUP // 2)]
    resolvent(grams, inverse, w)
    for copy in loads:
        copy.wait()

    acc[...] = jnp.zeros_like(acc)
    saves = [pltpu.make_async_copy(w, w_out, save.at[share // tile + 4])]
    saves[0].start()
    for k in range(share // tile):
        here = slice(k * tile, (k + 1) * tile)
        m0 = merge_rows(block[: 2 * rows, here], w[0])
        m1 = merge_rows(block[2 * rows :, here], w[1])
        m[:rows, here] = m0
        m[rows:, here] = m1
        saves.append(pltpu.make_async_copy(m.at[:, here], m_ref.at[:, here], save.at[k]))
        saves[-1].start()
        acc[0] += dot(m0, m0, NT)
        acc[1] += dot(m0, m1, NT)
        acc[2] += dot(m1, m1, NT)
    start = raw
    for i, ref in enumerate((e_ref, f_ref)):
        source = m.at[:, start : start + ref.shape[1]]
        saves.append(pltpu.make_async_copy(source, ref, save.at[share // tile + i]))
        saves[-1].start()
        start += ref.shape[1]
    lower = lax.broadcasted_iota(jnp.int32, (rows, rows), 0) >= lax.broadcasted_iota(jnp.int32, (rows, rows), 1)
    row = jnp.sum(jnp.where(eye_mask(rows), acc[2], 0.0), axis=0, keepdims=True)
    acc[2] = jnp.where(lower, acc[0], acc[2])
    part = rows // (GROUP * CORES)
    for s in range(GROUP):
        to = me ^ s
        for ref, seat in ((give_ref, to * CORES + 1 - core), (keep_ref, to * CORES + core)):
            here = pl.ds(pl.multiple_of(seat * part, part), part)
            ref[s, :part] = acc[1, here, :]
            ref[s, part : 2 * part] = acc[2, here, :]
            ref[s, 2 * part :] = jnp.broadcast_to(row, (8, rows))
    for i, (source, target) in enumerate(((give_ref, give_out), (keep_ref, keep_out))):
        saves.append(pltpu.make_async_copy(source, target, save.at[share // tile + 2 + i]))
        saves[-1].start()
    for copy in saves:
        copy.wait()


def first(place, diagonals, crosses, x, pieces, raw, ahead, tile=512):
    rows, share = pieces[0].shape
    pairs = GROUP // 2
    out = shape(GROUP, 2 * rows // (GROUP * CORES) + 8, rows)
    return pl.pallas_call(
        functools.partial(first_kernel, raw, tile),
        out_shape=tuple(shape(pairs * rows, n, dtype=BF16) for n in (share, *ahead)) + (shape(pairs, rows, 2 * rows, dtype=BF16), out, out),
        in_specs=[SMEM] + [VMEM] * (4 * GROUP) + [HBM] * 4,
        out_specs=(ANY,) * 6,
        scratch_shapes=[
            pltpu.VMEM((pairs, rows, rows), F32),
            pltpu.VMEM((GROUP, rows, rows), F32),
            pltpu.VMEM((pairs, rows, rows), F32),
            pltpu.VMEM((GROUP * rows, share), BF16),
            pltpu.VMEM((pairs * rows, share), BF16),
            pltpu.VMEM((3, rows, rows), F32),
            pltpu.VMEM(out.shape, F32),
            pltpu.VMEM(out.shape, F32),
            pltpu.VMEM((pairs, rows, 2 * rows), BF16),
            pltpu.SemaphoreType.DMA((GROUP,)),
            pltpu.SemaphoreType.DMA((share // tile + 5,)),
        ],
        cost_estimate=cost(2 * pairs * rows**3 * 40 + 14 * rows * rows * share, 12 * rows * share),
        name="first",
    )(place, *diagonals, *crosses, x, *pieces)


def second_kernel(*refs):
    place, bundles, m_ref, refs = refs[0], refs[1:9], refs[9], refs[10:]
    a_ref, b_ref, w_out, gram, inverse, m, w_ref, merged, load, save = refs
    me, core = place[0], place[1]
    rows = m.shape[0] // 2
    copy = pltpu.make_async_copy(m_ref.at[:, m_ref.shape[1] - m.shape[1] :], m, load)
    copy.start()
    part = rows // (GROUP * CORES)
    for c in range(CORES):
        for s in range(GROUP):
            seat = (me ^ s) * CORES + (core ^ c)
            for b in range(2):
                gram[b, pl.ds(pl.multiple_of(seat * part, part), part), :] = bundles[c * GROUP + s][b * part : (b + 1) * part]
    packed = gram[1]
    turned = packed.T
    lower = lax.broadcasted_iota(jnp.int32, (rows, rows), 0) >= lax.broadcasted_iota(jnp.int32, (rows, rows), 1)
    diagonal = jnp.broadcast_to(bundles[0][2 * part : 2 * part + 1], (rows, rows))
    upper_gram = jnp.where(eye_mask(rows), diagonal, jnp.where(lower, turned, packed))
    resolvent([(jnp.where(lower, packed, turned), gram[0], upper_gram)], inverse, w_ref)
    copy.wait()
    saves = [pltpu.make_async_copy(w_ref, w_out, save.at[2])]
    saves[0].start()
    half = a_ref.shape[1]
    for i, ref in enumerate((a_ref, b_ref)):
        here = slice(i * half, (i + 1) * half)
        merged[:, here] = merge_rows(m[:, here], w_ref[0])
        saves.append(pltpu.make_async_copy(merged.at[:, here], ref, save.at[i]))
        saves[-1].start()
    for save_copy in saves:
        save_copy.wait()


def second(place, bundles, m, early):
    rows, share = m.shape[0] // 2, m.shape[1]
    half = (share - early) // 2
    return pl.pallas_call(
        second_kernel,
        out_shape=(shape(rows, half, dtype=BF16),) * 2 + (shape(1, rows, 2 * rows, dtype=BF16),),
        in_specs=[SMEM] + [VMEM] * (2 * GROUP) + [ANY],
        out_specs=(ANY,) * 3,
        scratch_shapes=[
            pltpu.VMEM((2, rows, rows), F32),
            pltpu.VMEM((1, rows, rows), F32),
            pltpu.VMEM((2 * rows, 2 * half), BF16),
            pltpu.VMEM((1, rows, 2 * rows), BF16),
            pltpu.VMEM((rows, 2 * half), BF16),
            pltpu.SemaphoreType.DMA,
            pltpu.SemaphoreType.DMA((3,)),
        ],
        cost_estimate=cost(2 * rows**3 * 40 + 8 * rows * rows * half, 6 * rows * share),
        name="second",
    )(place, *bundles, m)


def raw_merge_kernel(share, place, w0, w1, x, xs, ys, d, _, out, block, pair, buffer, load, save):
    me = place[0]
    rows, raw = d.shape
    saves = []
    sources = {}
    for v in PEERS:
        mine = x.at[:, pl.ds(pl.multiple_of((me ^ v) * share, 128), raw)]
        across = {1: xs.at[GROUP - 1], 2: ys.at[GROUP - 1], 3: d}[v]
        sources[v] = (mine, xs.at[SHARES_X.index(v ^ 1)], ys.at[SHARES_Y.index(v ^ 2)], across)
    loads = {}
    for v, group in sources.items():
        for s, source in enumerate(group):
            target = block.at[v - 1, pl.ds(pl.multiple_of((me ^ s) * rows, rows), rows)]
            loads[v, s] = pltpu.make_async_copy(source, target, load.at[(v - 1) * GROUP + s])
            loads[v, s].start()
    for v in sources:
        for s in range(GROUP):
            loads[v, s].wait()
        for j in range(GROUP // 2):
            pair[j * rows : (j + 1) * rows] = merge_rows(block[v - 1, 2 * j * rows : 2 * (j + 1) * rows], w0[j])
        buffer[v - 1] = merge_rows(pair[...], w1[0])
        target = out.at[:, pl.ds(pl.multiple_of((me ^ v) * share, 128), raw)]
        saves.append(pltpu.make_async_copy(buffer.at[v - 1], target, save.at[v - 1]))
        saves[-1].start()
    for copy in saves:
        copy.wait()


def raw_merge(place, w0, w1, x, messages, out, share):
    rows, raw = messages[2].shape
    return pl.pallas_call(
        functools.partial(raw_merge_kernel, share),
        out_shape=shape(*out.shape, dtype=BF16),
        in_specs=[SMEM, VMEM, VMEM] + [HBM] * 5,
        out_specs=HBM,
        scratch_shapes=[
            pltpu.VMEM((GROUP - 1, GROUP * rows, raw), BF16),
            pltpu.VMEM((2 * rows, raw), BF16),
            pltpu.VMEM((GROUP - 1, rows, raw), BF16),
            pltpu.SemaphoreType.DMA(((GROUP - 1) * GROUP,)),
            pltpu.SemaphoreType.DMA((GROUP - 1,)),
        ],
        input_output_aliases={7: 0},
        cost_estimate=cost(12 * rows * rows * raw * (GROUP - 1), 10 * rows * raw * (GROUP - 1)),
        compiler_params=WHOLE,
        name="raw_merge",
    )(place, w0, w1, x, *messages, out)


def late_kernel(share, raw, place, w, a, b, m, *refs):
    early, (out, mine, own, buffer, load, save) = refs[:-6], refs[-6:]
    me, size, half = place[0], mine.shape[1], a.shape[1]
    copy = pltpu.make_async_copy(m.at[:, :size], mine, load)
    copy.start()
    saves = []

    def put(source, owner, column):
        target = out.at[:, pl.ds(pl.multiple_of(owner * share + column, 128), source.shape[1])]
        saves.append(pltpu.make_async_copy(source, target, save.at[len(saves)]))
        saves[-1].start()

    put(a, me, size)
    put(b, me, size + half)
    work = [(pair, s, raw) for pair, s in zip(early, PEERS)]
    work += [(pair, s, raw + early[0].shape[1]) for pair, s in zip(early[len(PEERS) :], PEERS)]
    for pair, s, column in work:
        spot = buffer.at[s - 1, :, column - raw : column - raw + pair.shape[1]]
        spot[...] = merge_rows(pair[...], w[0])
        put(spot, me ^ s, column)
    copy.wait()
    own[...] = merge_rows(mine[...], w[0])
    put(own, me, 0)
    for copy in saves:
        copy.wait()


def late(place, w, a, b, m, pairs, raw, share):
    rows, size = a.shape[0], share - 2 * a.shape[1]
    return pl.pallas_call(
        functools.partial(late_kernel, share, raw),
        out_shape=shape(rows, GROUP * share, dtype=BF16),
        in_specs=[SMEM] + [VMEM] * 3 + [HBM] + [VMEM] * len(pairs),
        out_specs=HBM,
        scratch_shapes=[
            pltpu.VMEM((2 * rows, size), BF16),
            pltpu.VMEM((rows, size), BF16),
            pltpu.VMEM((GROUP - 1, rows, size - raw), BF16),
            pltpu.SemaphoreType.DMA,
            pltpu.SemaphoreType.DMA((len(pairs) + 3,)),
        ],
        cost_estimate=cost(4 * rows * rows * size * GROUP, 6 * rows * size * GROUP),
        name="late",
    )(place, w, a, b, m, *pairs)


def put_kernel(spots, share, place, *refs):
    count = len(spots)
    blocks, out, buffers, load, save = refs[:count], refs[count + 1], refs[count + 2 : -2], refs[-2], refs[-1]
    loads, saves = [], []
    for i, ((s, column), block, buffer) in enumerate(zip(spots, blocks, buffers)):
        start = pl.multiple_of((place[0] ^ s) * share + column, 128)
        loads.append(pltpu.make_async_copy(block, buffer, load.at[i]))
        loads[-1].start()
        saves.append(pltpu.make_async_copy(buffer, out.at[:, pl.ds(start, block.shape[1])], save.at[i]))
    for load_copy, save_copy in zip(loads, saves):
        load_copy.wait()
        save_copy.start()
    for copy in saves:
        copy.wait()


def put(place, out, blocks, spots, share):
    size = sum(b.size for b in blocks)
    return pl.pallas_call(
        functools.partial(put_kernel, spots, share),
        out_shape=shape(*out.shape, dtype=out.dtype),
        in_specs=[SMEM] + [HBM] * (len(blocks) + 1),
        out_specs=HBM,
        scratch_shapes=[pltpu.VMEM(b.shape, b.dtype) for b in blocks] + [pltpu.SemaphoreType.DMA((len(blocks),))] * 2,
        input_output_aliases={1 + len(blocks): 0},
        cost_estimate=cost(0, 4 * size),
        compiler_params=WHOLE,
        name="put",
    )(place, *blocks, out)


def over_chips(block):
    chips = lax.axis_size("feat") // CORES
    return total([block] + [send(block, "feat", CORES * s) for s in range(1, chips)])


def gather_group(bundle):
    mine = [bundle] + send_all([bundle] * len(PEERS), "dp", PEERS)
    return mine + [send(b, "feat", 1) for b in mine]


def run(sketches):
    x = sketches[0]
    rows, columns = x.shape
    share = columns // GROUP
    raw, ahead = 3 * share // 16, (3 * share // 16, share // 8)
    early = raw + sum(ahead)
    me = lax.axis_index("dp") % GROUP
    place = jnp.stack([me, lax.axis_index("feat") % CORES]).astype(jnp.int32)

    cuts, source = {}, x
    for s in PEERS:
        cuts[s] = lax.dynamic_slice(source, (0, (me ^ s) * share), (rows, share))
        if s == 2:
            source, cuts = lax.optimization_barrier((source, cuts))
    pieces = {s: send(cut, "dp", s) for s, cut in cuts.items()}
    keep, give = own_gram(place, x)
    own = over_chips(total([keep, send(give, "feat", 1)]))
    near, to_x, to_y, to_d = near_gram(place, x, pieces[1], raw)
    p2, p3, own, near = lax.optimization_barrier((pieces[2], pieces[3], own, near))

    keep, give, to_x = far_gram(place, near, p2, p3, to_x)
    parts = fold(keep, send(give, "feat", 1))
    parts, own, to_d = lax.optimization_barrier((parts, own, to_d))
    mine = total([parts[0]] + send_all(parts[1:], "dp", PEERS))
    diagonals = gather_group(own)
    from_d = send(to_d, "dp", 3)
    bundle = over_chips(mine)
    bundle, to_x, to_y = lax.optimization_barrier((bundle, to_x, to_y))
    crosses = gather_group(bundle)
    messages = [send(to_x, "dp", 1), send(to_y, "dp", 2), from_d]
    m, e, f, w0, keep, give = first(place, diagonals, crosses, x, [pieces[1], p2, p3], raw, ahead)

    parts = fold(keep, send(give, "feat", 1))
    parts, e, f = lax.optimization_barrier((parts, e, f))
    mine = total([parts[0]] + send_all(parts[1:], "dp", PEERS))
    pairs_a, pairs_b = [[send(block, "dp", s) for s in (1, 2)] for block in (e, f)]
    bundles = gather_group(over_chips(mine))
    pairs = pairs_a + [send(pairs_a[0], "dp", 2)] + pairs_b + [send(pairs_b[1], "dp", 1)]
    a, b, w1 = second(place, bundles, m, early)

    ax, by = send(a, "dp", 1), send(b, "dp", 2)
    bx, ay = send(b, "dp", 1), send(a, "dp", 2)
    ad, bd = send(ax, "dp", 2), send(by, "dp", 1)
    left, right = early, early + a.shape[1]
    out = late(place, w1, a, b, m, pairs, raw, share)
    out = raw_merge(place, w0, w1, x, messages, out, share)
    out = put(place, out, [ax, by, bx, ay], ((1, left), (2, right), (1, right), (2, left)), share)
    out = put(place, out, [ad, bd], ((3, left), (3, right)), share)
    return out[None]


def solution(mesh):
    spec = P("dp", None, "feat")
    return jax.shard_map(run, mesh=mesh, in_specs=(spec,), out_specs=spec, check_vma=False)
```

```python
import functools

import jax
import jax.numpy as jnp
from jax import lax
from jax.experimental import pallas as pl
from jax.experimental.pallas import tpu as pltpu
from jax.sharding import PartitionSpec as P


LEVELS = 2
GROUP = 2**LEVELS
CORES = 2
PEERS = tuple(range(1, GROUP))
F32, BF16 = jnp.float32, jnp.bfloat16
NT = (((1,), (1,)), ((), ()))
NN = (((1,), (0,)), ((), ()))
VMEM = pl.BlockSpec(memory_space=pltpu.VMEM)
SMEM = pl.BlockSpec(memory_space=pltpu.SMEM)
ANY = pl.BlockSpec(memory_space=pl.ANY)
HBM = pl.BlockSpec(memory_space=pltpu.HBM)


def send(block, axis, shift):
    count = lax.axis_size(axis)
    return lax.ppermute(block, axis, [(i, i ^ shift) for i in range(count)])


def send_all(blocks, axis, shifts):
    return [send(b, axis, s) for b, s in zip(blocks, shifts)]


def dot(a, b, dims=NN):
    return lax.dot_general(a, b, dims, preferred_element_type=F32)


def shape(*dims, dtype=F32):
    return jax.ShapeDtypeStruct(dims, dtype)


WHOLE = pltpu.CompilerParams(vmem_limit_bytes=67_043_328)


def cost(flops, nbytes):
    return pl.CostEstimate(flops=int(flops), bytes_accessed=int(nbytes), transcendentals=0)


def halves(a):
    high = a.astype(BF16)
    return high, (a - high.astype(F32)).astype(BF16)


def product(a, b, dims=NN):
    (ah, al), (bh, bl) = a, b
    return dot(ah, bh, dims) + (dot(ah, bl, dims) + dot(al, bh, dims))


def eye_mask(n):
    return lax.broadcasted_iota(jnp.int32, (n, n), 0) == lax.broadcasted_iota(jnp.int32, (n, n), 1)


def narrow(k):
    mask = eye_mask(k.shape[0])
    diag = jnp.where(mask, k, 0.0)
    row = 1.0 / jnp.sum(diag, axis=0, keepdims=True)
    col = 1.0 / jnp.sum(diag, axis=1, keepdims=True)
    rest = jnp.where(mask, 0.0, k)
    scaled = rest * row
    return jnp.where(mask, row, -scaled * col), jnp.sum(scaled * (rest * col))


def invert(kernels, x_ref, eye):
    parts = [halves(k) for k in kernels]
    spread = jnp.float32(0.0)
    for j, k in enumerate(kernels):
        x_ref[j], norm = narrow(k)
        spread = jnp.maximum(spread, norm)

    def step():
        worst = jnp.float32(0.0)
        for j, part in enumerate(parts):
            x = x_ref[j]
            xs = halves(x)
            rest = eye - product(part, xs)
            worst = jnp.maximum(worst, jnp.sum(rest * rest))
            x_ref[j] = x + dot(xs[0], rest.astype(BF16))
        return worst

    step()
    lax.while_loop(lambda s: (s[0] < 24) & (s[1] > 1e-6) & (spread < WIDE), lambda s: (s[0] + 1, step()), (jnp.int32(2), step()))
    return spread


def full(a, b, dims=NN):
    return lax.dot_general(a, b, dims, precision=lax.Precision.HIGHEST, preferred_element_type=F32)


def invert_wide(k, x_ref, eye, limit):
    bound = jnp.minimum(jnp.max(jnp.sum(jnp.abs(k), axis=0, keepdims=True)), limit)
    x_ref[...] = eye * (2.0 / (1.0 + bound))

    def step(state):
        x = x_ref[...]
        rest = eye - full(k, x)
        x_ref[...] = x + full(x, rest)
        return state[0] + 1, jnp.sum(rest * rest)

    lax.while_loop(lambda s: (s[0] < 24) & (s[1] > 1e-6), step, (jnp.int32(0), jnp.float32(1.0)))


WIDE = 0.9


def resolvent(grams, x_ref, out_ref):
    n = grams[0][0].shape[0]
    mask = eye_mask(n)
    eye = jnp.where(mask, 1.0, 0.0)
    scaled = []
    for a, b, d in grams:
        scale = (2 * n) / jnp.sum(jnp.where(mask, a + d, 0.0))
        scaled.append((eye + a * scale, b * scale, eye + d * scale))
    spread = invert([d for _, _, d in scaled], x_ref, eye)
    ties, schurs = [], []
    for j, (a, b, d) in enumerate(scaled):
        bs = halves(b)
        tie = halves(product(bs, halves(x_ref[j])))
        ties.append(tie)
        schurs.append(a - product(tie, bs, NT))
    spread = jnp.maximum(spread, invert(schurs, x_ref, eye))
    for j, tie in enumerate(ties):
        x = x_ref[j]
        out_ref[j, :, :n] = x.astype(BF16)
        out_ref[j, :, n:] = (-product(halves(x), tie)).astype(BF16)

    @pl.when(jnp.logical_not(spread < WIDE))
    def _():
        for j, (a, b, d) in enumerate(scaled):
            x = x_ref.at[j]
            invert_wide(d, x, eye, 1.0 + 2 * n)
            tie = full(b, x[...])
            invert_wide(a - full(tie, b, NT), x, eye, 1.0 + 2 * n)
            out_ref[j, :, :n] = x[...].astype(BF16)
            out_ref[j, :, n:] = (-full(x[...], tie)).astype(BF16)


def own_gram_kernel(place, x_ref, keep_ref, give_ref, acc):
    step = pl.program_id(0)
    core = place[1]
    half = keep_ref.shape[0]

    @pl.when(step == 0)
    def _():
        acc[...] = jnp.zeros_like(acc)

    acc[...] += dot(x_ref[...], x_ref[...], NT)

    @pl.when(step == pl.num_programs(0) - 1)
    def _():
        keep_ref[...] = acc[pl.ds(pl.multiple_of(core * half, half), half), :]
        give_ref[...] = acc[pl.ds(pl.multiple_of((1 - core) * half, half), half), :]


def own_gram(place, x, tile=2048):
    rows, columns = x.shape
    half = shape(rows // CORES, rows)
    spec = pl.BlockSpec((rows // CORES, rows), lambda k, place: (0, 0))
    return pl.pallas_call(
        own_gram_kernel,
        out_shape=(half, half),
        grid_spec=pltpu.PrefetchScalarGridSpec(
            num_scalar_prefetch=1,
            grid=(columns // tile,),
            in_specs=[pl.BlockSpec((rows, tile), lambda k, place: (0, k))],
            out_specs=(spec, spec),
            scratch_shapes=[pltpu.VMEM((rows, rows), F32)],
        ),
        cost_estimate=cost(2 * rows * rows * columns, 2 * rows * columns),
        name="own_gram",
    )(place, x)


def pair_gram(me, sources, block, load, chunk):
    rows, share = block.shape[1:]
    copies = []
    for k in range(share // chunk):
        here = slice(k * chunk, (k + 1) * chunk)
        for i, (s, source) in enumerate(sources):
            target = block.at[(me ^ s) % 2, :, here]
            copies.append(pltpu.make_async_copy(source(k * chunk, chunk), target, load.at[2 * k + i]))
            copies[-1].start()
    value = jnp.zeros((rows, rows), F32)
    for k in range(share // chunk):
        copies[2 * k].wait()
        copies[2 * k + 1].wait()
        here = slice(k * chunk, (k + 1) * chunk)
        value = value + dot(block[0, :, here], block[1, :, here], NT)
    return value


SHARES_X, SHARES_Y = (0, 2, 3), (0, 1, 3)


def near_gram_kernel(chunk, place, x, p1, out_ref, x_ref, y_ref, d_ref, block, pack, load, save):
    me = place[0]
    share, raw = p1.shape[1], d_ref.shape[1]

    def mine(column, size, t=0):
        return x.at[:, pl.ds(pl.multiple_of((me ^ t) * share + column, 128), size)]

    def theirs(column, size):
        return p1.at[:, column : column + size]

    packs = [pltpu.make_async_copy(mine(0, raw, t), pack.at[t], save.at[t]) for t in range(GROUP)]
    packs.append(pltpu.make_async_copy(theirs(0, raw), pack.at[GROUP], save.at[GROUP]))
    for copy in packs:
        copy.start()
    out_ref[...] = pair_gram(me, ((0, mine), (1, theirs)), block, load, chunk)
    for copy in packs:
        copy.wait()
    targets = [(t, x_ref.at[i]) for i, t in enumerate(SHARES_X)] + [(t, y_ref.at[i]) for i, t in enumerate(SHARES_Y)]
    targets += [(GROUP, y_ref.at[GROUP - 1]), (0, d_ref)]
    copies = [pltpu.make_async_copy(pack.at[t], target, save.at[i]) for i, (t, target) in enumerate(targets)]
    for copy in copies:
        copy.start()
    for copy in copies:
        copy.wait()


def near_gram(place, x, p1, raw, chunk=512):
    rows, share = p1.shape
    message = shape(GROUP, rows, raw, dtype=BF16)
    return pl.pallas_call(
        functools.partial(near_gram_kernel, chunk),
        out_shape=(shape(rows, rows), message, message, shape(rows, raw, dtype=BF16)),
        in_specs=[SMEM, HBM, HBM],
        out_specs=(VMEM, HBM, HBM, HBM),
        scratch_shapes=[
            pltpu.VMEM((2, rows, share), BF16),
            pltpu.VMEM((GROUP + 1, rows, raw), BF16),
            pltpu.SemaphoreType.DMA((2 * share // chunk,)),
            pltpu.SemaphoreType.DMA((2 * GROUP,)),
        ],
        cost_estimate=cost(2 * rows * rows * share, 4 * rows * share),
        compiler_params=WHOLE,
        name="near_gram",
    )(place, x, p1)


def far_gram_kernel(chunk, place, near, p2, p3, _, keep_out, give_out, x_ref, block, acc, keep_ref, give_ref, load, save):
    me, core = place[0], place[1]
    first_load = pltpu.make_async_copy(near, acc.at[me // 2], save.at[3])
    first_load.start()
    sources = tuple((s, lambda column, size, p=p: p.at[:, column : column + size]) for s, p in ((2, p2), (3, p3)))
    acc[1 - me // 2] = pair_gram(me, sources, block, load, chunk)
    copies = [pltpu.make_async_copy(block.at[(me ^ 2) % 2, :, : x_ref.shape[2]], x_ref.at[GROUP - 1], save.at[0])]
    copies[0].start()
    first_load.wait()
    part = keep_ref.shape[1]
    for s in range(GROUP):
        to = me ^ s
        pair, start = to // 2, (to % 2) * (CORES * part)
        keep_ref[s] = acc[pair, pl.ds(pl.multiple_of(start + core * part, part), part), :]
        give_ref[s] = acc[pair, pl.ds(pl.multiple_of(start + (1 - core) * part, part), part), :]
    for i, (source, target) in enumerate(((give_ref, give_out), (keep_ref, keep_out))):
        copies.append(pltpu.make_async_copy(source, target, save.at[1 + i]))
        copies[-1].start()
    for copy in copies:
        copy.wait()


def far_gram(place, near, p2, p3, message, chunk=512):
    rows, share = p2.shape
    out = shape(GROUP, rows // (2 * CORES), rows)
    return pl.pallas_call(
        functools.partial(far_gram_kernel, chunk),
        out_shape=(out, out, shape(*message.shape, dtype=BF16)),
        in_specs=[SMEM, HBM, HBM, HBM, HBM],
        out_specs=(HBM, HBM, HBM),
        scratch_shapes=[
            pltpu.VMEM((2, rows, share), BF16),
            pltpu.VMEM((GROUP // 2, rows, rows), F32),
            pltpu.VMEM(out.shape, F32),
            pltpu.VMEM(out.shape, F32),
            pltpu.SemaphoreType.DMA((2 * share // chunk,)),
            pltpu.SemaphoreType.DMA((4,)),
        ],
        input_output_aliases={4: 2},
        cost_estimate=cost(2 * rows * rows * share, 4 * rows * share),
        compiler_params=WHOLE,
        name="far_gram",
    )(place, near, p2, p3, message)


def fold(mine, theirs):
    return [mine[s] + theirs[s] for s in range(mine.shape[0])]


def total(arrays):
    return functools.reduce(jnp.add, arrays)


def merge_rows(stacked, w):
    lower = stacked[: w.shape[0]]
    return (lower.astype(F32) - dot(w, stacked)).astype(BF16)


def first_kernel(raw, tile, *refs):
    place, tails, crosses, (x, p1, p2, p3), refs = refs[0], refs[1:9], refs[9:17], refs[17:21], refs[21:]
    m_ref, e_ref, f_ref, w_out, keep_out, give_out, cross, diag, inverse, block, m, acc, keep_ref, give_ref, w, load, save = refs
    me, core = place[0], place[1]
    rows, share = p1.shape
    sources = [x.at[:, pl.ds(pl.multiple_of(me * share, share), share)], p1, p2, p3]
    loads = [
        pltpu.make_async_copy(source, block.at[pl.ds(pl.multiple_of((me ^ s) * rows, rows), rows)], load.at[s])
        for s, source in enumerate(sources)
    ]
    for copy in loads:
        copy.start()

    part, half = rows // (2 * CORES), rows // CORES
    for c in range(CORES):
        for s in range(GROUP):
            source, seat = me ^ s, core ^ c
            start = (source % 2) * (CORES * part) + seat * part
            cross[source // 2, pl.ds(pl.multiple_of(start, part), part), :] = crosses[c * GROUP + s][...]
            diag[source, pl.ds(pl.multiple_of(seat * half, half), half), :] = tails[c * GROUP + s][...]
    grams = [(diag[2 * j], cross[j], diag[2 * j + 1]) for j in range(GROUP // 2)]
    resolvent(grams, inverse, w)
    for copy in loads:
        copy.wait()

    acc[...] = jnp.zeros_like(acc)
    saves = [pltpu.make_async_copy(w, w_out, save.at[share // tile + 4])]
    saves[0].start()
    for k in range(share // tile):
        here = slice(k * tile, (k + 1) * tile)
        m0 = merge_rows(block[: 2 * rows, here], w[0])
        m1 = merge_rows(block[2 * rows :, here], w[1])
        m[:rows, here] = m0
        m[rows:, here] = m1
        saves.append(pltpu.make_async_copy(m.at[:, here], m_ref.at[:, here], save.at[k]))
        saves[-1].start()
        acc[0] += dot(m0, m0, NT)
        acc[1] += dot(m0, m1, NT)
        acc[2] += dot(m1, m1, NT)
    start = raw
    for i, ref in enumerate((e_ref, f_ref)):
        source = m.at[:, start : start + ref.shape[1]]
        saves.append(pltpu.make_async_copy(source, ref, save.at[share // tile + i]))
        saves[-1].start()
        start += ref.shape[1]
    lower = lax.broadcasted_iota(jnp.int32, (rows, rows), 0) >= lax.broadcasted_iota(jnp.int32, (rows, rows), 1)
    row = jnp.sum(jnp.where(eye_mask(rows), acc[2], 0.0), axis=0, keepdims=True)
    acc[2] = jnp.where(lower, acc[0], acc[2])
    part = rows // (GROUP * CORES)
    for s in range(GROUP):
        to = me ^ s
        for ref, seat in ((give_ref, to * CORES + 1 - core), (keep_ref, to * CORES + core)):
            here = pl.ds(pl.multiple_of(seat * part, part), part)
            ref[s, :part] = acc[1, here, :]
            ref[s, part : 2 * part] = acc[2, here, :]
            ref[s, 2 * part :] = jnp.broadcast_to(row, (8, rows))
    for i, (source, target) in enumerate(((give_ref, give_out), (keep_ref, keep_out))):
        saves.append(pltpu.make_async_copy(source, target, save.at[share // tile + 2 + i]))
        saves[-1].start()
    for copy in saves:
        copy.wait()


def first(place, diagonals, crosses, x, pieces, raw, ahead, tile=512):
    rows, share = pieces[0].shape
    pairs = GROUP // 2
    out = shape(GROUP, 2 * rows // (GROUP * CORES) + 8, rows)
    return pl.pallas_call(
        functools.partial(first_kernel, raw, tile),
        out_shape=tuple(shape(pairs * rows, n, dtype=BF16) for n in (share, *ahead)) + (shape(pairs, rows, 2 * rows, dtype=BF16), out, out),
        in_specs=[SMEM] + [VMEM] * (4 * GROUP) + [HBM] * 4,
        out_specs=(ANY,) * 6,
        scratch_shapes=[
            pltpu.VMEM((pairs, rows, rows), F32),
            pltpu.VMEM((GROUP, rows, rows), F32),
            pltpu.VMEM((pairs, rows, rows), F32),
            pltpu.VMEM((GROUP * rows, share), BF16),
            pltpu.VMEM((pairs * rows, share), BF16),
            pltpu.VMEM((3, rows, rows), F32),
            pltpu.VMEM(out.shape, F32),
            pltpu.VMEM(out.shape, F32),
            pltpu.VMEM((pairs, rows, 2 * rows), BF16),
            pltpu.SemaphoreType.DMA((GROUP,)),
            pltpu.SemaphoreType.DMA((share // tile + 5,)),
        ],
        cost_estimate=cost(2 * pairs * rows**3 * 40 + 14 * rows * rows * share, 12 * rows * share),
        name="first",
    )(place, *diagonals, *crosses, x, *pieces)


def second_kernel(*refs):
    place, bundles, m_ref, refs = refs[0], refs[1:9], refs[9], refs[10:]
    a_ref, b_ref, w_out, gram, inverse, m, w_ref, merged, load, save = refs
    me, core = place[0], place[1]
    rows = m.shape[0] // 2
    copy = pltpu.make_async_copy(m_ref.at[:, m_ref.shape[1] - m.shape[1] :], m, load)
    copy.start()
    part = rows // (GROUP * CORES)
    for c in range(CORES):
        for s in range(GROUP):
            seat = (me ^ s) * CORES + (core ^ c)
            for b in range(2):
                gram[b, pl.ds(pl.multiple_of(seat * part, part), part), :] = bundles[c * GROUP + s][b * part : (b + 1) * part]
    packed = gram[1]
    turned = packed.T
    lower = lax.broadcasted_iota(jnp.int32, (rows, rows), 0) >= lax.broadcasted_iota(jnp.int32, (rows, rows), 1)
    diagonal = jnp.broadcast_to(bundles[0][2 * part : 2 * part + 1], (rows, rows))
    upper_gram = jnp.where(eye_mask(rows), diagonal, jnp.where(lower, turned, packed))
    resolvent([(jnp.where(lower, packed, turned), gram[0], upper_gram)], inverse, w_ref)
    copy.wait()
    saves = [pltpu.make_async_copy(w_ref, w_out, save.at[2])]
    saves[0].start()
    half = a_ref.shape[1]
    for i, ref in enumerate((a_ref, b_ref)):
        here = slice(i * half, (i + 1) * half)
        merged[:, here] = merge_rows(m[:, here], w_ref[0])
        saves.append(pltpu.make_async_copy(merged.at[:, here], ref, save.at[i]))
        saves[-1].start()
    for save_copy in saves:
        save_copy.wait()


def second(place, bundles, m, early):
    rows, share = m.shape[0] // 2, m.shape[1]
    half = (share - early) // 2
    return pl.pallas_call(
        second_kernel,
        out_shape=(shape(rows, half, dtype=BF16),) * 2 + (shape(1, rows, 2 * rows, dtype=BF16),),
        in_specs=[SMEM] + [VMEM] * (2 * GROUP) + [ANY],
        out_specs=(ANY,) * 3,
        scratch_shapes=[
            pltpu.VMEM((2, rows, rows), F32),
            pltpu.VMEM((1, rows, rows), F32),
            pltpu.VMEM((2 * rows, 2 * half), BF16),
            pltpu.VMEM((1, rows, 2 * rows), BF16),
            pltpu.VMEM((rows, 2 * half), BF16),
            pltpu.SemaphoreType.DMA,
            pltpu.SemaphoreType.DMA((3,)),
        ],
        cost_estimate=cost(2 * rows**3 * 40 + 8 * rows * rows * half, 6 * rows * share),
        name="second",
    )(place, *bundles, m)


def raw_merge_kernel(share, place, w0, w1, x, xs, ys, d, _, out, block, pair, buffer, load, save):
    me = place[0]
    rows, raw = d.shape
    saves = []
    sources = {}
    for v in PEERS:
        mine = x.at[:, pl.ds(pl.multiple_of((me ^ v) * share, 128), raw)]
        across = {1: xs.at[GROUP - 1], 2: ys.at[GROUP - 1], 3: d}[v]
        sources[v] = (mine, xs.at[SHARES_X.index(v ^ 1)], ys.at[SHARES_Y.index(v ^ 2)], across)
    loads = {}
    for v, group in sources.items():
        for s, source in enumerate(group):
            target = block.at[v - 1, pl.ds(pl.multiple_of((me ^ s) * rows, rows), rows)]
            loads[v, s] = pltpu.make_async_copy(source, target, load.at[(v - 1) * GROUP + s])
            loads[v, s].start()
    for v in sources:
        for s in range(GROUP):
            loads[v, s].wait()
        for j in range(GROUP // 2):
            pair[j * rows : (j + 1) * rows] = merge_rows(block[v - 1, 2 * j * rows : 2 * (j + 1) * rows], w0[j])
        buffer[v - 1] = merge_rows(pair[...], w1[0])
        target = out.at[:, pl.ds(pl.multiple_of((me ^ v) * share, 128), raw)]
        saves.append(pltpu.make_async_copy(buffer.at[v - 1], target, save.at[v - 1]))
        saves[-1].start()
    for copy in saves:
        copy.wait()


def raw_merge(place, w0, w1, x, messages, out, share):
    rows, raw = messages[2].shape
    return pl.pallas_call(
        functools.partial(raw_merge_kernel, share),
        out_shape=shape(*out.shape, dtype=BF16),
        in_specs=[SMEM, VMEM, VMEM] + [HBM] * 5,
        out_specs=HBM,
        scratch_shapes=[
            pltpu.VMEM((GROUP - 1, GROUP * rows, raw), BF16),
            pltpu.VMEM((2 * rows, raw), BF16),
            pltpu.VMEM((GROUP - 1, rows, raw), BF16),
            pltpu.SemaphoreType.DMA(((GROUP - 1) * GROUP,)),
            pltpu.SemaphoreType.DMA((GROUP - 1,)),
        ],
        input_output_aliases={7: 0},
        cost_estimate=cost(12 * rows * rows * raw * (GROUP - 1), 10 * rows * raw * (GROUP - 1)),
        compiler_params=WHOLE,
        name="raw_merge",
    )(place, w0, w1, x, *messages, out)


def late_kernel(share, raw, place, w_in, a, b, m, *refs):
    early, (out, w, mine, own, ends, wide, thin, buffer, load, save) = refs[:-10], refs[-10:]
    me, size, half = place[0], mine.shape[1], a.shape[1]
    boxes = [box.at[i] for box in (wide, thin) for i in range(len(PEERS))]
    moves = [(w_in, w), *zip(early, boxes), (m.at[:, :size], mine), (a, ends.at[0]), (b, ends.at[1])]
    loads = [pltpu.make_async_copy(source, target, load.at[i]) for i, (source, target) in enumerate(moves)]
    for copy in loads:
        copy.start()
    saves = []

    def put(source, owner, column):
        target = out.at[:, pl.ds(pl.multiple_of(owner * share + column, 128), source.shape[1])]
        saves.append(pltpu.make_async_copy(source, target, save.at[len(saves)]))
        saves[-1].start()

    loads[0].wait()
    for i, box in enumerate(boxes):
        loads[1 + i].wait()
        s, column = PEERS[i % len(PEERS)], 0 if i < len(PEERS) else wide.shape[2]
        spot = buffer.at[s - 1, :, column : column + box.shape[1]]
        spot[...] = merge_rows(box[...], w[0])
        put(spot, me ^ s, raw + column)
    loads[-3].wait()
    own[...] = merge_rows(mine[...], w[0])
    put(own, me, 0)
    for i in range(2):
        loads[i - 2].wait()
        put(ends.at[i], me, size + i * half)
    for copy in saves:
        copy.wait()


def late(place, w, a, b, m, pairs, raw, share):
    rows, half = a.shape
    size = share - 2 * half
    boxes = [pltpu.VMEM((len(PEERS), *pairs[i].shape), BF16) for i in (0, len(PEERS))]
    return pl.pallas_call(
        functools.partial(late_kernel, share, raw),
        out_shape=shape(rows, GROUP * share, dtype=BF16),
        in_specs=[SMEM] + [HBM] * (4 + len(pairs)),
        out_specs=HBM,
        scratch_shapes=[
            pltpu.VMEM(w.shape, BF16),
            pltpu.VMEM((2 * rows, size), BF16),
            pltpu.VMEM((rows, size), BF16),
            pltpu.VMEM((2, rows, half), BF16),
            *boxes,
            pltpu.VMEM((GROUP - 1, rows, size - raw), BF16),
            pltpu.SemaphoreType.DMA((len(pairs) + 4,)),
            pltpu.SemaphoreType.DMA((len(pairs) + 3,)),
        ],
        cost_estimate=cost(4 * rows * rows * size * GROUP, 6 * rows * size * GROUP),
        compiler_params=WHOLE,
        name="late",
    )(place, w, a, b, m, *pairs)


def put_kernel(spots, share, place, *refs):
    count = len(spots)
    blocks, out, buffers, load, save = refs[:count], refs[count + 1], refs[count + 2 : -2], refs[-2], refs[-1]
    loads, saves = [], []
    for i, ((s, column), block, buffer) in enumerate(zip(spots, blocks, buffers)):
        start = pl.multiple_of((place[0] ^ s) * share + column, 128)
        loads.append(pltpu.make_async_copy(block, buffer, load.at[i]))
        loads[-1].start()
        saves.append(pltpu.make_async_copy(buffer, out.at[:, pl.ds(start, block.shape[1])], save.at[i]))
    for load_copy, save_copy in zip(loads, saves):
        load_copy.wait()
        save_copy.start()
    for copy in saves:
        copy.wait()


def put(place, out, blocks, spots, share):
    size = sum(b.size for b in blocks)
    return pl.pallas_call(
        functools.partial(put_kernel, spots, share),
        out_shape=shape(*out.shape, dtype=out.dtype),
        in_specs=[SMEM] + [HBM] * (len(blocks) + 1),
        out_specs=HBM,
        scratch_shapes=[pltpu.VMEM(b.shape, b.dtype) for b in blocks] + [pltpu.SemaphoreType.DMA((len(blocks),))] * 2,
        input_output_aliases={1 + len(blocks): 0},
        cost_estimate=cost(0, 4 * size),
        compiler_params=WHOLE,
        name="put",
    )(place, *blocks, out)


def over_chips(block):
    chips = lax.axis_size("feat") // CORES
    return total([block] + [send(block, "feat", CORES * s) for s in range(1, chips)])


def gather_group(bundle):
    mine = [bundle] + send_all([bundle] * len(PEERS), "dp", PEERS)
    return mine + [send(b, "feat", 1) for b in mine]


def run(sketches):
    x = sketches[0]
    rows, columns = x.shape
    share = columns // GROUP
    raw, ahead = 3 * share // 16, (3 * share // 16, share // 8)
    early = raw + sum(ahead)
    me = lax.axis_index("dp") % GROUP
    place = jnp.stack([me, lax.axis_index("feat") % CORES]).astype(jnp.int32)

    cuts, source = {}, x
    for s in PEERS:
        cuts[s] = lax.dynamic_slice(source, (0, (me ^ s) * share), (rows, share))
        if s == 2:
            source, cuts = lax.optimization_barrier((source, cuts))
    pieces = {s: send(cut, "dp", s) for s, cut in cuts.items()}
    keep, give = own_gram(place, x)
    own = over_chips(total([keep, send(give, "feat", 1)]))
    near, to_x, to_y, to_d = near_gram(place, x, pieces[1], raw)
    p2, p3, own, near = lax.optimization_barrier((pieces[2], pieces[3], own, near))

    keep, give, to_x = far_gram(place, near, p2, p3, to_x)
    parts = fold(keep, send(give, "feat", 1))
    parts, own, to_d = lax.optimization_barrier((parts, own, to_d))
    mine = total([parts[0]] + send_all(parts[1:], "dp", PEERS))
    diagonals = gather_group(own)
    from_d = send(to_d, "dp", 3)
    bundle = over_chips(mine)
    bundle, to_x, to_y = lax.optimization_barrier((bundle, to_x, to_y))
    crosses = gather_group(bundle)
    messages = [send(to_x, "dp", 1), send(to_y, "dp", 2), from_d]
    m, e, f, w0, keep, give = first(place, diagonals, crosses, x, [pieces[1], p2, p3], raw, ahead)

    parts = fold(keep, send(give, "feat", 1))
    parts, e, f = lax.optimization_barrier((parts, e, f))
    mine = total([parts[0]] + send_all(parts[1:], "dp", PEERS))
    pairs_a, pairs_b = [[send(block, "dp", s) for s in (1, 2)] for block in (e, f)]
    bundles = gather_group(over_chips(mine))
    pairs = pairs_a + [send(pairs_a[0], "dp", 2)] + pairs_b + [send(pairs_b[1], "dp", 1)]
    a, b, w1 = second(place, bundles, m, early)

    ax, by = send(a, "dp", 1), send(b, "dp", 2)
    bx, ay = send(b, "dp", 1), send(a, "dp", 2)
    ad, bd = send(ax, "dp", 2), send(by, "dp", 1)
    left, right = early, early + a.shape[1]
    out = late(place, w1, a, b, m, pairs, raw, share)
    out = raw_merge(place, w0, w1, x, messages, out, share)
    out = put(place, out, [ax, by, bx, ay], ((1, left), (2, right), (1, right), (2, left)), share)
    out = put(place, out, [ad, bd], ((3, left), (3, right)), share)
    return out[None]


def solution(mesh):
    spec = P("dp", None, "feat")
    return jax.shard_map(run, mesh=mesh, in_specs=(spec,), out_specs=spec, check_vma=False)
```

```python
import functools

import jax
import jax.numpy as jnp
from jax import lax
from jax.experimental import pallas as pl
from jax.experimental.pallas import tpu as pltpu
from jax.sharding import PartitionSpec as P


LEVELS = 2
GROUP = 2**LEVELS
CORES = 2
PEERS = tuple(range(1, GROUP))
F32, BF16 = jnp.float32, jnp.bfloat16
NT = (((1,), (1,)), ((), ()))
NN = (((1,), (0,)), ((), ()))
VMEM = pl.BlockSpec(memory_space=pltpu.VMEM)
SMEM = pl.BlockSpec(memory_space=pltpu.SMEM)
ANY = pl.BlockSpec(memory_space=pl.ANY)
HBM = pl.BlockSpec(memory_space=pltpu.HBM)


def send(block, axis, shift):
    count = lax.axis_size(axis)
    return lax.ppermute(block, axis, [(i, i ^ shift) for i in range(count)])


def send_all(blocks, axis, shifts):
    return [send(b, axis, s) for b, s in zip(blocks, shifts)]


def dot(a, b, dims=NN):
    return lax.dot_general(a, b, dims, preferred_element_type=F32)


def shape(*dims, dtype=F32):
    return jax.ShapeDtypeStruct(dims, dtype)


WHOLE = pltpu.CompilerParams(vmem_limit_bytes=67_043_328)


def cost(flops, nbytes):
    return pl.CostEstimate(flops=int(flops), bytes_accessed=int(nbytes), transcendentals=0)


def halves(a):
    high = a.astype(BF16)
    return high, (a - high.astype(F32)).astype(BF16)


def product(a, b, dims=NN):
    (ah, al), (bh, bl) = a, b
    return dot(ah, bh, dims) + (dot(ah, bl, dims) + dot(al, bh, dims))


def eye_mask(n):
    return lax.broadcasted_iota(jnp.int32, (n, n), 0) == lax.broadcasted_iota(jnp.int32, (n, n), 1)


def narrow(k):
    mask = eye_mask(k.shape[0])
    diag = jnp.where(mask, k, 0.0)
    row = 1.0 / jnp.sum(diag, axis=0, keepdims=True)
    col = 1.0 / jnp.sum(diag, axis=1, keepdims=True)
    rest = jnp.where(mask, 0.0, k)
    scaled = rest * row
    return jnp.where(mask, row, -scaled * col), jnp.sum(scaled * (rest * col))


def invert(kernels, x_ref, eye):
    parts = [halves(k) for k in kernels]
    spread = jnp.float32(0.0)
    for j, k in enumerate(kernels):
        x_ref[j], norm = narrow(k)
        spread = jnp.maximum(spread, norm)

    def step():
        worst = jnp.float32(0.0)
        for j, part in enumerate(parts):
            x = x_ref[j]
            xs = halves(x)
            rest = eye - product(part, xs)
            worst = jnp.maximum(worst, jnp.sum(rest * rest))
            x_ref[j] = x + dot(xs[0], rest.astype(BF16))
        return worst

    step()
    lax.while_loop(lambda s: (s[0] < 24) & (s[1] > 1e-6) & (spread < WIDE), lambda s: (s[0] + 1, step()), (jnp.int32(2), step()))
    return spread


def full(a, b, dims=NN):
    return lax.dot_general(a, b, dims, precision=lax.Precision.HIGHEST, preferred_element_type=F32)


def invert_wide(k, x_ref, eye, limit):
    bound = jnp.minimum(jnp.max(jnp.sum(jnp.abs(k), axis=0, keepdims=True)), limit)
    x_ref[...] = eye * (2.0 / (1.0 + bound))

    def step(state):
        x = x_ref[...]
        rest = eye - full(k, x)
        x_ref[...] = x + full(x, rest)
        return state[0] + 1, jnp.sum(rest * rest)

    lax.while_loop(lambda s: (s[0] < 24) & (s[1] > 1e-6), step, (jnp.int32(0), jnp.float32(1.0)))


WIDE = 0.9


def resolvent(grams, x_ref, out_ref):
    n = grams[0][0].shape[0]
    mask = eye_mask(n)
    eye = jnp.where(mask, 1.0, 0.0)
    scaled = []
    for a, b, d in grams:
        scale = (2 * n) / jnp.sum(jnp.where(mask, a + d, 0.0))
        scaled.append((eye + a * scale, b * scale, eye + d * scale))
    spread = invert([d for _, _, d in scaled], x_ref, eye)
    ties, schurs = [], []
    for j, (a, b, d) in enumerate(scaled):
        bs = halves(b)
        tie = halves(product(bs, halves(x_ref[j])))
        ties.append(tie)
        schurs.append(a - product(tie, bs, NT))
    spread = jnp.maximum(spread, invert(schurs, x_ref, eye))
    for j, tie in enumerate(ties):
        x = x_ref[j]
        out_ref[j, :, :n] = x.astype(BF16)
        out_ref[j, :, n:] = (-product(halves(x), tie)).astype(BF16)

    @pl.when(jnp.logical_not(spread < WIDE))
    def _():
        for j, (a, b, d) in enumerate(scaled):
            x = x_ref.at[j]
            invert_wide(d, x, eye, 1.0 + 2 * n)
            tie = full(b, x[...])
            invert_wide(a - full(tie, b, NT), x, eye, 1.0 + 2 * n)
            out_ref[j, :, :n] = x[...].astype(BF16)
            out_ref[j, :, n:] = (-full(x[...], tie)).astype(BF16)


def own_gram_kernel(place, x_ref, keep_ref, give_ref, acc):
    step = pl.program_id(0)
    core = place[1]
    half = keep_ref.shape[0]

    @pl.when(step == 0)
    def _():
        acc[...] = jnp.zeros_like(acc)

    acc[...] += dot(x_ref[...], x_ref[...], NT)

    @pl.when(step == pl.num_programs(0) - 1)
    def _():
        keep_ref[...] = acc[pl.ds(pl.multiple_of(core * half, half), half), :]
        give_ref[...] = acc[pl.ds(pl.multiple_of((1 - core) * half, half), half), :]


def own_gram(place, x, tile=2048):
    rows, columns = x.shape
    half = shape(rows // CORES, rows)
    spec = pl.BlockSpec((rows // CORES, rows), lambda k, place: (0, 0))
    return pl.pallas_call(
        own_gram_kernel,
        out_shape=(half, half),
        grid_spec=pltpu.PrefetchScalarGridSpec(
            num_scalar_prefetch=1,
            grid=(columns // tile,),
            in_specs=[pl.BlockSpec((rows, tile), lambda k, place: (0, k))],
            out_specs=(spec, spec),
            scratch_shapes=[pltpu.VMEM((rows, rows), F32)],
        ),
        cost_estimate=cost(2 * rows * rows * columns, 2 * rows * columns),
        name="own_gram",
    )(place, x)


def pair_gram(me, sources, block, load, chunk):
    rows, share = block.shape[1:]
    copies = []
    for k in range(share // chunk):
        here = slice(k * chunk, (k + 1) * chunk)
        for i, (s, source) in enumerate(sources):
            target = block.at[(me ^ s) % 2, :, here]
            copies.append(pltpu.make_async_copy(source(k * chunk, chunk), target, load.at[2 * k + i]))
            copies[-1].start()
    value = jnp.zeros((rows, rows), F32)
    for k in range(share // chunk):
        copies[2 * k].wait()
        copies[2 * k + 1].wait()
        here = slice(k * chunk, (k + 1) * chunk)
        value = value + dot(block[0, :, here], block[1, :, here], NT)
    return value


SHARES_X, SHARES_Y = (0, 2, 3), (0, 1, 3)


def near_gram_kernel(chunk, place, x, p1, out_ref, x_ref, y_ref, d_ref, block, pack, load, save):
    me = place[0]
    share, raw = p1.shape[1], d_ref.shape[1]

    def mine(column, size, t=0):
        return x.at[:, pl.ds(pl.multiple_of((me ^ t) * share + column, 128), size)]

    def theirs(column, size):
        return p1.at[:, column : column + size]

    packs = [pltpu.make_async_copy(mine(0, raw, t), pack.at[t], save.at[t]) for t in range(GROUP)]
    packs.append(pltpu.make_async_copy(theirs(0, raw), pack.at[GROUP], save.at[GROUP]))
    for copy in packs:
        copy.start()
    out_ref[...] = pair_gram(me, ((0, mine), (1, theirs)), block, load, chunk)
    for copy in packs:
        copy.wait()
    targets = [(t, x_ref.at[i]) for i, t in enumerate(SHARES_X)] + [(t, y_ref.at[i]) for i, t in enumerate(SHARES_Y)]
    targets += [(GROUP, y_ref.at[GROUP - 1]), (0, d_ref)]
    copies = [pltpu.make_async_copy(pack.at[t], target, save.at[i]) for i, (t, target) in enumerate(targets)]
    for copy in copies:
        copy.start()
    for copy in copies:
        copy.wait()


def near_gram(place, x, p1, raw, chunk=512):
    rows, share = p1.shape
    message = shape(GROUP, rows, raw, dtype=BF16)
    return pl.pallas_call(
        functools.partial(near_gram_kernel, chunk),
        out_shape=(shape(rows, rows), message, message, shape(rows, raw, dtype=BF16)),
        in_specs=[SMEM, HBM, HBM],
        out_specs=(VMEM, HBM, HBM, HBM),
        scratch_shapes=[
            pltpu.VMEM((2, rows, share), BF16),
            pltpu.VMEM((GROUP + 1, rows, raw), BF16),
            pltpu.SemaphoreType.DMA((2 * share // chunk,)),
            pltpu.SemaphoreType.DMA((2 * GROUP,)),
        ],
        cost_estimate=cost(2 * rows * rows * share, 4 * rows * share),
        compiler_params=WHOLE,
        name="near_gram",
    )(place, x, p1)


def far_gram_kernel(chunk, place, near, p2, p3, _, keep_out, give_out, x_ref, block, acc, keep_ref, give_ref, load, save):
    me, core = place[0], place[1]
    first_load = pltpu.make_async_copy(near, acc.at[me // 2], save.at[3])
    first_load.start()
    sources = tuple((s, lambda column, size, p=p: p.at[:, column : column + size]) for s, p in ((2, p2), (3, p3)))
    acc[1 - me // 2] = pair_gram(me, sources, block, load, chunk)
    copies = [pltpu.make_async_copy(block.at[(me ^ 2) % 2, :, : x_ref.shape[2]], x_ref.at[GROUP - 1], save.at[0])]
    copies[0].start()
    first_load.wait()
    part = keep_ref.shape[1]
    for s in range(GROUP):
        to = me ^ s
        pair, start = to // 2, (to % 2) * (CORES * part)
        keep_ref[s] = acc[pair, pl.ds(pl.multiple_of(start + core * part, part), part), :]
        give_ref[s] = acc[pair, pl.ds(pl.multiple_of(start + (1 - core) * part, part), part), :]
    for i, (source, target) in enumerate(((give_ref, give_out), (keep_ref, keep_out))):
        copies.append(pltpu.make_async_copy(source, target, save.at[1 + i]))
        copies[-1].start()
    for copy in copies:
        copy.wait()


def far_gram(place, near, p2, p3, message, chunk=512):
    rows, share = p2.shape
    out = shape(GROUP, rows // (2 * CORES), rows)
    return pl.pallas_call(
        functools.partial(far_gram_kernel, chunk),
        out_shape=(out, out, shape(*message.shape, dtype=BF16)),
        in_specs=[SMEM, HBM, HBM, HBM, HBM],
        out_specs=(HBM, HBM, HBM),
        scratch_shapes=[
            pltpu.VMEM((2, rows, share), BF16),
            pltpu.VMEM((GROUP // 2, rows, rows), F32),
            pltpu.VMEM(out.shape, F32),
            pltpu.VMEM(out.shape, F32),
            pltpu.SemaphoreType.DMA((2 * share // chunk,)),
            pltpu.SemaphoreType.DMA((4,)),
        ],
        input_output_aliases={4: 2},
        cost_estimate=cost(2 * rows * rows * share, 4 * rows * share),
        compiler_params=WHOLE,
        name="far_gram",
    )(place, near, p2, p3, message)


def fold(mine, theirs):
    return [mine[s] + theirs[s] for s in range(mine.shape[0])]


def total(arrays):
    return functools.reduce(jnp.add, arrays)


def merge_rows(stacked, w):
    lower = stacked[: w.shape[0]]
    return (lower.astype(F32) - dot(w, stacked)).astype(BF16)


def first_kernel(raw, tile, *refs):
    place, tails, crosses, (x, p1, p2, p3), refs = refs[0], refs[1:9], refs[9:17], refs[17:21], refs[21:]
    m_ref, e_ref, f_ref, w_out, keep_out, give_out, cross, diag, inverse, block, m, acc, keep_ref, give_ref, w, load, save = refs
    me, core = place[0], place[1]
    rows, share = p1.shape
    sources = [x.at[:, pl.ds(pl.multiple_of(me * share, share), share)], p1, p2, p3]
    loads = [
        pltpu.make_async_copy(source, block.at[pl.ds(pl.multiple_of((me ^ s) * rows, rows), rows)], load.at[s])
        for s, source in enumerate(sources)
    ]
    for copy in loads:
        copy.start()

    part, half = rows // (2 * CORES), rows // CORES
    for c in range(CORES):
        for s in range(GROUP):
            source, seat = me ^ s, core ^ c
            start = (source % 2) * (CORES * part) + seat * part
            cross[source // 2, pl.ds(pl.multiple_of(start, part), part), :] = crosses[c * GROUP + s][...]
            diag[source, pl.ds(pl.multiple_of(seat * half, half), half), :] = tails[c * GROUP + s][...]
    grams = [(diag[2 * j], cross[j], diag[2 * j + 1]) for j in range(GROUP // 2)]
    resolvent(grams, inverse, w)
    for copy in loads:
        copy.wait()

    acc[...] = jnp.zeros_like(acc)
    saves = [pltpu.make_async_copy(w, w_out, save.at[share // tile + 4])]
    saves[0].start()
    for k in range(share // tile):
        here = slice(k * tile, (k + 1) * tile)
        m0 = merge_rows(block[: 2 * rows, here], w[0])
        m1 = merge_rows(block[2 * rows :, here], w[1])
        m[:rows, here] = m0
        m[rows:, here] = m1
        saves.append(pltpu.make_async_copy(m.at[:, here], m_ref.at[:, here], save.at[k]))
        saves[-1].start()
        acc[0] += dot(m0, m0, NT)
        acc[1] += dot(m0, m1, NT)
        acc[2] += dot(m1, m1, NT)
    start = raw
    for i, ref in enumerate((e_ref, f_ref)):
        source = m.at[:, start : start + ref.shape[1]]
        saves.append(pltpu.make_async_copy(source, ref, save.at[share // tile + i]))
        saves[-1].start()
        start += ref.shape[1]
    lower = lax.broadcasted_iota(jnp.int32, (rows, rows), 0) >= lax.broadcasted_iota(jnp.int32, (rows, rows), 1)
    row = jnp.sum(jnp.where(eye_mask(rows), acc[2], 0.0), axis=0, keepdims=True)
    acc[2] = jnp.where(lower, acc[0], acc[2])
    part = rows // (GROUP * CORES)
    for s in range(GROUP):
        to = me ^ s
        for ref, seat in ((give_ref, to * CORES + 1 - core), (keep_ref, to * CORES + core)):
            here = pl.ds(pl.multiple_of(seat * part, part), part)
            ref[s, :part] = acc[1, here, :]
            ref[s, part : 2 * part] = acc[2, here, :]
            ref[s, 2 * part :] = jnp.broadcast_to(row, (8, rows))
    for i, (source, target) in enumerate(((give_ref, give_out), (keep_ref, keep_out))):
        saves.append(pltpu.make_async_copy(source, target, save.at[share // tile + 2 + i]))
        saves[-1].start()
    for copy in saves:
        copy.wait()


def first(place, diagonals, crosses, x, pieces, raw, ahead, tile=512):
    rows, share = pieces[0].shape
    pairs = GROUP // 2
    out = shape(GROUP, 2 * rows // (GROUP * CORES) + 8, rows)
    return pl.pallas_call(
        functools.partial(first_kernel, raw, tile),
        out_shape=tuple(shape(pairs * rows, n, dtype=BF16) for n in (share, *ahead)) + (shape(pairs, rows, 2 * rows, dtype=BF16), out, out),
        in_specs=[SMEM] + [VMEM] * (4 * GROUP) + [HBM] * 4,
        out_specs=(ANY,) * 6,
        scratch_shapes=[
            pltpu.VMEM((pairs, rows, rows), F32),
            pltpu.VMEM((GROUP, rows, rows), F32),
            pltpu.VMEM((pairs, rows, rows), F32),
            pltpu.VMEM((GROUP * rows, share), BF16),
            pltpu.VMEM((pairs * rows, share), BF16),
            pltpu.VMEM((3, rows, rows), F32),
            pltpu.VMEM(out.shape, F32),
            pltpu.VMEM(out.shape, F32),
            pltpu.VMEM((pairs, rows, 2 * rows), BF16),
            pltpu.SemaphoreType.DMA((GROUP,)),
            pltpu.SemaphoreType.DMA((share // tile + 5,)),
        ],
        cost_estimate=cost(2 * pairs * rows**3 * 40 + 14 * rows * rows * share, 12 * rows * share),
        name="first",
    )(place, *diagonals, *crosses, x, *pieces)


def second_kernel(*refs):
    place, bundles, m_ref, refs = refs[0], refs[1:9], refs[9], refs[10:]
    a_ref, b_ref, w_out, gram, inverse, m, w_ref, merged, load, save = refs
    me, core = place[0], place[1]
    rows = m.shape[0] // 2
    copy = pltpu.make_async_copy(m_ref.at[:, m_ref.shape[1] - m.shape[1] :], m, load)
    copy.start()
    part = rows // (GROUP * CORES)
    for c in range(CORES):
        for s in range(GROUP):
            seat = (me ^ s) * CORES + (core ^ c)
            for b in range(2):
                gram[b, pl.ds(pl.multiple_of(seat * part, part), part), :] = bundles[c * GROUP + s][b * part : (b + 1) * part]
    packed = gram[1]
    turned = packed.T
    lower = lax.broadcasted_iota(jnp.int32, (rows, rows), 0) >= lax.broadcasted_iota(jnp.int32, (rows, rows), 1)
    diagonal = jnp.broadcast_to(bundles[0][2 * part : 2 * part + 1], (rows, rows))
    upper_gram = jnp.where(eye_mask(rows), diagonal, jnp.where(lower, turned, packed))
    resolvent([(jnp.where(lower, packed, turned), gram[0], upper_gram)], inverse, w_ref)
    copy.wait()
    saves = [pltpu.make_async_copy(w_ref, w_out, save.at[2])]
    saves[0].start()
    half = a_ref.shape[1]
    for i, ref in enumerate((a_ref, b_ref)):
        here = slice(i * half, (i + 1) * half)
        merged[:, here] = merge_rows(m[:, here], w_ref[0])
        saves.append(pltpu.make_async_copy(merged.at[:, here], ref, save.at[i]))
        saves[-1].start()
    for save_copy in saves:
        save_copy.wait()


def second(place, bundles, m, early):
    rows, share = m.shape[0] // 2, m.shape[1]
    half = (share - early) // 2
    return pl.pallas_call(
        second_kernel,
        out_shape=(shape(rows, half, dtype=BF16),) * 2 + (shape(1, rows, 2 * rows, dtype=BF16),),
        in_specs=[SMEM] + [VMEM] * (2 * GROUP) + [ANY],
        out_specs=(ANY,) * 3,
        scratch_shapes=[
            pltpu.VMEM((2, rows, rows), F32),
            pltpu.VMEM((1, rows, rows), F32),
            pltpu.VMEM((2 * rows, 2 * half), BF16),
            pltpu.VMEM((1, rows, 2 * rows), BF16),
            pltpu.VMEM((rows, 2 * half), BF16),
            pltpu.SemaphoreType.DMA,
            pltpu.SemaphoreType.DMA((3,)),
        ],
        cost_estimate=cost(2 * rows**3 * 40 + 8 * rows * rows * half, 6 * rows * share),
        name="second",
    )(place, *bundles, m)


def raw_merge_kernel(share, place, w0, w1, x, xs, ys, d, _, out, block, pair, buffer, load, save):
    me = place[0]
    rows, raw = d.shape
    saves = []
    sources = {}
    for v in PEERS:
        mine = x.at[:, pl.ds(pl.multiple_of((me ^ v) * share, 128), raw)]
        across = {1: xs.at[GROUP - 1], 2: ys.at[GROUP - 1], 3: d}[v]
        sources[v] = (mine, xs.at[SHARES_X.index(v ^ 1)], ys.at[SHARES_Y.index(v ^ 2)], across)
    loads = {}
    for v, group in sources.items():
        for s, source in enumerate(group):
            target = block.at[v - 1, pl.ds(pl.multiple_of((me ^ s) * rows, rows), rows)]
            loads[v, s] = pltpu.make_async_copy(source, target, load.at[(v - 1) * GROUP + s])
            loads[v, s].start()
    for v in sources:
        for s in range(GROUP):
            loads[v, s].wait()
        for j in range(GROUP // 2):
            pair[j * rows : (j + 1) * rows] = merge_rows(block[v - 1, 2 * j * rows : 2 * (j + 1) * rows], w0[j])
        buffer[v - 1] = merge_rows(pair[...], w1[0])
        target = out.at[:, pl.ds(pl.multiple_of((me ^ v) * share, 128), raw)]
        saves.append(pltpu.make_async_copy(buffer.at[v - 1], target, save.at[v - 1]))
        saves[-1].start()
    for copy in saves:
        copy.wait()


def raw_merge(place, w0, w1, x, messages, out, share):
    rows, raw = messages[2].shape
    return pl.pallas_call(
        functools.partial(raw_merge_kernel, share),
        out_shape=shape(*out.shape, dtype=BF16),
        in_specs=[SMEM, VMEM, VMEM] + [HBM] * 5,
        out_specs=HBM,
        scratch_shapes=[
            pltpu.VMEM((GROUP - 1, GROUP * rows, raw), BF16),
            pltpu.VMEM((2 * rows, raw), BF16),
            pltpu.VMEM((GROUP - 1, rows, raw), BF16),
            pltpu.SemaphoreType.DMA(((GROUP - 1) * GROUP,)),
            pltpu.SemaphoreType.DMA((GROUP - 1,)),
        ],
        input_output_aliases={7: 0},
        cost_estimate=cost(12 * rows * rows * raw * (GROUP - 1), 10 * rows * raw * (GROUP - 1)),
        compiler_params=WHOLE,
        name="raw_merge",
    )(place, w0, w1, x, *messages, out)


def late_kernel(share, raw, place, w, a, b, m, *refs):
    early, (out, mine, own, buffer, load, save) = refs[:-6], refs[-6:]
    me, size, half = place[0], mine.shape[1], a.shape[1]
    copy = pltpu.make_async_copy(m.at[:, :size], mine, load)
    copy.start()
    saves = []

    def put(source, owner, column):
        target = out.at[:, pl.ds(pl.multiple_of(owner * share + column, 128), source.shape[1])]
        saves.append(pltpu.make_async_copy(source, target, save.at[len(saves)]))
        saves[-1].start()

    put(a, me, size)
    put(b, me, size + half)
    work = [(pair, s, raw) for pair, s in zip(early, PEERS)]
    work += [(pair, s, raw + early[0].shape[1]) for pair, s in zip(early[len(PEERS) :], PEERS)]
    for pair, s, column in work:
        spot = buffer.at[s - 1, :, column - raw : column - raw + pair.shape[1]]
        spot[...] = merge_rows(pair[...], w[0])
        put(spot, me ^ s, column)
    copy.wait()
    own[...] = merge_rows(mine[...], w[0])
    put(own, me, 0)
    for copy in saves:
        copy.wait()


def late(place, w, a, b, m, pairs, raw, share):
    rows, size = a.shape[0], share - 2 * a.shape[1]
    return pl.pallas_call(
        functools.partial(late_kernel, share, raw),
        out_shape=shape(rows, GROUP * share, dtype=BF16),
        in_specs=[SMEM] + [VMEM] * 3 + [HBM] + [VMEM] * len(pairs),
        out_specs=HBM,
        scratch_shapes=[
            pltpu.VMEM((2 * rows, size), BF16),
            pltpu.VMEM((rows, size), BF16),
            pltpu.VMEM((GROUP - 1, rows, size - raw), BF16),
            pltpu.SemaphoreType.DMA,
            pltpu.SemaphoreType.DMA((len(pairs) + 3,)),
        ],
        cost_estimate=cost(4 * rows * rows * size * GROUP, 6 * rows * size * GROUP),
        name="late",
    )(place, w, a, b, m, *pairs)


def put_kernel(spots, share, place, *refs):
    count = len(spots)
    blocks, out, buffers, load, save = refs[:count], refs[count + 1], refs[count + 2 : -2], refs[-2], refs[-1]
    loads, saves = [], []
    for i, ((s, column), block, buffer) in enumerate(zip(spots, blocks, buffers)):
        start = pl.multiple_of((place[0] ^ s) * share + column, 128)
        loads.append(pltpu.make_async_copy(block, buffer, load.at[i]))
        loads[-1].start()
        saves.append(pltpu.make_async_copy(buffer, out.at[:, pl.ds(start, block.shape[1])], save.at[i]))
    for load_copy, save_copy in zip(loads, saves):
        load_copy.wait()
        save_copy.start()
    for copy in saves:
        copy.wait()


def put(place, out, blocks, spots, share):
    size = sum(b.size for b in blocks)
    return pl.pallas_call(
        functools.partial(put_kernel, spots, share),
        out_shape=shape(*out.shape, dtype=out.dtype),
        in_specs=[SMEM] + [HBM] * (len(blocks) + 1),
        out_specs=HBM,
        scratch_shapes=[pltpu.VMEM(b.shape, b.dtype) for b in blocks] + [pltpu.SemaphoreType.DMA((len(blocks),))] * 2,
        input_output_aliases={1 + len(blocks): 0},
        cost_estimate=cost(0, 4 * size),
        compiler_params=WHOLE,
        name="put",
    )(place, *blocks, out)


def over_chips(block):
    chips = lax.axis_size("feat") // CORES
    return total([block] + [send(block, "feat", CORES * s) for s in range(1, chips)])


def gather_group(bundle):
    mine = [bundle] + send_all([bundle] * len(PEERS), "dp", PEERS)
    return mine + [send(b, "feat", 1) for b in mine]


def run(sketches):
    x = sketches[0]
    rows, columns = x.shape
    share = columns // GROUP
    raw, ahead = share // 4, (share // 8, share // 8)
    early = raw + sum(ahead)
    me = lax.axis_index("dp") % GROUP
    place = jnp.stack([me, lax.axis_index("feat") % CORES]).astype(jnp.int32)

    cuts, source = {}, x
    for s in PEERS:
        cuts[s] = lax.dynamic_slice(source, (0, (me ^ s) * share), (rows, share))
        if s == 2:
            source, cuts = lax.optimization_barrier((source, cuts))
    pieces = {s: send(cut, "dp", s) for s, cut in cuts.items()}
    keep, give = own_gram(place, x)
    own = over_chips(total([keep, send(give, "feat", 1)]))
    near, to_x, to_y, to_d = near_gram(place, x, pieces[1], raw)
    p2, p3, own, near = lax.optimization_barrier((pieces[2], pieces[3], own, near))

    keep, give, to_x = far_gram(place, near, p2, p3, to_x)
    parts = fold(keep, send(give, "feat", 1))
    parts, own, to_d = lax.optimization_barrier((parts, own, to_d))
    mine = total([parts[0]] + send_all(parts[1:], "dp", PEERS))
    diagonals = gather_group(own)
    from_d = send(to_d, "dp", 3)
    bundle = over_chips(mine)
    bundle, to_x, to_y = lax.optimization_barrier((bundle, to_x, to_y))
    crosses = gather_group(bundle)
    messages = [send(to_x, "dp", 1), send(to_y, "dp", 2), from_d]
    m, e, f, w0, keep, give = first(place, diagonals, crosses, x, [pieces[1], p2, p3], raw, ahead)

    parts = fold(keep, send(give, "feat", 1))
    parts, e, f = lax.optimization_barrier((parts, e, f))
    mine = total([parts[0]] + send_all(parts[1:], "dp", PEERS))
    pairs_a, pairs_b = [[send(block, "dp", s) for s in (1, 2)] for block in (e, f)]
    bundles = gather_group(over_chips(mine))
    pairs = pairs_a + [send(pairs_a[0], "dp", 2)] + pairs_b + [send(pairs_b[1], "dp", 1)]
    a, b, w1 = second(place, bundles, m, early)

    ax, by = send(a, "dp", 1), send(b, "dp", 2)
    bx, ay = send(b, "dp", 1), send(a, "dp", 2)
    ad, bd = send(ax, "dp", 2), send(by, "dp", 1)
    left, right = early, early + a.shape[1]
    out = late(place, w1, a, b, m, pairs, raw, share)
    out = raw_merge(place, w0, w1, x, messages, out, share)
    out = put(place, out, [ax, by, bx, ay], ((1, left), (2, right), (1, right), (2, left)), share)
    out = put(place, out, [ad, bd], ((3, left), (3, right)), share)
    return out[None]


def solution(mesh):
    spec = P("dp", None, "feat")
    return jax.shard_map(run, mesh=mesh, in_specs=(spec,), out_specs=spec, check_vma=False)
```
